32 devices in a mesh: dp: 2 (over x), ctx: 4 (over y, core), tensor: 4 (over z).
Axes of the slice: x: 2, y: 2, z: 4, core: 2. Of those that a mesh axis runs over, the one named last changes fastest.
Arguments:
- tokens: bfloat16 [2, 4096, 768], P('dp', 'ctx'), may hold values from -6 to 6
- cotangent: bfloat16 [2, 4096, 768], P('dp', 'ctx'), may hold values from -6 to 6
- segments: int32 [2, 2048], P('dp'), may hold values from 0 to 11, never falling along the last dimension, each value on 1 to 256 neighbouring positions
- pairing: int32 [12, 2], replicated, may hold values from 0 to 1, each once within a row
- project: bfloat16 [768, 3, 768], P('dp', None, 'tensor'), may hold values from -0.21875 to 0.21875
- offsets: bfloat16 [2, 768], P(None, ('tensor', 'dp')), may hold values from -3 to 3
- combine: bfloat16 [768, 768], P('tensor', 'dp'), may hold values from -6 to 6
- baseline: bfloat16 [768], P('dp'), may hold values from -3 to 3
- scaling: bfloat16 [768], P('dp'), may hold values from 0.25 to 1.75
- shifting: bfloat16 [768], P('dp'), may hold values from -3 to 3
- expand: bfloat16 [768, 3072], P('dp', 'tensor'), may hold values from -0.21875 to 0.21875
- thresholds: bfloat16 [3072], P(('tensor', 'dp')), may hold values from -3 to 3
- shrink: bfloat16 [3072, 768], P('tensor', 'dp'), may hold values from -0.109375 to 0.109375
- settling: bfloat16 [768], P('dp'), may hold values from -3 to 3
- rescaling: bfloat16 [768], P('dp'), may hold values from 0.25 to 1.75
- reshifting: bfloat16 [768], P('dp'), may hold values from -3 to 3
Outputs:
- layer_out: bfloat16 [2, 4096, 768], P('dp', 'ctx')
- grad_tokens: float32 [2, 4096, 768], P('dp', 'ctx')
- grad_project: float32 [768, 3, 768], P('dp', None, 'tensor')
- grad_offsets: float32 [2, 768], P(None, ('tensor', 'dp'))
- grad_combine: float32 [768, 768], P('tensor', 'dp')
- grad_baseline: float32 [768], P('dp')
- grad_scaling: float32 [768], P('dp')
- grad_shifting: float32 [768], P('dp')
- grad_expand: float32 [768, 3072], P('dp', 'tensor')
- grad_thresholds: float32 [3072], P(('tensor', 'dp'))
- grad_shrink: float32 [3072, 768], P('tensor', 'dp')
- grad_settling: float32 [768], P('dp')
- grad_rescaling: float32 [768], P('dp')
- grad_reshifting: float32 [768], P('dp')
The draws below stay inside these ranges and needn't reach their ends.
Inputs may be any that keep to these rules, and one draw needn't show every extreme that they name: `segments`: along a group's row the numbers never fall, every number of 0 to 11 appears, each continuation has 1 to 256 tokens and one has exactly 256. `pairing`: each row is a permutation of 0 and 1.
All inputs are finite; a program needn't handle non-finite values.
Results may differ from the reference program's by a relative error of at most 0.018.
Values may be sent and summed in bfloat16 or wider, within the bound.
No kernel may reach another device: no remote copies, remote signals or barrier semaphores. Data moves between devices by JAX's collectives and lax.ppermute only.
A program may use at most 192 MiB of HBM per device.

```python
import math
import jax
import jax.numpy as jnp
import numpy as np
from jax import lax

D = 768
H = 12
HD = 64
FF = 3072
P_SIZE = 2048
LMAX = 256
CONT = 12
CT = 2048
QB = 512
B = 1152
GTOK = 4096
GROUPS = 2


def block_levels(rng, shape, cuts, smallest, high):
    def one(dim, shards_of):
        steps = jax.random.uniform(jax.random.fold_in(jax.random.fold_in(rng, 6), dim), (shards_of,), jnp.float32, smallest / len(cuts), high / len(cuts))
        return jnp.repeat(jnp.exp(steps), shape[dim] // shards_of).reshape((-1,) + (1,) * (len(shape) - dim - 1))

    loudness = one(*cuts[0])
    for cut in cuts[1:]:
        loudness = loudness * one(*cut)
    return loudness


def profile(amount, total, bound, slope):
    weights = [(1 << 20) // math.isqrt(grade ** slope) + 1 for grade in range(2, amount + 1)]
    rest, holding = total - bound - (amount - 1), [1] * (amount - 1)
    while rest > 0:
        movable = [i for i in range(amount - 1) if holding[i] < bound]
        mass, remaining = sum([weights[i] for i in movable]), rest
        for i in movable:
            extra = min(bound - holding[i], max(1, remaining * weights[i] // mass), rest)
            holding[i] = holding[i] + extra
            rest = rest - extra
    return np.array([bound] + holding)


def uneven_parts(own_key, count, total, reach, lean):
    if count == 2:
        one = jax.random.randint(own_key, (), max(1, total - reach), min(reach, total - 1) + 1)
        return jnp.stack([one, total - one])
    tallies = jnp.asarray(profile(count, total, reach, lean), jnp.int32)
    couples = (count - 1) // 2
    donor, sink = tallies[1:1 + 2 * couples:2], tallies[2:2 + 2 * couples:2]
    slack = jnp.minimum(donor - 1, reach - sink)
    moved = jax.random.randint(jax.random.fold_in(own_key, 1), (couples,), 0, 1 << 20) % (slack + 1)
    tallies = tallies.at[1:1 + 2 * couples:2].set(donor - moved).at[2:2 + 2 * couples:2].set(sink + moved)
    return tallies[jax.random.permutation(jax.random.fold_in(own_key, 2), count)]


def normal_values(stream_key, shape, scale, most, shards=(), held_as=jnp.bfloat16):
    level = block_levels(stream_key, shape, shards, -0.22, 0.18) if shards else 1.0
    entries = jax.random.normal(stream_key, shape, jnp.float32) * scale * level
    return jnp.minimum(jnp.maximum(entries, -most), most).astype(held_as)


def setup_inputs(seed: int = 0) -> dict:
    seeds = jax.random.split(jax.random.key(seed), 17)
    tokens = normal_values(seeds[0], (GROUPS, GTOK, D), 1.0, 6.0, ((0, 2), (1, 4)))
    cotangent = normal_values(seeds[1], (GROUPS, GTOK, D), 1.0, 6.0, ((0, 2), (1, 4)))
    segments = jax.vmap(lambda own: jnp.searchsorted(jnp.cumsum(uneven_parts(own, CONT, CT, LMAX, 2)), jnp.arange(CT), side="right"))(jax.random.split(seeds[2], GROUPS)).reshape((GROUPS, CT)).astype(jnp.int32)
    pairing = jax.vmap(lambda own: jax.random.permutation(own, 2))(jax.random.split(seeds[3], H)).reshape((H, 2)).astype(jnp.int32)
    project = normal_values(seeds[4], (D, 3, D), D ** -0.5, 0.21875, ((0, 2), (2, 4)))
    offsets = normal_values(seeds[5], (2, D), 0.5, 3.0, ((1, 8),))
    combine = normal_values(seeds[6], (D, D), (max(1, 4 * D // P_SIZE)) ** -0.5, 6.0, ((0, 4), (1, 2)))
    baseline = normal_values(seeds[7], (D,), 0.5, 3.0, ((0, 2),))
    scaling = jnp.clip(1.0 + 0.15 * jax.random.normal(seeds[8], (D,), jnp.float32), 0.25, 1.75).astype(jnp.bfloat16)
    shifting = normal_values(seeds[9], (D,), 0.5, 3.0, ((0, 2),))
    expand = normal_values(seeds[10], (D, FF), D ** -0.5, 0.21875, ((0, 2), (1, 4)))
    thresholds = normal_values(seeds[11], (FF,), 0.5, 3.0, ((0, 8),))
    shrink = normal_values(seeds[12], (FF, D), FF ** -0.5, 0.109375, ((0, 4), (1, 2)))
    settling = normal_values(seeds[13], (D,), 0.5, 3.0, ((0, 2),))
    rescaling = jnp.clip(1.0 + 0.15 * jax.random.normal(seeds[14], (D,), jnp.float32), 0.25, 1.75).astype(jnp.bfloat16)
    reshifting = normal_values(seeds[15], (D,), 0.5, 3.0, ((0, 2),))
    return dict(tokens=tokens, cotangent=cotangent, segments=segments, pairing=pairing, project=project, offsets=offsets, combine=combine, baseline=baseline, scaling=scaling, shifting=shifting, expand=expand, thresholds=thresholds, shrink=shrink, settling=settling, rescaling=rescaling, reshifting=reshifting)


EPS = 1e-06
NEG = -1e+30
HIGH = lax.Precision.HIGHEST

@jax.custom_vjp
def low(v):
    return lax.optimization_barrier(v.astype(jnp.bfloat16)).astype(jnp.float32)

@jax.custom_vjp
def low_back(v):
    return v

def low_keep(v):
    return (low(v), None)

def low_pass(kept, grad):
    return (grad,)

def back_keep(v):
    return (v, None)

def back_low(kept, grad):
    return (low(grad),)
low.defvjp(low_keep, low_pass)
low_back.defvjp(back_keep, back_low)

def layer_norm(value, gain, shift):
    mean = lax.optimization_barrier(jnp.mean(value, axis=-1, keepdims=True))
    centred = value - mean
    spread = lax.optimization_barrier(jnp.mean(centred * centred, axis=-1, keepdims=True))
    return centred * lax.rsqrt(spread + EPS) * gain + shift

def product(left, right):
    return jnp.dot(left, right, precision=HIGH, preferred_element_type=jnp.float32)

def group_layer(x_group, seg_row, pairing, params):
    project, offsets, combine, baseline, scaling, shifting, expand, thresholds, shrink, settling, rescaling, reshifting = params
    length = x_group.shape[0]
    joined = product(x_group, project.reshape(D, 3 * D)).reshape(length, 3, D)
    query = low(low_back(joined[:, 0] + offsets[0])).reshape(length, H, HD)
    key = low(low_back(joined[:, 1])).reshape(length, H, HD)
    value = low(low_back(joined[:, 2] + offsets[1])).reshape(length, H, HD)
    positions = jnp.arange(length, dtype=jnp.int32)
    seg_full = jnp.concatenate([jnp.full((P_SIZE,), -1, jnp.int32), seg_row.astype(jnp.int32)])
    blocks = (positions >= B).astype(jnp.int32)
    scale = HD ** (-0.5)

    def tile(index):
        start = (index * QB).astype(jnp.int32)
        query_tile = lax.dynamic_slice_in_dim(query, start, QB, 0)
        query_pos = start + jnp.arange(QB, dtype=jnp.int32)
        query_blk = (query_pos >= B).astype(jnp.int32)
        query_seg = lax.dynamic_slice_in_dim(seg_full, start, QB, 0)
        paired = jnp.where(query_blk[None, :] == 1, pairing[:, 1:2], pairing[:, 0:1])
        prompt_ok = (positions < P_SIZE)[None, None, :] & (blocks[None, None, :] == paired[:, :, None])
        later_ok = (positions >= P_SIZE)[None, None, :] & (query_seg[:, None] == seg_full[None, :])[None, :, :] & (pairing[:, 1] == 1)[:, None, None]
        raw = low_back(jnp.einsum('qhd,khd->hqk', query_tile, key, precision=HIGH) * scale)
        scores = jnp.where(prompt_ok | later_ok, raw, NEG)
        peak = lax.optimization_barrier(jnp.max(scores, axis=2, keepdims=True))
        expo = jnp.exp(scores - peak)
        probs = low(expo / lax.optimization_barrier(jnp.sum(expo, axis=2, keepdims=True)))
        return jnp.einsum('hqk,khd->qhd', probs, value, precision=HIGH).reshape(QB, D)
    mixed = lax.map(jax.checkpoint(tile), jnp.arange(length // QB, dtype=jnp.int32)).reshape(length, D)
    mixed = low(low_back(mixed))
    attended = low_back(product(mixed, combine))
    first = x_group + attended + baseline
    normed = layer_norm(first, scaling, shifting)
    inner = low_back(product(low(normed), expand) + thresholds)
    active = low(jax.nn.gelu(inner, approximate=False))
    feed = low_back(product(active, shrink))
    second = normed + feed + settling
    return layer_norm(second, rescaling, reshifting)

def reference(tokens, cotangent, segments, pairing, project, offsets, combine, baseline, scaling, shifting, expand, thresholds, shrink, settling, rescaling, reshifting):
    params = tuple((item.astype(jnp.float32) for item in (project, offsets, combine, baseline, scaling, shifting, expand, thresholds, shrink, settling, rescaling, reshifting)))
    x_all = tokens.astype(jnp.float32)

    def forward(x_in, weights):

        def one_group(carry, inputs):
            return (carry, group_layer(inputs[0], inputs[1], pairing, weights))
        _, outputs = lax.scan(one_group, jnp.zeros((), jnp.float32), (x_in, segments))
        return outputs
    result, back = jax.vjp(forward, x_all, params)
    grad_x, grads = back(cotangent.astype(jnp.float32))
    return (result.astype(jnp.bfloat16), grad_x, grads[0], grads[1], grads[2], grads[3], grads[4], grads[5], grads[6], grads[7], grads[8], grads[9], grads[10], grads[11])
```

```python
import functools
import math

import jax
import jax.numpy as jnp
from jax import lax
from jax.experimental import pallas as pl
from jax.experimental.pallas import tpu as pltpu
from jax.sharding import PartitionSpec as P

P_SIZE = 2048
LMAX = 256
B = 1152
HD = 64
EPS = 1e-06
NEG = -1e30

BF = jnp.bfloat16
F32 = jnp.float32

VM = pl.BlockSpec(memory_space=pltpu.VMEM)
ANY = pl.BlockSpec(memory_space=pl.ANY)
SM = pl.BlockSpec(memory_space=pltpu.SMEM)
LIMIT = 60 << 20


def call(body, outs, scratch=(), ins=None, cost=None):
    out_specs = tuple([VM] * len(outs)) if isinstance(outs, tuple) else VM
    return pl.pallas_call(
        body,
        out_shape=outs,
        in_specs=ins,
        out_specs=out_specs,
        scratch_shapes=scratch,
        cost_estimate=cost,
        compiler_params=pltpu.CompilerParams(vmem_limit_bytes=LIMIT),
    )


def sds(shape, dtype):
    return jax.ShapeDtypeStruct(shape, dtype)


def cost(flops, nbytes, trans=0):
    return pl.CostEstimate(flops=int(flops), bytes_accessed=int(nbytes), transcendentals=int(trans))


def dot(a, b):
    return lax.dot_general(a, b, (((1,), (0,)), ((), ())), preferred_element_type=F32)


def dot_t(a, b):
    return lax.dot_general(a, b, (((1,), (1,)), ((), ())), preferred_element_type=F32)


def tdot(a, b):
    return lax.dot_general(a, b, (((0,), (0,)), ((), ())), preferred_element_type=F32)


def mult(value, by):
    return pl.multiple_of(value * by, by)


CTX, Z, X, C, Y, PAIR = 0, 1, 2, 3, 4, 8


def qkv_body(sc, x_ref, w0_ref, w1_ref, bias_ref, q_ref, kv_ref):
    half = w0_ref.shape[1]
    wide = q_ref.shape[0]
    acc = bias_ref[...].astype(F32)
    a0 = x_ref[:, pl.ds(mult(sc[X], half), half)]
    a1 = x_ref[:, pl.ds(mult(1 - sc[X], half), half)]
    out = dot_t(w0_ref[...], a0) + dot_t(w1_ref[...], a1) + acc
    low = out.astype(BF)
    q_ref[...] = low[:wide] * jnp.asarray(HD**-0.5, BF)
    kv_ref[...] = low[wide:]


def load_pairs(sc, own, par, ra, rb, pbuf, cbuf, sems):
    rows = own.shape[1]
    here = pl.ds(mult(sc[C], rows), rows)
    there = pl.ds(mult(1 - sc[C], rows), rows)

    def run(moves):
        copies = [
            pltpu.make_async_copy(src, dst, sems.at[i]) for i, (src, dst) in enumerate(moves)
        ]
        for copy in copies:
            copy.start()
        for copy in copies:
            copy.wait()

    @pl.when(sc[Y] == 0)
    def _():
        run([(own, pbuf.at[:, here]), (par, pbuf.at[:, there])])

    @pl.when(sc[Y] == 1)
    def _():
        run(
            [
                (ra, pbuf.at[:, here]),
                (rb, pbuf.at[:, there]),
                (own, cbuf.at[:, here]),
                (par, cbuf.at[:, there]),
            ]
        )


def prompt_pass(sc, h, index, start, tile):
    first = jnp.where(start >= B, 1, 0)
    last = jnp.where(start + tile // 2 >= B, 1, 0)
    mixed = jnp.where(first != last, 1, 0)
    blk = jnp.where(index == 0, first, last)
    paired = sc[PAIR + 2 * h + blk]
    lane = lax.broadcasted_iota(jnp.int32, (1, tile), 1)
    wanted = jnp.where(lane >= tile // 2, last, first)
    mine = jnp.where(wanted == blk, 1, 0)
    low = mine * (paired * B)
    high = mine * (B + paired * (P_SIZE - B))
    key_start = pl.multiple_of(paired * (P_SIZE - B), 128)
    return mixed, key_start, low, high


def window_start(sc, t, rows, tile):
    local = sc[C] * rows + t * tile
    return pl.multiple_of(jnp.clip(local - LMAX, 0, 2 * rows - tile - 2 * LMAX), 128)


CHUNK = 384


def fwd_body(k, sc, q_ref, span_ref, own, par, ra, rb, o_ref, lse_ref, pbuf, cbuf, s_buf, sems):
    load_pairs(sc, own, par, ra, rb, pbuf, cbuf, sems)
    rows = own.shape[1]
    wide, tile = o_ref.shape
    heads = wide // HD
    t = sc[Z] ^ k
    start = sc[CTX] * rows + t * tile
    cols = pl.ds(mult(t, tile), tile)

    def one_pass(src, key_start, size, low, high, q_h, h, carry):
        peak, total, acc = carry
        k_rows = pl.ds(mult(h, HD), HD)
        v_rows = pl.ds(mult(h, HD) + wide, HD)
        new_peak = peak
        for j in range(size // CHUNK):
            keys = src[k_rows, pl.ds(key_start + j * CHUNK, CHUNK)]
            s = tdot(keys, q_h)
            pos = lax.broadcasted_iota(jnp.int32, s.shape, 0) + (key_start + j * CHUNK)
            s = jnp.where((pos >= low) & (pos < high), s, NEG)
            s_buf[j * CHUNK : (j + 1) * CHUNK, :] = s
            new_peak = jnp.maximum(new_peak, jnp.max(s, axis=0, keepdims=True))
        alpha = jnp.exp(peak - new_peak)
        total = total * alpha
        acc = acc * alpha
        for j in range(size // CHUNK):
            e = jnp.exp(s_buf[j * CHUNK : (j + 1) * CHUNK, :] - new_peak)
            total = total + jnp.sum(e, axis=0, keepdims=True)
            vals = src[v_rows, pl.ds(key_start + j * CHUNK, CHUNK)]
            acc = acc + dot(vals, e.astype(BF))
        return new_peak, total, acc

    def one_head(h, _):
        q_h = q_ref[pl.ds(mult(h, HD), HD), cols]

        def prompt(index, carry):
            _, key_start, low, high = prompt_pass(sc, h, index, start, tile)
            return one_pass(pbuf, key_start, B, low, high, q_h, h, carry)

        def window(index, carry):
            first = window_start(sc, t, rows, tile)
            low = span_ref[0:1, cols]
            high = span_ref[1:2, cols]
            return one_pass(cbuf, first, tile + 2 * LMAX, low, high, q_h, h, carry)

        mixed = prompt_pass(sc, h, 0, start, tile)[0]
        carry = (
            jnp.full((1, tile), NEG, F32),
            jnp.zeros((1, tile), F32),
            jnp.zeros((HD, tile), F32),
        )
        carry = lax.fori_loop(0, 1 + mixed, prompt, carry)
        near = jnp.where((sc[Y] == 1) & (sc[PAIR + 2 * h + 1] == 1), 1, 0)
        peak, total, acc = lax.fori_loop(0, near, window, carry)
        o_ref[pl.ds(mult(h, HD), HD), :] = (acc / total).astype(BF)
        lse_ref[pl.ds(mult(h, 8), 8), :] = jnp.broadcast_to(peak + jnp.log(total), (8, tile))
        return 0

    lax.fori_loop(0, heads, one_head, 0)


def bwd_body(
    sc,
    q_ref,
    span_ref,
    own,
    par,
    ra,
    rb,
    *refs,
):
    o_in = refs[0:4]
    lse_in = refs[4:8]
    g_in = refs[8:12]
    dq_ref, d_own, d_par, d_r0, d_r1 = refs[12:17]
    pbuf, cbuf, o_s, lse_s, g_s, acc_p, acc_c, sems = refs[17:]
    load_pairs(sc, own, par, ra, rb, pbuf, cbuf, sems)
    rows = own.shape[1]
    wide, tile = o_in[0].shape
    heads = wide // HD
    for k in range(4):
        o_s[k] = o_in[k][...]
        lse_s[k] = lse_in[k][...]
        g_s[k] = g_in[k][...]

    def one_pass(src, acc_ref, key_start, size, low, high, q_h, g_h, lse, delta, h, dq):
        k_rows = pl.ds(mult(h, HD), HD)
        v_rows = pl.ds(mult(h, HD) + wide, HD)
        zero = jnp.zeros_like(q_h)
        both = jnp.concatenate(
            [jnp.concatenate([q_h, zero], axis=1), jnp.concatenate([zero, g_h], axis=1)], axis=0
        )
        for j in range(size // CHUNK):
            place = pl.ds(key_start + j * CHUNK, CHUNK)
            keys = src[k_rows, place]
            vals = src[v_rows, place]
            s = tdot(keys, q_h)
            pos = lax.broadcasted_iota(jnp.int32, s.shape, 0) + (key_start + j * CHUNK)
            s = jnp.where((pos >= low) & (pos < high), s, NEG)
            probs = jnp.exp(s - lse)
            ds = probs * (tdot(vals, g_h) - delta)
            ds = ds.astype(BF)
            dq = dq + dot(keys, ds)
            acc_ref[place, :] += dot_t(jnp.concatenate([ds, probs.astype(BF)], axis=1), both)
        return dq

    def one_head(h, _):
        acc_p[...] = jnp.zeros_like(acc_p)
        acc_c[...] = jnp.zeros_like(acc_c)
        h_rows = pl.ds(mult(h, HD), HD)

        def one_tile(k, _):
            t = sc[Z] ^ k
            start = sc[CTX] * rows + t * tile
            cols = pl.ds(mult(t, tile), tile)
            q_h = q_ref[h_rows, cols]
            g_h = g_s[k, h_rows, :]
            o_h = o_s[k, h_rows, :]
            lse = lse_s[k, pl.ds(mult(h, 8), 8), :][0:1]
            delta = jnp.sum(o_h.astype(F32) * g_h.astype(F32), axis=0, keepdims=True)

            def prompt(index, dq):
                _, key_start, low, high = prompt_pass(sc, h, index, start, tile)
                return one_pass(
                    pbuf, acc_p, key_start, B, low, high, q_h, g_h, lse, delta, h, dq
                )

            def window(index, dq):
                first = window_start(sc, t, rows, tile)
                low = span_ref[0:1, cols]
                high = span_ref[1:2, cols]
                return one_pass(
                    cbuf, acc_c, first, tile + 2 * LMAX, low, high, q_h, g_h, lse, delta, h, dq
                )

            mixed = prompt_pass(sc, h, 0, start, tile)[0]
            dq = lax.fori_loop(0, 1 + mixed, prompt, jnp.zeros((HD, tile), F32))
            near = jnp.where((sc[Y] == 1) & (sc[PAIR + 2 * h + 1] == 1), 1, 0)
            dq = lax.fori_loop(0, near, window, dq)
            dq_ref[k, h_rows, :] = (dq * HD**-0.5).astype(BF)
            return 0

        lax.fori_loop(0, 4, one_tile, 0)

        def give(acc, row, out):
            turned = acc[pl.ds(mult(row, rows), rows), :].T.astype(BF)
            out[h_rows, :] = turned[:HD]
            out[pl.ds(mult(h, HD) + wide, HD), :] = turned[HD:]

        @pl.when(sc[Y] == 0)
        def _():
            give(acc_p, sc[C], d_own)
            give(acc_p, 1 - sc[C], d_par)

        @pl.when(sc[Y] == 1)
        def _():
            give(acc_c, sc[C], d_own)
            give(acc_c, 1 - sc[C], d_par)
            give(acc_p, sc[C], d_r0)
            give(acc_p, 1 - sc[C], d_r1)

        return 0

    lax.fori_loop(0, heads, one_head, 0)


def norm(value):
    mean = jnp.mean(value, axis=-1, keepdims=True)
    centred = value - mean
    inv = lax.rsqrt(jnp.mean(centred * centred, axis=-1, keepdims=True) + EPS)
    return centred * inv, inv


def norm_back(e, n, inv):
    return (
        e - jnp.mean(e, axis=-1, keepdims=True) - n * jnp.mean(e * n, axis=-1, keepdims=True)
    ) * inv


def mid_body(sc, *refs):
    mixed = refs[0:4]
    x_ref, cot_ref = refs[4:6]
    packs = refs[6:14]
    pieces = refs[14:30]
    (
        out_ref,
        mb0,
        mb1,
        mb2,
        mb3,
        nl_ref,
        fb_ref,
        ab_ref,
        act_own,
        act_oth,
        ib_own,
        ib_oth,
        mix_own,
        mix_oth,
        gf_ref,
        small_ref,
    ) = refs[30:46]
    we, ws, wc, mix_s, act_s, gp_s, ib_s, vec_s, thr_s, mb_s, sems, osems = refs[46:]
    wide, tile = mixed[0].shape
    width = x_ref.shape[1]
    half = width // 2
    hidden = we.shape[1]
    block = hidden // 4
    hb = block // 2
    hw = wide // 2
    c = sc[C]

    stages = [[], [], []]
    for k in range(4):
        z = sc[Z] ^ k
        for j in range(2):
            xc = pl.ds(mult(sc[X] ^ j, half), half)
            for i in range(2):
                cc = c ^ i
                piece = pieces[k * 4 + j * 2 + i]
                n = len(stages[0])
                stages[0].append(
                    pltpu.make_async_copy(
                        piece.at[pl.ds(half + hb, hw), :],
                        wc.at[pl.ds(pl.multiple_of(z * wide + cc * hw, hw), hw), xc],
                        sems.at[0, n],
                    )
                )
                stages[1].append(
                    pltpu.make_async_copy(
                        piece.at[pl.ds(0, half), :],
                        we.at[xc, pl.ds(pl.multiple_of(z * block + cc * hb, hb), hb)],
                        sems.at[1, n],
                    )
                )
                stages[2].append(
                    pltpu.make_async_copy(
                        piece.at[pl.ds(half, hb), :],
                        ws.at[pl.ds(pl.multiple_of(z * block + cc * hb, hb), hb), xc],
                        sems.at[2, n],
                    )
                )
    for stage in stages:
        for copy in stage:
            copy.start()

    for k in range(4):
        mix_s[pl.ds(mult(sc[Z] ^ k, wide), wide), :] = mixed[k][...]
        for j in range(2):
            pack = packs[k * 2 + j]
            at = pl.multiple_of((sc[Z] ^ k) * block + (sc[X] ^ j) * half, 128)
            thr_s[:, pl.ds(at, half)] = pack[...].astype(F32)
            if k == 0:
                vec_s[:, pl.ds(mult(sc[X] ^ j, half), half)] = pack[...].astype(F32)

    baseline = vec_s[0:1, :]
    scaling = vec_s[1:2, :]
    shifting = vec_s[2:3, :]
    settling = vec_s[3:4, :]
    rescaling = vec_s[4:5, :]
    reshifting = vec_s[5:6, :]

    for copy in stages[0]:
        copy.wait()
    first = x_ref[...].astype(F32) + tdot(mix_s[...], wc[...]) + baseline
    n1, inv1 = norm(first)
    normed = n1 * scaling + shifting
    low = normed.astype(BF)
    nl_ref[...] = low
    for copy in stages[1]:
        copy.wait()
    for copy in stages[2]:
        copy.wait()
    feed = jnp.zeros((tile, width), F32)
    for n in range(4):
        cols = slice(n * block, (n + 1) * block)
        inner = dot(low, we[:, cols]) + thr_s[6:7, cols]
        cdf = 0.5 * (1.0 + lax.erf(inner * (0.5**0.5)))
        pdf = jnp.exp(-0.5 * inner * inner) * (1.0 / math.sqrt(2.0 * math.pi))
        active = (inner * cdf).astype(BF)
        act_s[:, cols] = active
        gp_s[:, cols] = cdf + inner * pdf
        feed = feed + dot(active, ws[cols, :])
    second = normed + feed + settling
    n2, inv2 = norm(second)
    out_ref[...] = (n2 * rescaling + reshifting).astype(BF)
    dy = cot_ref[...].astype(F32)
    small_ref[...] = jnp.zeros_like(small_ref)
    small_ref[4:5, :] = jnp.sum(dy * n2, axis=0, keepdims=True)
    small_ref[5:6, :] = jnp.sum(dy, axis=0, keepdims=True)
    grad = norm_back(rescaling * dy, n2, inv2)
    small_ref[3:4, :] = jnp.sum(grad, axis=0, keepdims=True)
    feed_back = grad.astype(BF)
    fb_ref[...] = feed_back
    for n in range(4):
        cols = slice(n * block, (n + 1) * block)
        inner_back = (dot_t(feed_back, ws[cols, :]) * gp_s[:, cols]).astype(BF)
        ib_s[:, cols] = inner_back
        small_ref[8 + n : 9 + n, :] = jnp.sum(inner_back.astype(F32), axis=0, keepdims=True)
        grad = grad + dot_t(inner_back, we[:, cols])
    small_ref[1:2, :] = jnp.sum(grad * n1, axis=0, keepdims=True)
    small_ref[2:3, :] = jnp.sum(grad, axis=0, keepdims=True)
    grad_first = norm_back(scaling * grad, n1, inv1)
    small_ref[0:1, :] = jnp.sum(grad_first, axis=0, keepdims=True)
    gf_ref[...] = grad_first
    attended_back = grad_first.astype(BF)
    ab_ref[...] = attended_back
    mb_s[...] = dot_t(wc[...], attended_back).astype(BF)
    for k, mb in enumerate((mb0, mb1, mb2, mb3)):
        mb[...] = mb_s[pl.ds(mult(sc[Z] ^ k, wide), wide), :]
    for n in range(4):
        mine = pl.ds(pl.multiple_of(n * block + c * hb, 128), hb)
        other = pl.ds(pl.multiple_of(n * block + (1 - c) * hb, 128), hb)
        cols = slice(n * hb, (n + 1) * hb)
        act_own[:, cols] = act_s[:, mine]
        act_oth[:, cols] = act_s[:, other]
        ib_own[:, cols] = ib_s[:, mine]
        ib_oth[:, cols] = ib_s[:, other]
        mine = pl.ds(pl.multiple_of(n * wide + c * hw, hw), hw)
        other = pl.ds(pl.multiple_of(n * wide + (1 - c) * hw, hw), hw)
        mix_own[n * hw : (n + 1) * hw, :] = mix_s[mine, :]
        mix_oth[n * hw : (n + 1) * hw, :] = mix_s[other, :]


def wg_body(sc, *refs):
    nl, fb, ab, act, ib, mix = [(refs[i], refs[6 + i]) for i in range(6)]
    outs = refs[12:14]
    half = nl[0].shape[1] // 2
    hb = act[0].shape[1] // 4
    hw = mix[0].shape[0] // 4
    for j in range(2):
        xc = pl.ds(mult(sc[X] ^ j, half), half)
        for k in range(4):
            z = sc[Z] ^ k
            zc = pl.ds(mult(z, hb), hb)
            e = sum(tdot(nl[i][:, xc], ib[i][:, zc]) for i in range(2)).astype(BF)
            s = sum(tdot(act[i][:, zc], fb[i][:, xc]) for i in range(2)).astype(BF)
            zr = pl.ds(mult(z, hw), hw)
            m = sum(dot(mix[i][zr, :], ab[i][:, xc]) for i in range(2)).astype(BF)
            for yh in range(2):
                out = outs[j].at[sc[Y] ^ yh, k]
                out[0 : half // 2, :] = e[yh * (half // 2) : (yh + 1) * (half // 2)]
                out[half // 2 : half // 2 + hb // 2, :] = s[yh * (hb // 2) : (yh + 1) * (hb // 2)]
                out[half // 2 + hb // 2 :, :] = m[yh * (hw // 2) : (yh + 1) * (hw // 2)]


def wfin_body(sc, *refs):
    quarters = refs[0:4]
    e_ref, s_ref, m_ref = refs[4:7]
    he = e_ref.shape[0] // 2
    hb = e_ref.shape[1] // 2
    hs = hb // 2
    hm = m_ref.shape[0] // 4
    for i in range(2):
        for j in range(2):
            part = quarters[2 * i + j]
            c = sc[C] ^ i
            y = sc[Y] ^ j
            e_ref[pl.ds(mult(y, he), he), pl.ds(mult(c, hb), hb)] = part[0:he, :].astype(F32)
            at = pl.multiple_of(c * hb + y * hs, hs)
            s_ref[pl.ds(at, hs), :] = part[he : he + hs, :].astype(F32)
            at = pl.multiple_of((c * 2 + y) * hm, hm)
            m_ref[pl.ds(at, hm), :] = part[he + hs :, :].astype(F32)


def kvfin_body(sc, a_ref, b_ref, c_ref, out_ref):
    tile = out_ref.shape[2]
    for k in range(4):
        cols = pl.ds(mult(sc[Z] ^ k, tile), tile)
        total = a_ref[:, cols].astype(F32) + b_ref[:, cols].astype(F32)
        out_ref[k] = (total + c_ref[:, cols].astype(F32)).astype(BF)


def gp_body(sc, dq_ref, kv_ref, x_ref, out_ref, sum_ref, acc):
    wide = dq_ref.shape[1]
    tile = dq_ref.shape[2]
    ones = jnp.ones((8, tile), BF)
    top = bot = s_top = s_bot = 0.0
    for k in range(4):
        rows = x_ref[pl.ds(mult(sc[Z] ^ k, tile), tile), :]
        top = top + dot(dq_ref[k], rows)
        bot = bot + dot(kv_ref[k], rows)
        s_top = s_top + dot_t(ones, dq_ref[k])
        s_bot = s_bot + dot_t(ones, kv_ref[k, wide:, :])
    acc[:wide, :] = top
    acc[wide:, :] = bot
    sum_ref[...] = jnp.zeros_like(sum_ref)
    sum_ref[:, 0:wide] = s_top
    sum_ref[:, wide : 2 * wide] = s_bot
    n_rows = out_ref.shape[3]
    n_cols = out_ref.shape[4]
    for i in range(2):
        for j in range(2):
            at = pl.multiple_of(((sc[C] ^ i) * 2 + (sc[Y] ^ j)) * n_rows, n_rows)
            for m in range(2):
                cols = pl.ds(mult(sc[X] ^ m, n_cols), n_cols)
                out_ref[i, j, m] = acc[pl.ds(at, n_rows), cols].astype(BF)


def ib_body(sc, *refs):
    dq = refs[0:4]
    kv = refs[4:8]
    gf_ref = refs[8]
    pieces = refs[9:25]
    out_ref, wp, jb, sems = refs[25:]
    wide = dq[0].shape[0]
    half = wp.shape[2] // 2
    hr = wp.shape[1] // 2
    copies = []
    for k in range(4):
        for j in range(2):
            for i in range(2):
                copies.append(
                    pltpu.make_async_copy(
                        pieces[k * 4 + j * 2 + i],
                        wp.at[
                            k,
                            pl.ds(mult(sc[C] ^ i, hr), hr),
                            pl.ds(mult(sc[X] ^ j, half), half),
                        ],
                        sems.at[len(copies)],
                    )
                )
    for copy in copies:
        copy.start()
    for k in range(4):
        jb[k, :wide, :] = dq[k][...]
        jb[k, wide:, :] = kv[k][...]
    for copy in copies:
        copy.wait()
    total = gf_ref[...]
    for k in range(4):
        total = total + tdot(jb[k], wp[k])
    out_ref[...] = total.astype(BF)


def join_body(dtype, sc, *refs):
    out = refs[4]
    tile = refs[0].shape[0]
    for k in range(4):
        out[pl.ds(mult(sc[Z] ^ k, tile), tile), :] = refs[k][...].astype(dtype)


def gpfin_body(sc, *refs):
    out = refs[4]
    n_rows = refs[0].shape[0]
    for i in range(2):
        for j in range(2):
            at = pl.multiple_of(((sc[C] ^ i) * 2 + (sc[Y] ^ j)) * n_rows, n_rows)
            out[pl.ds(at, n_rows), :] = refs[2 * i + j][...].astype(F32)


def make_device(n_dp, n_ctx, n_t, generic):
    def swap(axis, size, k):
        return lambda v: lax.ppermute(v, axis, [(i, i ^ k) for i in range(size)])

    pc = swap("ctx", n_ctx, 1)
    py = swap("ctx", n_ctx, 2)
    px = swap("dp", n_dp, 1)
    pz = [lambda v: v] + [swap("tensor", n_t, k) for k in range(1, n_t)]

    def on_device(
        tokens,
        cotangent,
        segments,
        pairing,
        project,
        offsets,
        combine,
        baseline,
        scaling,
        shifting,
        expand,
        thresholds,
        shrink,
        settling,
        rescaling,
        reshifting,
    ):
        _, rows, width = tokens.shape
        heads = pairing.shape[0] // n_t
        wide = heads * HD
        tile = rows // n_t
        half = width // 2
        block = expand.shape[1]
        hidden = block * n_t
        hb = block // 2
        hw = wide // 2
        x = tokens[0]
        cot = cotangent[0]
        ctx = lax.axis_index("ctx")
        z = lax.axis_index("tensor")
        dp = lax.axis_index("dp")
        xi = jnp.zeros_like(dp) if generic else dp
        c = ctx & 1
        y = ctx >> 1
        pairs = lax.dynamic_slice_in_dim(pairing, z * heads, heads, 0).reshape(-1)
        sc = jnp.concatenate(
            [jnp.stack([ctx, z, xi, c, y, c, c, c]).astype(jnp.int32), pairs.astype(jnp.int32)]
        )

        def both_halves(v, axis):
            full = lax.all_gather(v, "dp", axis=axis, tiled=True)
            return jnp.split(full, 2, axis=axis)

        wt = jnp.transpose(project, (1, 2, 0)).reshape(3 * wide, -1)
        vectors = [baseline, scaling, shifting, settling, rescaling, reshifting]

        def pack_small(vecs, thr, off):
            line = jnp.concatenate([off[0], off[1], jnp.zeros((half - wide,), BF)])
            return jnp.stack(vecs + [thr, line])

        def pack_weights(e, s, m):
            return jnp.concatenate(
                [
                    lax.dynamic_slice_in_dim(e, c * hb, hb, 1),
                    lax.dynamic_slice_in_dim(s, c * hb, hb, 0),
                    lax.dynamic_slice_in_dim(m, c * hw, hw, 0),
                ]
            )

        def half_project(w):
            return lax.dynamic_slice_in_dim(w, c * (3 * hw), 3 * hw, 0)

        if generic:
            wts = both_halves(wt, 1)
            vec_h = [both_halves(v, 0) for v in vectors]
            thr_h = both_halves(thresholds, 0)
            off_h = both_halves(offsets, 1)
            smalls = [
                pack_small([v[j] for v in vec_h], thr_h[j], off_h[j]) for j in range(2)
            ]
            es, ss, ms = both_halves(expand, 0), both_halves(shrink, 1), both_halves(combine, 1)
            wpacks = [pack_weights(es[j], ss[j], ms[j]) for j in range(2)]
            small_pieces = [[p(s) for s in smalls] for p in pz]
            weight_halves = [[p(w) for w in wpacks] for p in pz]
            proj_halves = [[p(half_project(w)) for w in wts] for p in pz]
        else:
            wts = [wt, px(wt)]
            small = pack_small(vectors, thresholds, offsets)
            small_z = [p(small) for p in pz]
            small_pieces = [[s, px(s)] for s in small_z]
            wpack = pack_weights(expand, shrink, combine)
            weight_halves = [[w, px(w)] for w in [p(wpack) for p in pz]]
            proj_halves = [[w, px(w)] for w in [p(half_project(wt)) for p in pz]]
        weight_pieces = [w for k in range(4) for j in range(2) for w in (weight_halves[k][j], pc(weight_halves[k][j]))]
        proj_pieces = [w for k in range(4) for j in range(2) for w in (proj_halves[k][j], pc(proj_halves[k][j]))]
        packs = [small_pieces[k][j] for k in range(4) for j in range(2)]

        hq = wide // 2
        lines = [small_pieces[0][j][7] for j in range(2)]
        lines = [jnp.where(xi == 0, lines[j], lines[1 - j]) for j in range(2)]
        bias = jnp.concatenate(
            [
                lines[0][:hq],
                lines[1][:hq],
                jnp.zeros((wide,), BF),
                lines[0][hq : 2 * hq],
                lines[1][hq : 2 * hq],
            ]
        ).astype(F32)[:, None]
        qT, kvT = call(
            qkv_body,
            (sds((wide, rows), BF), sds((2 * wide, rows), BF)),
            ins=[SM] + [VM] * 4,
            cost=cost(2 * rows * width * 3 * wide, 4 * rows * width),
        )(sc, x, wts[0], wts[1], bias)

        seg = segments[0]
        mine = lax.dynamic_slice_in_dim(seg, c * rows, rows, 0)
        low = jnp.sum((seg[:, None] < mine[None, :]).astype(jnp.int32), axis=0)
        high = jnp.sum((seg[:, None] <= mine[None, :]).astype(jnp.int32), axis=0)
        span = jnp.concatenate(
            [low[None], high[None], jnp.zeros((6, rows), jnp.int32)], axis=0
        )

        par = pc(kvT)
        ra = lax.ppermute(kvT, "ctx", [(0, 2), (1, 3)])
        rb = pc(ra)

        kv_scratch = [pltpu.VMEM((2 * wide, 2 * rows), BF), pltpu.VMEM((2 * wide, 2 * rows), BF)]
        o_tiles = [None] * 4
        lses = [None] * 4
        for k in (1, 2, 3, 0):
            o_tiles[k], lses[k] = call(
                functools.partial(fwd_body, k),
                (sds((wide, tile), BF), sds((8 * heads, tile), F32)),
                ins=[SM, VM, VM] + [ANY] * 4,
                scratch=kv_scratch
                + [pltpu.VMEM((B, tile), F32), pltpu.SemaphoreType.DMA((4,))],
                cost=cost(4 * B * tile * wide, 4 * 2 * wide * rows, B * tile * heads),
            )(sc, qT, span, kvT, par, ra, rb)
        mixed = [pz[k](o_tiles[k]) for k in range(4)]

        x_mine = lax.dynamic_slice_in_dim(x, z * tile, tile, 0)
        cot_mine = lax.dynamic_slice_in_dim(cot, z * tile, tile, 0)
        outs = call(
            mid_body,
            (
                sds((tile, width), BF),
                *[sds((wide, tile), BF)] * 4,
                *[sds((tile, width), BF)] * 3,
                *[sds((tile, hidden // 2), BF)] * 4,
                *[sds((width // 2, tile), BF)] * 2,
                sds((tile, width), F32),
                sds((16, width), F32),
            ),
            ins=[SM] + [VM] * 14 + [ANY] * 16,
            scratch=[
                pltpu.VMEM((width, hidden), BF),
                pltpu.VMEM((hidden, width), BF),
                pltpu.VMEM((width, width), BF),
                pltpu.VMEM((width, tile), BF),
                pltpu.VMEM((tile, hidden), BF),
                pltpu.VMEM((tile, hidden), F32),
                pltpu.VMEM((tile, hidden), BF),
                pltpu.VMEM((8, width), F32),
                pltpu.VMEM((8, hidden), F32),
                pltpu.VMEM((width, tile), BF),
                pltpu.SemaphoreType.DMA((3, 16)),
                pltpu.SemaphoreType.DMA((1,)),
            ],
            cost=cost(8 * tile * width * hidden + 4 * tile * width * width, 4 * width * hidden),
        )(sc, *mixed, x_mine, cot_mine, *packs, *weight_pieces)
        out_low = outs[0]
        mb = outs[1:5]
        nl, fb, ab, act_own, act_oth, ib_own, ib_oth, mix_own, mix_oth, grad_first, small_sum = outs[5:]
        grads = [pz[k](mb[k]) for k in range(4)]

        theirs = [pc(v) for v in (nl, fb, ab, act_oth, ib_oth, mix_oth)]
        n_part = half // 2 + hb // 2 + hw // 2
        g_own, g_oth = call(
            wg_body,
            tuple([sds((2, 4, n_part, half), BF)] * 2),
            ins=[SM] + [VM] * 12,
            cost=cost(4 * tile * width * hidden, 4 * width * hidden),
        )(sc, nl, fb, ab, act_own, ib_own, mix_own, *theirs)

        outs = call(
            bwd_body,
            (sds((4, wide, tile), BF), *[sds((2 * wide, rows), BF)] * 4),
            ins=[SM, VM, VM] + [ANY] * 4 + [VM] * 12,
            scratch=kv_scratch
            + [
                pltpu.VMEM((4, wide, tile), BF),
                pltpu.VMEM((4, 8 * heads, tile), F32),
                pltpu.VMEM((4, wide, tile), BF),
                pltpu.VMEM((2 * rows, 2 * HD), F32),
                pltpu.VMEM((2 * rows, 2 * HD), F32),
                pltpu.SemaphoreType.DMA((4,)),
            ],
            cost=cost(10 * B * rows * wide, 4 * 4 * wide * rows, B * rows * heads),
        )(sc, qT, span, kvT, par, ra, rb, *o_tiles, *lses, *grads)
        dq, d_own, d_par, d_r0, d_r1 = outs
        got_par = pc(d_par)
        got_r = pc(d_r1)
        prompt_part = (d_r0.astype(F32) + got_r.astype(F32)).astype(BF)
        from_y = lax.ppermute(prompt_part, "ctx", [(2, 0), (3, 1)])
        kv_back = call(
            kvfin_body,
            sds((4, 2 * wide, tile), BF),
            ins=[SM] + [VM] * 3,
            cost=cost(2 * wide * rows, 8 * wide * rows),
        )(sc, d_own, got_par, from_y)

        jq = [dq[0]] + [pz[k](dq[k]) for k in range(1, 4)]
        jkv = [kv_back[0]] + [pz[k](kv_back[k]) for k in range(1, 4)]
        gp, sums = call(
            gp_body,
            (sds((2, 2, 2, 3 * wide // 4, half), BF), sds((8, width), F32)),
            ins=[SM] + [VM] * 3,
            scratch=[pltpu.VMEM((3 * wide, width), F32)],
            cost=cost(2 * rows * width * 3 * wide, 4 * rows * width),
        )(sc, dq, kv_back, x)

        low_tokens = call(
            ib_body,
            sds((tile, width), BF),
            ins=[SM] + [VM] * 9 + [ANY] * 16,
            scratch=[
                pltpu.VMEM((4, 3 * wide, width), BF),
                pltpu.VMEM((4, 3 * wide, tile), BF),
                pltpu.SemaphoreType.DMA((16,)),
            ],
            cost=cost(8 * tile * width * 3 * wide, 8 * width * 3 * wide),
        )(sc, *jq, *jkv, grad_first, *proj_pieces)
        token_tiles = [low_tokens] + [pz[k](low_tokens) for k in range(1, 4)]
        grad_tokens = call(
            functools.partial(join_body, F32),
            sds((rows, width), F32),
            ins=[SM] + [VM] * 4,
            cost=cost(rows * width, 6 * rows * width),
        )(sc, *token_tiles)
        layer_tiles = [out_low] + [pz[k](out_low) for k in range(1, 4)]
        layer_out = call(
            functools.partial(join_body, BF),
            sds((rows, width), BF),
            ins=[SM] + [VM] * 4,
            cost=cost(rows * width, 4 * rows * width),
        )(sc, *layer_tiles)

        def add(a, b):
            return (a.astype(F32) + b.astype(F32)).astype(BF)

        def reduce_ff(g):
            s = add(g[0], py(g[1]))
            got = [pz[k](s[k]) for k in range(1, 4)]
            mine = s[0].astype(F32) + got[0].astype(F32) + got[1].astype(F32) + got[2].astype(F32)
            mine = mine.astype(BF)
            quarters = [mine, py(mine)]
            quarters = quarters + [pc(q) for q in quarters]
            return call(
                wfin_body,
                (sds((half, block), F32), sds((block, half), F32), sds((wide, half), F32)),
                ins=[SM] + [VM] * 4,
                cost=cost(2 * half * block, 12 * half * block),
            )(sc, *quarters)

        def reduce_gp(g):
            s = add(g[0], pc(g[1]))
            mine = add(s[0], py(s[1]))
            quarters = [mine, py(mine)]
            return quarters

        def finish_gp(quarters):
            quarters = quarters + [pc(q) for q in quarters]
            return call(
                gpfin_body,
                sds((3 * wide, half), F32),
                ins=[SM] + [VM] * 4,
                cost=cost(3 * wide * half, 6 * 3 * wide * half),
            )(sc, *quarters)

        def gp_cy(g):
            s = add(g[0], pc(g[1]))
            return add(s[0], py(s[1]))

        if generic:
            parts = [reduce_ff(g) for g in (g_own, g_oth)]

            def scatter(v, axis):
                return lax.psum_scatter(
                    v.astype(BF), "dp", scatter_dimension=axis, tiled=True
                ).astype(F32)

            grad_expand = scatter(jnp.concatenate([p[0] for p in parts], axis=0), 0)
            grad_shrink = scatter(jnp.concatenate([p[1] for p in parts], axis=1), 1)
            grad_combine = scatter(jnp.concatenate([p[2] for p in parts], axis=1), 1)
            summed = gp_cy(gp)
            both = []
            for j in range(2):
                both.append(finish_gp([summed[j], py(summed[j])]))
            grad_project = scatter(jnp.concatenate(both, axis=1), 1)
        else:
            g = add(g_own, px(g_oth))
            grad_expand, grad_shrink, grad_combine = reduce_ff(g)
            summed = gp_cy(gp)
            mine = add(summed[0], px(summed[1]))
            grad_project = finish_gp([mine, py(mine)])
        grad_project = jnp.transpose(grad_project.reshape(3, wide, -1), (2, 0, 1))

        slot = lax.broadcasted_iota(jnp.int32, (16, 1), 0) == 12 + z
        total = small_sum + jnp.where(slot, sums[0:1], 0.0)
        total = total + pc(total)
        total = total + py(total)
        total = lax.psum(total, "dp") if generic else total + px(total)
        total = total + pz[1](total)
        total = total + pz[2](total)
        n_vec = baseline.shape[0]

        def row(r):
            return lax.dynamic_slice(total, (r, dp * n_vec), (1, n_vec))[0]

        n_off = offsets.shape[1]
        grad_offsets = jnp.concatenate(
            [lax.dynamic_slice(total, (12 + z, dp * n_off + i * wide), (1, n_off)) for i in range(2)]
        )
        return (
            layer_out[None],
            grad_tokens[None],
            grad_project,
            grad_offsets,
            grad_combine,
            row(0),
            row(1),
            row(2),
            grad_expand,
            row(8 + z),
            grad_shrink,
            row(3),
            row(4),
            row(5),
        )

    return on_device


def solution(mesh):
    in_specs = (
        P("dp", "ctx", None),
        P("dp", "ctx", None),
        P("dp", None),
        P(),
        P("dp", None, "tensor"),
        P(None, ("tensor", "dp")),
        P("tensor", "dp"),
        P("dp"),
        P("dp"),
        P("dp"),
        P("dp", "tensor"),
        P(("tensor", "dp")),
        P("tensor", "dp"),
        P("dp"),
        P("dp"),
        P("dp"),
    )
    out_specs = (
        P("dp", "ctx", None),
        P("dp", "ctx", None),
        P("dp", None, "tensor"),
        P(None, ("tensor", "dp")),
        P("tensor", "dp"),
        P("dp"),
        P("dp"),
        P("dp"),
        P("dp", "tensor"),
        P(("tensor", "dp")),
        P("tensor", "dp"),
        P("dp"),
        P("dp"),
        P("dp"),
    )
    n_dp = mesh.shape["dp"]
    on_device = make_device(n_dp, mesh.shape["ctx"], mesh.shape["tensor"], n_dp != 2)
    return jax.shard_map(
        on_device, mesh=mesh, in_specs=in_specs, out_specs=out_specs, check_vma=False
    )
```

```python
import functools
import math

import jax
import jax.numpy as jnp
from jax import lax
from jax.experimental import pallas as pl
from jax.experimental.pallas import tpu as pltpu
from jax.sharding import Mesh
from jax.sharding import PartitionSpec as P

P_SIZE = 2048
LMAX = 256
B = 1152
HD = 64
EPS = 1e-06
NEG = -1e30

BF = jnp.bfloat16
F32 = jnp.float32

VM = pl.BlockSpec(memory_space=pltpu.VMEM)
ANY = pl.BlockSpec(memory_space=pl.ANY)
SM = pl.BlockSpec(memory_space=pltpu.SMEM)
LIMIT = 60 << 20


def call(body, outs, scratch=(), ins=None, cost=None):
    out_specs = tuple([VM] * len(outs)) if isinstance(outs, tuple) else VM
    return pl.pallas_call(
        body,
        out_shape=outs,
        in_specs=ins,
        out_specs=out_specs,
        scratch_shapes=scratch,
        cost_estimate=cost,
        compiler_params=pltpu.CompilerParams(vmem_limit_bytes=LIMIT),
    )


def sds(shape, dtype):
    return jax.ShapeDtypeStruct(shape, dtype)


def cost(flops, nbytes, trans=0):
    return pl.CostEstimate(flops=int(flops), bytes_accessed=int(nbytes), transcendentals=int(trans))


def dot(a, b):
    return lax.dot_general(a, b, (((1,), (0,)), ((), ())), preferred_element_type=F32)


def dot_t(a, b):
    return lax.dot_general(a, b, (((1,), (1,)), ((), ())), preferred_element_type=F32)


def tdot(a, b):
    return lax.dot_general(a, b, (((0,), (0,)), ((), ())), preferred_element_type=F32)


def mult(value, by):
    return pl.multiple_of(value * by, by)


CTX, Z, X, C, Y, PAIR = 0, 1, 2, 3, 4, 8


def qkv_body(sc, x_ref, own_ref, small_ref, w0_ref, w1_ref, q_ref, kv_ref, wt_ref, oth, row):
    half = own_ref.shape[1]
    wide = q_ref.shape[0]
    part = own_ref.shape[0] // 2
    hq = wide // 2
    oth[pl.ds(mult(sc[C], part), part), :] = w0_ref[:part, :]
    oth[pl.ds(mult(1 - sc[C], part), part), :] = w1_ref[:part, :]
    mine, theirs = small_ref[...].astype(BF), w0_ref[part:, :]
    even = jnp.where(sc[X] == 0, mine, theirs)
    odd = jnp.where(sc[X] == 0, theirs, mine)
    row[...] = jnp.zeros_like(row)
    for at, rank in ((0, 7), (2 * wide, 8)):
        row[0:1, at : at + hq] = even[rank : rank + 1, :hq]
        row[0:1, at + hq : at + wide] = odd[rank : rank + 1, :hq]
    a0 = x_ref[:, pl.ds(mult(sc[X], half), half)]
    a1 = x_ref[:, pl.ds(mult(1 - sc[X], half), half)]
    first = lax.broadcasted_iota(jnp.int32, (row.shape[0], x_ref.shape[0]), 0) == 0
    bias = tdot(row[...], jnp.where(first, 1.0, 0.0).astype(BF))
    low = (dot_t(own_ref[...], a0) + dot_t(oth[...], a1) + bias).astype(BF)
    q_ref[...] = low[:wide] * jnp.asarray(HD**-0.5, BF)
    kv_ref[...] = low[wide:]
    wt_ref[:, pl.ds(mult(sc[X], half), half)] = own_ref[...]
    wt_ref[:, pl.ds(mult(1 - sc[X], half), half)] = oth[...]


def pack_body(sc, *refs):
    wt, e_ref, s_ref, m_ref, off = refs[0:5]
    vecs = refs[5:12]
    small, wtc, wc = refs[12:15]
    part = wt.shape[0] // 2
    hb = e_ref.shape[1] // 2
    hw = m_ref.shape[0] // 2
    half = s_ref.shape[1]
    c = sc[C]
    small[...] = jnp.zeros_like(small)
    for i, vec in enumerate(vecs):
        small[i : i + 1, :] = vec[...].astype(F32).reshape(1, half)
    small[7:9, : off.shape[1]] = off[...].astype(F32)
    low = small[...].astype(BF)
    wtc[:part, :] = wt[pl.ds(mult(c, part), part), :]
    wtc[part:, :] = low
    wc[:half, :] = e_ref[:, pl.ds(mult(c, hb), hb)]
    wc[half : half + hb, :] = s_ref[pl.ds(mult(c, hb), hb), :]
    wc[half + hb : half + hb + hw, :] = m_ref[pl.ds(mult(c, hw), hw), :]
    wc[half + hb + hw :, :] = low


def load_pairs(sc, own, par, ra, rb, pbuf, cbuf, sems):
    rows = own.shape[1]
    here = pl.ds(mult(sc[C], rows), rows)
    there = pl.ds(mult(1 - sc[C], rows), rows)

    def run(moves):
        copies = [
            pltpu.make_async_copy(src, dst, sems.at[i]) for i, (src, dst) in enumerate(moves)
        ]
        for copy in copies:
            copy.start()
        for copy in copies:
            copy.wait()

    @pl.when(sc[Y] == 0)
    def _():
        run([(own, pbuf.at[:, here]), (par, pbuf.at[:, there])])

    @pl.when(sc[Y] == 1)
    def _():
        run(
            [
                (ra, pbuf.at[:, here]),
                (rb, pbuf.at[:, there]),
                (own, cbuf.at[:, here]),
                (par, cbuf.at[:, there]),
            ]
        )


def prompt_pass(sc, h, index, start, tile):
    first = jnp.where(start >= B, 1, 0)
    last = jnp.where(start + tile // 2 >= B, 1, 0)
    mixed = jnp.where(first != last, 1, 0)
    blk = jnp.where(index == 0, first, last)
    paired = sc[PAIR + 2 * h + blk]
    lane = lax.broadcasted_iota(jnp.int32, (1, tile), 1)
    wanted = jnp.where(lane >= tile // 2, last, first)
    mine = jnp.where(wanted == blk, 1, 0)
    low = mine * (paired * B)
    high = mine * (B + paired * (P_SIZE - B))
    key_start = pl.multiple_of(paired * (P_SIZE - B), 128)
    return mixed, key_start, low, high


def window_start(sc, t, rows, tile):
    local = sc[C] * rows + t * tile
    return pl.multiple_of(jnp.clip(local - LMAX, 0, 2 * rows - tile - 2 * LMAX), 128)


CHUNK = 384


def fwd_body(k, sc, q_ref, span_ref, own, par, ra, rb, o_ref, lse_ref, pbuf, cbuf, s_buf, sems):
    load_pairs(sc, own, par, ra, rb, pbuf, cbuf, sems)
    rows = own.shape[1]
    wide, tile = o_ref.shape
    heads = wide // HD
    t = sc[Z] ^ k
    start = sc[CTX] * rows + t * tile
    cols = pl.ds(mult(t, tile), tile)

    def one_pass(src, key_start, size, low, high, q_h, h, carry):
        peak, total, acc = carry
        k_rows = pl.ds(mult(h, HD), HD)
        v_rows = pl.ds(mult(h, HD) + wide, HD)
        new_peak = peak
        for j in range(size // CHUNK):
            keys = src[k_rows, pl.ds(key_start + j * CHUNK, CHUNK)]
            s = tdot(keys, q_h)
            pos = lax.broadcasted_iota(jnp.int32, s.shape, 0) + (key_start + j * CHUNK)
            s = jnp.where((pos >= low) & (pos < high), s, NEG)
            s_buf[j * CHUNK : (j + 1) * CHUNK, :] = s
            new_peak = jnp.maximum(new_peak, jnp.max(s, axis=0, keepdims=True))
        alpha = jnp.exp(peak - new_peak)
        total = total * alpha
        acc = acc * alpha
        for j in range(size // CHUNK):
            e = jnp.exp(s_buf[j * CHUNK : (j + 1) * CHUNK, :] - new_peak)
            total = total + jnp.sum(e, axis=0, keepdims=True)
            vals = src[v_rows, pl.ds(key_start + j * CHUNK, CHUNK)]
            acc = acc + dot(vals, e.astype(BF))
        return new_peak, total, acc

    def one_head(h, _):
        q_h = q_ref[pl.ds(mult(h, HD), HD), cols]

        def prompt(index, carry):
            _, key_start, low, high = prompt_pass(sc, h, index, start, tile)
            return one_pass(pbuf, key_start, B, low, high, q_h, h, carry)

        def window(index, carry):
            first = window_start(sc, t, rows, tile)
            low = span_ref[0:1, cols]
            high = span_ref[1:2, cols]
            return one_pass(cbuf, first, tile + 2 * LMAX, low, high, q_h, h, carry)

        mixed = prompt_pass(sc, h, 0, start, tile)[0]
        carry = (
            jnp.full((1, tile), NEG, F32),
            jnp.zeros((1, tile), F32),
            jnp.zeros((HD, tile), F32),
        )
        carry = lax.fori_loop(0, 1 + mixed, prompt, carry)
        near = jnp.where((sc[Y] == 1) & (sc[PAIR + 2 * h + 1] == 1), 1, 0)
        peak, total, acc = lax.fori_loop(0, near, window, carry)
        o_ref[pl.ds(mult(h, HD), HD), :] = (acc / total).astype(BF)
        lse_ref[pl.ds(mult(h, 8), 8), :] = jnp.broadcast_to(peak + jnp.log(total), (8, tile))
        return 0

    lax.fori_loop(0, heads, one_head, 0)


def bwd_body(
    sc,
    q_ref,
    span_ref,
    own,
    par,
    ra,
    rb,
    *refs,
):
    o_in = refs[0:4]
    lse_in = refs[4:8]
    g_in = refs[8:12]
    dq_ref, d_own, d_par, d_r0, d_r1 = refs[12:17]
    pbuf, cbuf, o_s, lse_s, g_s, acc_p, acc_c, sems = refs[17:]
    load_pairs(sc, own, par, ra, rb, pbuf, cbuf, sems)
    rows = own.shape[1]
    wide, tile = o_in[0].shape
    heads = wide // HD
    for k in range(4):
        o_s[k] = o_in[k][...]
        lse_s[k] = lse_in[k][...]
        g_s[k] = g_in[k][...]

    def one_pass(src, acc_ref, key_start, size, low, high, q_h, g_h, lse, delta, h, dq):
        k_rows = pl.ds(mult(h, HD), HD)
        v_rows = pl.ds(mult(h, HD) + wide, HD)
        zero = jnp.zeros_like(q_h)
        both = jnp.concatenate(
            [jnp.concatenate([q_h, zero], axis=1), jnp.concatenate([zero, g_h], axis=1)], axis=0
        )
        for j in range(size // CHUNK):
            place = pl.ds(key_start + j * CHUNK, CHUNK)
            keys = src[k_rows, place]
            vals = src[v_rows, place]
            s = tdot(keys, q_h)
            pos = lax.broadcasted_iota(jnp.int32, s.shape, 0) + (key_start + j * CHUNK)
            s = jnp.where((pos >= low) & (pos < high), s, NEG)
            probs = jnp.exp(s - lse)
            ds = probs * (tdot(vals, g_h) - delta)
            ds = ds.astype(BF)
            dq = dq + dot(keys, ds)
            acc_ref[place, :] += dot_t(jnp.concatenate([ds, probs.astype(BF)], axis=1), both)
        return dq

    def one_head(h, _):
        acc_p[...] = jnp.zeros_like(acc_p)
        acc_c[...] = jnp.zeros_like(acc_c)
        h_rows = pl.ds(mult(h, HD), HD)

        def one_tile(k, _):
            t = sc[Z] ^ k
            start = sc[CTX] * rows + t * tile
            cols = pl.ds(mult(t, tile), tile)
            q_h = q_ref[h_rows, cols]
            g_h = g_s[k, h_rows, :]
            o_h = o_s[k, h_rows, :]
            lse = lse_s[k, pl.ds(mult(h, 8), 8), :][0:1]
            delta = jnp.sum(o_h.astype(F32) * g_h.astype(F32), axis=0, keepdims=True)

            def prompt(index, dq):
                _, key_start, low, high = prompt_pass(sc, h, index, start, tile)
                return one_pass(
                    pbuf, acc_p, key_start, B, low, high, q_h, g_h, lse, delta, h, dq
                )

            def window(index, dq):
                first = window_start(sc, t, rows, tile)
                low = span_ref[0:1, cols]
                high = span_ref[1:2, cols]
                return one_pass(
                    cbuf, acc_c, first, tile + 2 * LMAX, low, high, q_h, g_h, lse, delta, h, dq
                )

            mixed = prompt_pass(sc, h, 0, start, tile)[0]
            dq = lax.fori_loop(0, 1 + mixed, prompt, jnp.zeros((HD, tile), F32))
            near = jnp.where((sc[Y] == 1) & (sc[PAIR + 2 * h + 1] == 1), 1, 0)
            dq = lax.fori_loop(0, near, window, dq)
            dq_ref[k, h_rows, :] = (dq * HD**-0.5).astype(BF)
            return 0

        lax.fori_loop(0, 4, one_tile, 0)

        def give(acc, row, out):
            turned = acc[pl.ds(mult(row, rows), rows), :].T.astype(BF)
            out[h_rows, :] = turned[:HD]
            out[pl.ds(mult(h, HD) + wide, HD), :] = turned[HD:]

        @pl.when(sc[Y] == 0)
        def _():
            give(acc_p, sc[C], d_own)
            give(acc_p, 1 - sc[C], d_par)

        @pl.when(sc[Y] == 1)
        def _():
            give(acc_c, sc[C], d_own)
            give(acc_c, 1 - sc[C], d_par)
            give(acc_p, sc[C], d_r0)
            give(acc_p, 1 - sc[C], d_r1)

        return 0

    lax.fori_loop(0, heads, one_head, 0)


def norm(value):
    mean = jnp.mean(value, axis=-1, keepdims=True)
    centred = value - mean
    inv = lax.rsqrt(jnp.mean(centred * centred, axis=-1, keepdims=True) + EPS)
    return centred * inv, inv


def norm_back(e, n, inv):
    return (
        e - jnp.mean(e, axis=-1, keepdims=True) - n * jnp.mean(e * n, axis=-1, keepdims=True)
    ) * inv


def mid_body(sc, *refs):
    mixed = refs[0:4]
    x_hbm, cot_hbm = refs[4:6]
    packs = refs[6:8]
    (
        out_ref,
        mb0,
        mb1,
        mb2,
        mb3,
        nl_ref,
        fb_ref,
        ab_ref,
        act_own,
        act_oth,
        ib_own,
        ib_oth,
        mix_own,
        mix_oth,
        gf_ref,
    ) = refs[8:23]
    we, ws, wc, mix_s, act_s, gp_s, ib_s, vec_s, thr_s, mb_s, pk_s, x_ref, cot_ref, small_ref, sems, psems = refs[23:]
    wide, tile = mixed[0].shape
    width = x_ref.shape[1]
    half = width // 2
    hidden = we.shape[1]
    block = hidden // 4
    hb = block // 2
    hw = wide // 2
    c = sc[C]
    n_pack = half + hb + hw + 16

    stages = [[], [], []]
    small = []

    def move(stage, src, dst):
        n = len(stages[stage])
        stages[stage].append(pltpu.make_async_copy(src, dst, sems.at[stage, n]))

    for xh in range(2):
        xc = pl.ds(xh * half, half)
        for z in range(4):
            at = (xh * 4 + z) * n_pack
            for i in range(2):
                cc = c ^ i
                rows = pl.multiple_of(z * wide + cc * hw, hw)
                move(
                    0,
                    packs[i].at[pl.ds(at + half + hb, hw), :],
                    wc.at[pl.ds(rows, hw), xc],
                )
                place = pl.ds(pl.multiple_of(z * block + cc * hb, hb), hb)
                move(1, packs[i].at[pl.ds(at, half), :], we.at[xc, place])
                move(2, packs[i].at[pl.ds(at + half, hb), :], ws.at[place, xc])
            n = xh * 4 + z
            small.append(
                pltpu.make_async_copy(
                    packs[0].at[pl.ds(at + half + hb + hw, 16), :], pk_s.at[n], psems.at[n]
                )
            )
    mine = pl.ds(mult(sc[Z], tile), tile)
    small.append(pltpu.make_async_copy(x_hbm.at[mine, :], x_ref, psems.at[8]))
    small.append(pltpu.make_async_copy(cot_hbm.at[mine, :], cot_ref, psems.at[9]))
    for stage in [small] + stages:
        for copy in stage:
            copy.start()

    for copy in small:
        copy.wait()
    for k in range(4):
        mix_s[pl.ds(mult(sc[Z] ^ k, wide), wide), :] = mixed[k][...]
    for xh in range(2):
        for z in range(4):
            pack = pk_s[xh * 4 + z].astype(F32)
            at = z * block + xh * half
            thr_s[:, at : at + half] = pack[:8]
        vec_s[:, xh * half : (xh + 1) * half] = pk_s[xh * 4].astype(F32)[:8]

    baseline = vec_s[0:1, :]
    scaling = vec_s[1:2, :]
    shifting = vec_s[2:3, :]
    settling = vec_s[3:4, :]
    rescaling = vec_s[4:5, :]
    reshifting = vec_s[5:6, :]

    for copy in stages[0]:
        copy.wait()
    first = x_ref[...].astype(F32) + tdot(mix_s[...], wc[...]) + baseline
    n1, inv1 = norm(first)
    normed = n1 * scaling + shifting
    low = normed.astype(BF)
    nl_ref[...] = low
    for copy in stages[1]:
        copy.wait()
    for copy in stages[2]:
        copy.wait()
    feed = jnp.zeros((tile, width), F32)
    for n in range(4):
        cols = slice(n * block, (n + 1) * block)
        inner = dot(low, we[:, cols]) + thr_s[6:7, cols]
        cdf = 0.5 * (1.0 + lax.erf(inner * (0.5**0.5)))
        pdf = jnp.exp(-0.5 * inner * inner) * (1.0 / math.sqrt(2.0 * math.pi))
        active = (inner * cdf).astype(BF)
        act_s[:, cols] = active
        gp_s[:, cols] = cdf + inner * pdf
        feed = feed + dot(active, ws[cols, :])
    second = normed + feed + settling
    n2, inv2 = norm(second)
    out_ref[:tile, :] = (n2 * rescaling + reshifting).astype(BF)
    dy = cot_ref[...].astype(F32)
    small_ref[...] = jnp.zeros_like(small_ref)
    small_ref[4:5, :] = jnp.sum(dy * n2, axis=0, keepdims=True)
    small_ref[5:6, :] = jnp.sum(dy, axis=0, keepdims=True)
    grad = norm_back(rescaling * dy, n2, inv2)
    small_ref[3:4, :] = jnp.sum(grad, axis=0, keepdims=True)
    feed_back = grad.astype(BF)
    fb_ref[...] = feed_back
    for n in range(4):
        cols = slice(n * block, (n + 1) * block)
        inner_back = (dot_t(feed_back, ws[cols, :]) * gp_s[:, cols]).astype(BF)
        ib_s[:, cols] = inner_back
        small_ref[8 + n : 9 + n, :] = jnp.sum(inner_back.astype(F32), axis=0, keepdims=True)
        grad = grad + dot_t(inner_back, we[:, cols])
    small_ref[1:2, :] = jnp.sum(grad * n1, axis=0, keepdims=True)
    small_ref[2:3, :] = jnp.sum(grad, axis=0, keepdims=True)
    grad_first = norm_back(scaling * grad, n1, inv1)
    small_ref[0:1, :] = jnp.sum(grad_first, axis=0, keepdims=True)
    out_ref[tile:, :] = small_ref[...].astype(BF)
    gf_ref[...] = grad_first
    attended_back = grad_first.astype(BF)
    ab_ref[...] = attended_back
    mb_s[...] = dot_t(wc[...], attended_back).astype(BF)
    for k, mb in enumerate((mb0, mb1, mb2, mb3)):
        mb[...] = mb_s[pl.ds(mult(sc[Z] ^ k, wide), wide), :]
    for n in range(4):
        mine = pl.ds(pl.multiple_of(n * block + c * hb, 128), hb)
        other = pl.ds(pl.multiple_of(n * block + (1 - c) * hb, 128), hb)
        cols = slice(n * hb, (n + 1) * hb)
        act_own[:, cols] = act_s[:, mine]
        act_oth[:, cols] = act_s[:, other]
        ib_own[:, cols] = ib_s[:, mine]
        ib_oth[:, cols] = ib_s[:, other]
        mine = pl.ds(pl.multiple_of(n * wide + c * hw, hw), hw)
        other = pl.ds(pl.multiple_of(n * wide + (1 - c) * hw, hw), hw)
        mix_own[n * hw : (n + 1) * hw, :] = mix_s[mine, :]
        mix_oth[n * hw : (n + 1) * hw, :] = mix_s[other, :]


def wg_body(sc, *refs):
    nl, fb, ab, act, ib, mix = [(refs[i], refs[6 + i]) for i in range(6)]
    g_ref = refs[12]
    half = nl[0].shape[1] // 2
    hb = act[0].shape[1] // 4
    hw = mix[0].shape[0] // 4
    for x in range(2):
        xc = slice(x * half, (x + 1) * half)
        for z in range(4):
            zc = slice(z * hb, (z + 1) * hb)
            e = sum(tdot(nl[i][:, xc], ib[i][:, zc]) for i in range(2)).astype(BF)
            s = sum(tdot(act[i][:, zc], fb[i][:, xc]) for i in range(2)).astype(BF)
            zr = slice(z * hw, (z + 1) * hw)
            m = sum(dot(mix[i][zr, :], ab[i][:, xc]) for i in range(2)).astype(BF)
            at = 0
            for v in (e, s, m):
                n = v.shape[0] // 2
                for yh in range(2):
                    g_ref[yh, x, z, at : at + n, :] = v[yh * n : (yh + 1) * n]
                at += n


def wfin_body(sc, *refs):
    quarters = refs[0:4]
    e_ref, s_ref, m_ref = refs[4:7]
    he = e_ref.shape[0] // 2
    hb = e_ref.shape[1] // 2
    hs = hb // 2
    hm = m_ref.shape[0] // 4
    for i in range(2):
        c = sc[C] ^ i
        for j in range(2):
            part = quarters[2 * i + j]
            y = sc[Y] ^ j
            rows = pl.ds(mult(y, he), he)
            e_ref[rows, pl.ds(mult(c, hb), hb)] = part[:he, :].astype(F32)
            at = pl.multiple_of(c * hb + y * hs, hs)
            s_ref[pl.ds(at, hs), :] = part[he : he + hs, :].astype(F32)
            at = pl.multiple_of((c * 2 + y) * hm, hm)
            m_ref[pl.ds(at, hm), :] = part[he + hs :, :].astype(F32)


def ib_body(sc, a_ref, b_ref, c_ref, dq_ref, wt_ref, kv_ref, *outs):
    wide = dq_ref.shape[1]
    tile = dq_ref.shape[2]
    for k in (3, 2, 1, 0):
        cols = pl.ds(mult(sc[Z] ^ k, tile), tile)
        total = a_ref[:, cols].astype(F32) + b_ref[:, cols].astype(F32)
        kv = (total + c_ref[:, cols].astype(F32)).astype(BF)
        kv_ref[k] = kv
        part = tdot(dq_ref[k], wt_ref[:wide, :]) + tdot(kv, wt_ref[wide:, :])
        outs[k][...] = part.astype(BF)


def pair_body(a_ref, b_ref, out_ref):
    out_ref[...] = (a_ref[...].astype(F32) + b_ref[...].astype(F32)).astype(BF)


def fin_body(a_ref, b_ref, c_ref, gf_ref, out_ref):
    total = a_ref[...].astype(F32) + b_ref[...].astype(F32)
    out_ref[...] = (total + c_ref[...].astype(F32) + gf_ref[...]).astype(BF)


def gp_body(sc, dq_ref, kv_ref, x_ref, small_ref, out_ref, acc, line, parts):
    wide = dq_ref.shape[1]
    tile = dq_ref.shape[2]
    half = out_ref.shape[3]
    ones = jnp.ones((8, tile), BF)
    top = bot = s_top = s_bot = 0.0
    for k in range(4):
        rows = x_ref[pl.ds(mult(sc[Z] ^ k, tile), tile), :]
        top = top + dot(dq_ref[k], rows)
        bot = bot + dot(kv_ref[k], rows)
        s_top = s_top + dot_t(ones, dq_ref[k])
        s_bot = s_bot + dot_t(ones, kv_ref[k, wide:, :])
        parts[k] = small_ref[k].astype(F32)
    acc[:wide, :] = top
    acc[wide:, :] = bot
    parts[0] = ((parts[0] + parts[1]) + parts[2]) + parts[3]
    line[...] = jnp.zeros_like(line)
    line[0, 0:1, :wide] = s_top[0:1]
    line[0, 0:1, wide:] = s_bot[0:1]
    line[1, 0:1, :wide] = s_top[0:1]
    line[1, 0:1, wide:] = s_bot[0:1]
    for h in range(2):
        hc = slice(h * half, (h + 1) * half)
        line[h, 1:7, :] = parts[0, 0:6, hc]
        line[h, 7:8, :] = parts[0, pl.ds(8 + sc[Z], 1), hc]
    n_rows = out_ref.shape[2] - 16
    for i in range(2):
        at = pl.multiple_of((sc[C] ^ i) * n_rows, n_rows)
        for m in range(2):
            cols = pl.ds(mult(sc[X] ^ m, half), half)
            out_ref[i, m, :n_rows, :] = acc[pl.ds(at, n_rows), cols].astype(BF)
            out_ref[i, m, n_rows:, :] = line[sc[X] ^ m].astype(BF)


def join_body(dtype, sc, *refs):
    out = refs[4]
    tile = out.shape[0] // 4
    for k in range(4):
        out[pl.ds(mult(sc[Z] ^ k, tile), tile), :] = refs[k][:tile, :].astype(dtype)


def gpfin_body(sc, a_ref, b_ref, out, line, *vecs):
    n_rows = a_ref.shape[0] - 16
    rows = a_ref[n_rows : n_rows + 8, :].astype(F32)
    line[...] = rows
    for i, vec in enumerate(vecs):
        vec[...] = rows[1 + i]
    for i, ref in enumerate((a_ref, b_ref)):
        at = pl.multiple_of((sc[C] ^ i) * n_rows, n_rows)
        out[pl.ds(at, n_rows), :] = ref[:n_rows, :].astype(F32)


def make_device(n_dp, n_ctx, n_t, generic):
    def swap(axis, size, k):
        return lambda v: lax.ppermute(v, axis, [(i, i ^ k) for i in range(size)])

    pc = swap("core", 2, 1)
    py = swap("cy", n_ctx // 2, 1)
    px = swap("dp", n_dp, 1)
    pz = [lambda v: v] + [swap("tensor", n_t, k) for k in range(1, n_t)]

    def on_device(
        tokens,
        cotangent,
        segments,
        pairing,
        project,
        offsets,
        combine,
        baseline,
        scaling,
        shifting,
        expand,
        thresholds,
        shrink,
        settling,
        rescaling,
        reshifting,
    ):
        _, rows, width = tokens.shape
        heads = pairing.shape[0] // n_t
        wide = heads * HD
        tile = rows // n_t
        half = width // 2
        block = expand.shape[1]
        hidden = block * n_t
        hb = block // 2
        hw = wide // 2
        x = tokens[0]
        cot = cotangent[0]
        c = lax.axis_index("core")
        y = lax.axis_index("cy")
        ctx = 2 * y + c
        z = lax.axis_index("tensor")
        dp = lax.axis_index("dp")
        xi = jnp.zeros_like(dp) if generic else dp
        pairs = lax.dynamic_slice_in_dim(pairing, z * heads, heads, 0).reshape(-1)
        sc = jnp.concatenate(
            [jnp.stack([ctx, z, xi, c, y, c, c, c]).astype(jnp.int32), pairs.astype(jnp.int32)]
        )

        def both_halves(v, axis):
            full = lax.all_gather(v, "dp", axis=axis, tiled=True)
            return jnp.split(full, 2, axis=axis)

        wt = jnp.transpose(project, (1, 2, 0)).reshape(3 * wide, -1)
        vectors = [baseline, scaling, shifting, settling, rescaling, reshifting]

        hq = wide // 2
        part = 3 * wide // 2
        def pack(wt_h, e_h, s_h, m_h, off_h, vecs_h):
            return call(
                pack_body,
                (
                    sds((16, half), F32),
                    sds((part + 16, half), BF),
                    sds((half + hb + hw + 16, half), BF),
                ),
                ins=[SM] + [VM] * 12,
                cost=cost(0, 8 * half * width),
            )(sc, wt_h, e_h, s_h, m_h, off_h, *vecs_h)

        vectors = vectors + [thresholds]
        if generic:
            own_wt, other_wt = both_halves(wt, 1)
            parts = [both_halves(v, 0) for v in [expand] + vectors]
            cols = [both_halves(v, 1) for v in (shrink, combine, offsets)]
            packed = [
                pack(
                    w, parts[0][j], cols[0][j], cols[1][j], cols[2][j], [p[j] for p in parts[1:]]
                )
                for j, w in enumerate((own_wt, other_wt))
            ]
            small, wtc = packed[0][0], packed[0][1]
            got_wt = packed[1][1]
            weights = jnp.stack(
                [lax.all_gather(p[2], "tensor", axis=0) for p in packed]
            ).reshape(-1, half)
        else:
            own_wt = wt
            small, wtc, wpack = pack(wt, expand, shrink, combine, offsets, vectors)
            got_wt = px(wtc)
            weights = lax.all_gather(wpack, ("dp", "tensor"), axis=0, tiled=True)

        def after(v, *deps):
            return lax.optimization_barrier((v, *deps))[0]

        got_wt2 = pc(got_wt)

        qT, kvT, wt_full = call(
            qkv_body,
            (
                sds((wide, rows), BF),
                sds((2 * wide, rows), BF),
                sds((3 * wide, width), BF),
            ),
            ins=[SM] + [VM] * 5,
            scratch=[pltpu.VMEM((3 * wide, half), BF), pltpu.VMEM((16, 3 * wide), BF)],
            cost=cost(2 * rows * width * 3 * wide, 4 * rows * width),
        )(sc, x, own_wt, small, got_wt, got_wt2)

        seg = segments[0]
        mine = lax.dynamic_slice_in_dim(seg, c * rows, rows, 0)
        low = jnp.sum((seg[:, None] < mine[None, :]).astype(jnp.int32), axis=0)
        high = jnp.sum((seg[:, None] <= mine[None, :]).astype(jnp.int32), axis=0)
        span = jnp.concatenate(
            [low[None], high[None], jnp.zeros((6, rows), jnp.int32)], axis=0
        )

        par = pc(kvT)
        ra = lax.ppermute(kvT, "cy", [(0, 1)])
        rb = pc(ra)

        kv_scratch = [pltpu.VMEM((2 * wide, 2 * rows), BF), pltpu.VMEM((2 * wide, 2 * rows), BF)]
        o_tiles = [None] * 4
        lses = [None] * 4
        mixed = [None] * 4
        last = qT
        for k in (1, 2, 3, 0):
            last = after(qT, last) if k else after(qT, last, mixed[1])
            o_tiles[k], lses[k] = call(
                functools.partial(fwd_body, k),
                (sds((wide, tile), BF), sds((8 * heads, tile), F32)),
                ins=[SM, VM, VM] + [ANY] * 4,
                scratch=kv_scratch
                + [pltpu.VMEM((B, tile), F32), pltpu.SemaphoreType.DMA((4,))],
                cost=cost(4 * B * tile * wide, 4 * 2 * wide * rows, B * tile * heads),
            )(sc, last, span, kvT, par, ra, rb)
            last = o_tiles[k]
            mixed[k] = pz[k](o_tiles[k])
        weights2 = pc(after(weights, *mixed))

        outs = call(
            mid_body,
            (
                sds((tile + 16, width), BF),
                *[sds((wide, tile), BF)] * 4,
                *[sds((tile, width), BF)] * 3,
                *[sds((tile, hidden // 2), BF)] * 4,
                *[sds((width // 2, tile), BF)] * 2,
                sds((tile, width), F32),
            ),
            ins=[SM] + [VM] * 4 + [ANY] * 4,
            scratch=[
                pltpu.VMEM((width, hidden), BF),
                pltpu.VMEM((hidden, width), BF),
                pltpu.VMEM((width, width), BF),
                pltpu.VMEM((width, tile), BF),
                pltpu.VMEM((tile, hidden), BF),
                pltpu.VMEM((tile, hidden), F32),
                pltpu.VMEM((tile, hidden), BF),
                pltpu.VMEM((8, width), F32),
                pltpu.VMEM((8, hidden), F32),
                pltpu.VMEM((width, tile), BF),
                pltpu.VMEM((8, 16, half), BF),
                pltpu.VMEM((tile, width), BF),
                pltpu.VMEM((tile, width), BF),
                pltpu.VMEM((16, width), F32),
                pltpu.SemaphoreType.DMA((3, 16)),
                pltpu.SemaphoreType.DMA((10,)),
            ],
            cost=cost(8 * tile * width * hidden + 4 * tile * width * width, 4 * width * hidden),
        )(sc, *mixed, x, cot, weights, weights2)
        out_low = outs[0]
        mb = outs[1:5]
        nl, fb, ab, act_own, act_oth, ib_own, ib_oth, mix_own, mix_oth, grad_first = outs[5:]
        grads = [mb[0]] + [pz[k](mb[k]) for k in range(1, 4)]

        theirs = [pc(v) for v in (nl, fb, ab, act_oth, ib_oth, mix_oth)]
        gathered = lax.all_gather(out_low, "tensor", axis=0)
        layer_out = gathered[:, :tile].reshape(rows, width)

        outs = call(
            bwd_body,
            (sds((4, wide, tile), BF), *[sds((2 * wide, rows), BF)] * 4),
            ins=[SM, VM, VM] + [ANY] * 4 + [VM] * 12,
            scratch=kv_scratch
            + [
                pltpu.VMEM((4, wide, tile), BF),
                pltpu.VMEM((4, 8 * heads, tile), F32),
                pltpu.VMEM((4, wide, tile), BF),
                pltpu.VMEM((2 * rows, 2 * HD), F32),
                pltpu.VMEM((2 * rows, 2 * HD), F32),
                pltpu.SemaphoreType.DMA((4,)),
            ],
            cost=cost(10 * B * rows * wide, 4 * 4 * wide * rows, B * rows * heads),
        )(sc, qT, span, kvT, par, ra, rb, *o_tiles, *lses, *grads)
        dq, d_own, d_par, d_r0, d_r1 = outs
        got_par = pc(d_par)
        got_r = pc(d_r1)
        prompt_part = (d_r0.astype(F32) + got_r.astype(F32)).astype(BF)
        nl = after(nl, prompt_part)
        n_part = half // 2 + hb // 2 + hw // 2
        g = call(
            wg_body,
            sds((2, 2, 4, n_part, half), BF),
            ins=[SM] + [VM] * 12,
            cost=cost(4 * tile * width * hidden, 4 * width * hidden),
        )(sc, nl, fb, ab, act_own, ib_own, mix_own, *theirs)
        from_y = lax.ppermute(prompt_part, "cy", [(1, 0)])
        outs = call(
            ib_body,
            (sds((4, 2 * wide, tile), BF), *[sds((tile, width), BF)] * 4),
            ins=[SM] + [VM] * 5,
            cost=cost(2 * rows * width * 3 * wide, 8 * rows * width),
        )(sc, after(d_own, gathered), got_par, from_y, dq, wt_full)
        kv_back, back = outs[0], outs[1:]
        relay = call(pair_body, sds((tile, width), BF), ins=[VM] * 2)(back[2], pz[1](back[3]))
        near = pz[1](back[1])
        far = pz[2](relay)
        gp = call(
            gp_body,
            sds((2, 2, 3 * wide // 2 + 16, half), BF),
            ins=[SM] + [VM] * 4,
            scratch=[
                pltpu.VMEM((3 * wide, width), F32),
                pltpu.VMEM((2, 16, half), F32),
                pltpu.VMEM((4, 16, width), F32),
            ],
            cost=cost(2 * rows * width * 3 * wide, 4 * rows * width),
        )(sc, dq, kv_back, x, after(gathered[:, tile:], layer_out))

        def add(a, b):
            return (a.astype(F32) + b.astype(F32)).astype(BF)

        gp_c = add(gp[0], pc(gp[1]))
        low_tokens = call(
            fin_body,
            sds((tile, width), BF),
            ins=[VM] * 4,
            cost=cost(4 * tile * width, 12 * tile * width),
        )(back[0], near, far, after(grad_first, gp_c))
        gp_c = after(gp_c, low_tokens)
        tiles_near = pz[1](low_tokens)
        tiles_far = pz[2](low_tokens)
        token_tiles = [low_tokens, tiles_near, tiles_far, pz[1](tiles_far)]
        grad_tokens = call(
            functools.partial(join_body, F32),
            sds((rows, width), F32),
            ins=[SM] + [VM] * 4,
            cost=cost(rows * width, 6 * rows * width),
        )(sc, *token_tiles)
        def finish_ff(mine):
            quarters = [mine, py(mine)]
            quarters = quarters + [pc(q) for q in quarters]
            return call(
                wfin_body,
                (sds((half, block), F32), sds((block, half), F32), sds((wide, half), F32)),
                ins=[SM] + [VM] * 4,
            )(sc, *quarters)

        def finish_gp(mine):
            return call(
                gpfin_body,
                (
                    sds((3 * wide, half), F32),
                    sds((8, half), F32),
                    *[sds((half,), F32)] * 7,
                ),
                ins=[SM] + [VM] * 2,
            )(sc, mine, pc(mine))

        gp = add(gp_c, py(gp_c))
        if generic:
            g = lax.psum_scatter(g, "cy", scatter_dimension=0, tiled=False)
            parts = [
                finish_ff(lax.psum_scatter(v, "tensor", scatter_dimension=0, tiled=False))
                for v in (g[0], g[1])
            ]

            def scatter(two, axis):
                full = jnp.concatenate(two, axis=axis).astype(BF)
                return lax.psum_scatter(
                    full, "dp", scatter_dimension=axis, tiled=True
                ).astype(F32)

            summed = [scatter([p[i] for p in parts], i and 1) for i in range(3)]
            both = [finish_gp(gp[j]) for j in range(2)]
            grad_project = scatter([b[0] for b in both], 1)
            grad_offsets = scatter([both[0][1][0].reshape(2, wide)], 1)
            vecs = [scatter([b[2 + i] for b in both], 0) for i in range(7)]
        else:
            g = after(g, from_y)
            g = lax.psum_scatter(
                g.reshape(-1, half), ("cy", "dp"), scatter_dimension=0, tiled=True
            )
            g = after(g, tiles_near)
            g = lax.psum_scatter(g, "tensor", scatter_dimension=0, tiled=True)
            summed = finish_ff(g)
            grad_project, lines, *vecs = finish_gp(add(gp[0], px(gp[1])))
            n_off = offsets.shape[1]
            grad_offsets = lax.dynamic_slice_in_dim(
                lines[0].reshape(2, wide), dp * n_off, n_off, 1
            )
        grad_expand, grad_shrink, grad_combine = summed
        grad_project = jnp.transpose(grad_project.reshape(3, wide, -1), (2, 0, 1))

        return (
            layer_out[None],
            grad_tokens[None],
            grad_project,
            grad_offsets,
            grad_combine,
            vecs[0],
            vecs[1],
            vecs[2],
            grad_expand,
            vecs[6],
            grad_shrink,
            vecs[3],
            vecs[4],
            vecs[5],
        )

    return on_device


def solution(mesh):
    in_specs = (
        P("dp", ("cy", "core"), None),
        P("dp", ("cy", "core"), None),
        P("dp", None),
        P(),
        P("dp", None, "tensor"),
        P(None, ("tensor", "dp")),
        P("tensor", "dp"),
        P("dp"),
        P("dp"),
        P("dp"),
        P("dp", "tensor"),
        P(("tensor", "dp")),
        P("tensor", "dp"),
        P("dp"),
        P("dp"),
        P("dp"),
    )
    out_specs = (
        P("dp", ("cy", "core"), None),
        P("dp", ("cy", "core"), None),
        P("dp", None, "tensor"),
        P(None, ("tensor", "dp")),
        P("tensor", "dp"),
        P("dp"),
        P("dp"),
        P("dp"),
        P("dp", "tensor"),
        P(("tensor", "dp")),
        P("tensor", "dp"),
        P("dp"),
        P("dp"),
        P("dp"),
    )
    n_dp, n_ctx, n_t = mesh.shape["dp"], mesh.shape["ctx"], mesh.shape["tensor"]
    split = Mesh(mesh.devices.reshape(n_dp, n_ctx // 2, 2, n_t), ("dp", "cy", "core", "tensor"))
    on_device = make_device(n_dp, n_ctx, n_t, n_dp != 2)
    return jax.shard_map(
        on_device, mesh=split, in_specs=in_specs, out_specs=out_specs, check_vma=False
    )
```

```python
import functools
import math

import jax
import jax.numpy as jnp
from jax import lax
from jax.experimental import pallas as pl
from jax.experimental.pallas import tpu as pltpu
from jax.sharding import Mesh
from jax.sharding import PartitionSpec as P

P_SIZE = 2048
LMAX = 256
B = 1152
HD = 64
EPS = 1e-06
NEG = -1e30

BF = jnp.bfloat16
F32 = jnp.float32

VM = pl.BlockSpec(memory_space=pltpu.VMEM)
ANY = pl.BlockSpec(memory_space=pl.ANY)
SM = pl.BlockSpec(memory_space=pltpu.SMEM)
LIMIT = 60 << 20


def call(body, outs, scratch=(), ins=None, cost=None):
    out_specs = tuple([VM] * len(outs)) if isinstance(outs, tuple) else VM
    return pl.pallas_call(
        body,
        out_shape=outs,
        in_specs=ins,
        out_specs=out_specs,
        scratch_shapes=scratch,
        cost_estimate=cost,
        compiler_params=pltpu.CompilerParams(vmem_limit_bytes=LIMIT),
    )


def sds(shape, dtype):
    return jax.ShapeDtypeStruct(shape, dtype)


def cost(flops, nbytes, trans=0):
    return pl.CostEstimate(flops=int(flops), bytes_accessed=int(nbytes), transcendentals=int(trans))


def dot(a, b):
    return lax.dot_general(a, b, (((1,), (0,)), ((), ())), preferred_element_type=F32)


def dot_t(a, b):
    return lax.dot_general(a, b, (((1,), (1,)), ((), ())), preferred_element_type=F32)


def tdot(a, b):
    return lax.dot_general(a, b, (((0,), (0,)), ((), ())), preferred_element_type=F32)


def mult(value, by):
    return pl.multiple_of(value * by, by)


CTX, Z, X, C, Y, PAIR = 0, 1, 2, 3, 4, 8


def qkv_body(sc, x_ref, own_ref, small_ref, w0_ref, w1_ref, q_ref, kv_ref, wt_ref, oth, row):
    half = own_ref.shape[1]
    wide = q_ref.shape[0]
    part = own_ref.shape[0] // 2
    hq = wide // 2
    oth[pl.ds(mult(sc[C], part), part), :] = w0_ref[:part, :]
    oth[pl.ds(mult(1 - sc[C], part), part), :] = w1_ref[:part, :]
    mine, theirs = small_ref[...].astype(BF), w0_ref[part:, :]
    even = jnp.where(sc[X] == 0, mine, theirs)
    odd = jnp.where(sc[X] == 0, theirs, mine)
    row[...] = jnp.zeros_like(row)
    for at, rank in ((0, 7), (2 * wide, 8)):
        row[0:1, at : at + hq] = even[rank : rank + 1, :hq]
        row[0:1, at + hq : at + wide] = odd[rank : rank + 1, :hq]
    a0 = x_ref[:, pl.ds(mult(sc[X], half), half)]
    a1 = x_ref[:, pl.ds(mult(1 - sc[X], half), half)]
    first = lax.broadcasted_iota(jnp.int32, (row.shape[0], x_ref.shape[0]), 0) == 0
    bias = tdot(row[...], jnp.where(first, 1.0, 0.0).astype(BF))
    low = (dot_t(own_ref[...], a0) + dot_t(oth[...], a1) + bias).astype(BF)
    q_ref[...] = low[:wide] * jnp.asarray(HD**-0.5, BF)
    kv_ref[...] = low[wide:]
    wt_ref[:, pl.ds(mult(sc[X], half), half)] = own_ref[...]
    wt_ref[:, pl.ds(mult(1 - sc[X], half), half)] = oth[...]


def pack_body(sc, *refs):
    wt, e_ref, s_ref, m_ref, off = refs[0:5]
    vecs = refs[5:12]
    small, wtc, wc, tq = refs[12:16]
    part = wt.shape[0] // 2
    hb = e_ref.shape[1] // 2
    hw = m_ref.shape[0] // 2
    half = s_ref.shape[1]
    c = sc[C]
    small[...] = jnp.zeros_like(small)
    for i, vec in enumerate(vecs):
        small[i : i + 1, :] = vec[...].astype(F32).reshape(1, half)
    small[7:9, : off.shape[1]] = off[...].astype(F32)
    low = small[...].astype(BF)
    wtc[:part, :] = wt[pl.ds(mult(c, part), part), :]
    wtc[part:, :] = low
    hs = hb // 2
    y = sc[Y]
    wc[:half, :] = e_ref[:, pl.ds(mult(c, hb), hb)]
    wc[half:, :] = s_ref[pl.ds(mult(c, hb), hs), :]
    at = 0
    for ref, start, n in (
        (m_ref, (c * 2 + y) * (hw // 2), hw // 2),
        (s_ref, c * hb + hs + y * (hs // 2), hs // 2),
    ):
        tq[at : at + n, :] = ref[pl.ds(pl.multiple_of(start, 16), n), :]
        at += n
    tq[at:, :] = low


def load_pairs(sc, own, par, ra, rb, pbuf, cbuf, sems):
    rows = own.shape[1]
    here = pl.ds(mult(sc[C], rows), rows)
    there = pl.ds(mult(1 - sc[C], rows), rows)

    def run(moves):
        copies = [
            pltpu.make_async_copy(src, dst, sems.at[i]) for i, (src, dst) in enumerate(moves)
        ]
        for copy in copies:
            copy.start()
        for copy in copies:
            copy.wait()

    @pl.when(sc[Y] == 0)
    def _():
        run([(own, pbuf.at[:, here]), (par, pbuf.at[:, there])])

    @pl.when(sc[Y] == 1)
    def _():
        run(
            [
                (ra, pbuf.at[:, here]),
                (rb, pbuf.at[:, there]),
                (own, cbuf.at[:, here]),
                (par, cbuf.at[:, there]),
            ]
        )


def prompt_pass(sc, h, index, start, tile):
    first = jnp.where(start >= B, 1, 0)
    last = jnp.where(start + tile // 2 >= B, 1, 0)
    mixed = jnp.where(first != last, 1, 0)
    blk = jnp.where(index == 0, first, last)
    paired = sc[PAIR + 2 * h + blk]
    lane = lax.broadcasted_iota(jnp.int32, (1, tile), 1)
    wanted = jnp.where(lane >= tile // 2, last, first)
    mine = jnp.where(wanted == blk, 1, 0)
    low = mine * (paired * B)
    high = mine * (B + paired * (P_SIZE - B))
    key_start = pl.multiple_of(paired * (P_SIZE - B), 128)
    return mixed, key_start, low, high


def window_start(sc, t, rows, tile):
    local = sc[C] * rows + t * tile
    return pl.multiple_of(jnp.clip(local - LMAX, 0, 2 * rows - tile - 2 * LMAX), 128)


FAR = 1e30


def attend(src, state, q_h, h, at, n, ok, masks, cols):
    acc, peaks, totals = state
    wide = acc.shape[0]
    h_rows = pl.ds(mult(h, HD), HD)
    v_rows = pl.ds(mult(h, HD) + wide, HD)
    h8 = pl.ds(mult(h, 8), 8)
    place = pl.ds(at, n)
    s = tdot(src[h_rows, place], q_h)
    if masks is not None:
        pos = lax.broadcasted_iota(jnp.int32, s.shape, 0) + at
        s = jnp.where((pos >= masks[0]) & (pos < masks[1]), s, NEG)
    peak = peaks[h8, cols]
    new = jnp.maximum(peak, jnp.max(s, axis=0, keepdims=True))
    cap = new
    if ok is not None:
        new = jnp.where(ok, new, peak)
        cap = jnp.where(ok, new, FAR)
    e = jnp.exp(s - cap[0:1])
    alpha = jnp.exp(peak - new)
    peaks[h8, cols] = new
    totals[h8, cols] = totals[h8, cols] * alpha + jnp.sum(e, axis=0, keepdims=True)
    acc[h_rows, cols] = acc[h_rows, cols] * alpha[0:1] + dot(src[v_rows, place], e.astype(BF))


def attend_prompt(sc, src, state, q_h, h, blk, ok, cols):
    paired = sc[PAIR + 2 * h + blk]
    start = paired * B
    count = 4 - paired

    def run(i, _):
        at = pl.multiple_of(start + i * 256, 128)
        attend(src, state, q_h, h, at, 256, ok, None, cols)
        return 0

    lax.fori_loop(0, count, run, 0)
    at = pl.multiple_of(start + count * 256, 128)
    attend(src, state, q_h, h, at, 128, ok, None, cols)


def load_two(sc, first, second, buf, sems):
    rows = first.shape[1]
    copies = [
        pltpu.make_async_copy(first, buf.at[:, pl.ds(mult(sc[C], rows), rows)], sems.at[0]),
        pltpu.make_async_copy(second, buf.at[:, pl.ds(mult(1 - sc[C], rows), rows)], sems.at[1]),
    ]
    for copy in copies:
        copy.start()
    for copy in copies:
        copy.wait()


def fwd_near_body(sc, q_ref, span_ref, own, par, acc, peaks, totals, buf, sems):
    load_two(sc, own, par, buf, sems)
    rows = own.shape[1]
    tile = rows // 4
    state = (acc, peaks, totals)
    peaks[...] = jnp.full_like(peaks, NEG)
    totals[...] = jnp.zeros_like(totals)
    acc[...] = jnp.zeros_like(acc)
    whole = slice(0, rows)
    lane = lax.broadcasted_iota(jnp.int32, (8, rows), 1)
    late = jnp.logical_not((lane < B - rows) & (sc[CTX] == 1))

    def one_head(h, _):
        h_rows = pl.ds(mult(h, HD), HD)

        @pl.when(sc[Y] == 0)
        def _():
            attend_prompt(sc, buf, state, q_ref[h_rows, :], h, sc[CTX], late, whole)

        @pl.when(sc[CTX] == 1)
        def _():
            early = lax.broadcasted_iota(jnp.int32, (8, tile), 1) < B - rows
            attend_prompt(sc, buf, state, q_ref[h_rows, :tile], h, 0, early, slice(0, tile))

        def window(t, _):
            cols = pl.ds(mult(t, tile), tile)
            at = window_start(sc, t, rows, tile)
            masks = (span_ref[0:1, cols], span_ref[1:2, cols])
            n = tile + 2 * LMAX
            attend(buf, state, q_ref[h_rows, cols], h, at, n, None, masks, cols)
            return 0

        near = jnp.where((sc[Y] == 1) & (sc[PAIR + 2 * h + 1] == 1), 4, 0)
        lax.fori_loop(0, near, window, 0)
        return 0

    lax.fori_loop(0, acc.shape[0] // HD, one_head, 0)


def fwd_far_body(sc, q_ref, ra, rb, acc_in, peaks_in, totals_in, *refs):
    outs = refs[0:4]
    lse_ref = refs[4]
    buf, acc, peaks, totals, sems = refs[5:]
    rows = ra.shape[1]
    tile = outs[0].shape[1]
    acc[...] = acc_in[...]
    peaks[...] = peaks_in[...]
    totals[...] = totals_in[...]

    @pl.when(sc[Y] == 1)
    def _():
        load_two(sc, ra, rb, buf, sems)
        state = (acc, peaks, totals)

        def one_head(h, _):
            q_h = q_ref[pl.ds(mult(h, HD), HD), :]
            attend_prompt(sc, buf, state, q_h, h, 1, None, slice(0, rows))
            return 0

        lax.fori_loop(0, acc.shape[0] // HD, one_head, 0)

    lse_ref[...] = peaks[...] + jnp.log(totals[...])
    for h in range(acc.shape[0] // HD):
        h_rows = slice(h * HD, (h + 1) * HD)
        acc[h_rows, :] = acc[h_rows, :] / totals[8 * h : 8 * h + 1, :]
    for k in range(4):
        outs[k][...] = acc[:, pl.ds(mult(sc[Z] ^ k, tile), tile)].astype(BF)


def bwd_body(
    sc,
    q_ref,
    span_ref,
    own,
    par,
    ra,
    rb,
    *refs,
):
    o_in = refs[0:4]
    lse_s = refs[4]
    g_in = refs[5:9]
    dq_ref, d_own, d_par, d_r0, d_r1 = refs[9:14]
    pbuf, cbuf, o_s, g_s, acc_p, acc_c, p_rows, c_rows, both_s, dq_s, sems = refs[14:]
    load_pairs(sc, own, par, ra, rb, pbuf, cbuf, sems)
    rows = own.shape[1]
    wide, tile = o_in[0].shape
    heads = wide // HD
    for k in range(4):
        cols = pl.ds(mult(sc[Z] ^ k, tile), tile)
        o_s[:, cols] = o_in[k][...]
        g_s[:, cols] = g_in[k][...]
    later = jnp.where(sc[CTX] > 0, 1, 0)
    split = jnp.where(sc[CTX] == 1, 1, 0)
    early = B - rows

    def chunk(src, flat, acc_ref, place, pos, masks, both, lse, delta, h):
        n_q = lse.shape[1]
        pair = dot(flat[place, :], both)
        s = pair[:, :n_q]
        if masks is not None:
            row = lax.broadcasted_iota(jnp.int32, s.shape, 0) + pos
            s = jnp.where((row >= masks[0]) & (row < masks[1]), s, NEG)
        probs = jnp.exp(s - lse)
        ds = (probs * (pair[:, n_q:] - delta)).astype(BF)
        acc_ref[place, :] += dot_t(jnp.concatenate([ds, probs.astype(BF)], axis=1), both)
        return dot(src[pl.ds(mult(h, HD), HD), place], ds)

    def pair_up(q_h, g_h):
        zero = jnp.zeros_like(q_h)
        return jnp.concatenate(
            [jnp.concatenate([q_h, zero], axis=1), jnp.concatenate([zero, g_h], axis=1)], axis=0
        )

    def one_head(h, _):
        h_rows = pl.ds(mult(h, HD), HD)
        v_rows = pl.ds(mult(h, HD) + wide, HD)
        near = jnp.where((sc[Y] == 1) & (sc[PAIR + 2 * h + 1] == 1), 1, 0)

        def turn(src, dst):
            dst[...] = jnp.concatenate([src[h_rows, :], src[v_rows, :]], axis=0).T

        acc_p[...] = jnp.zeros_like(acc_p)
        turn(pbuf, p_rows)

        @pl.when(sc[Y] == 1)
        def _():
            acc_c[...] = jnp.zeros_like(acc_c)

        @pl.when(near == 1)
        def _():
            turn(cbuf, c_rows)

        lse = lse_s[pl.ds(mult(h, 8), 8), :][0:1]
        delta = jnp.sum(
            o_s[h_rows, :].astype(F32) * g_s[h_rows, :].astype(F32), axis=0, keepdims=True
        )
        both_s[...] = pair_up(q_ref[h_rows, :], g_s[h_rows, :])
        dq_s[...] = jnp.zeros_like(dq_s)
        lane = lax.broadcasted_iota(jnp.int32, lse.shape, 1)
        first = (lane < early) & (split == 1)

        def prompt(blk, both, lse, delta, n_q):
            start = sc[PAIR + 2 * h + blk] * B
            count = 4 - sc[PAIR + 2 * h + blk]

            def step(at, n):
                at = pl.multiple_of(at, 128)
                place = pl.ds(at, n)
                dq_s[:, :n_q] += chunk(
                    pbuf, p_rows, acc_p, place, at, None, both, lse, delta, h
                )

            def run(i, _):
                step(start + i * 256, 256)
                return 0

            lax.fori_loop(0, count, run, 0)
            step(start + count * 256, 128)

        prompt(later, both_s[...], jnp.where(first, FAR, lse), delta, rows)

        @pl.when(split == 1)
        def _():
            both = pair_up(q_ref[h_rows, :tile], g_s[h_rows, :tile])
            prompt(0, both, jnp.where(first, lse, FAR)[:, :tile], delta[:, :tile], tile)

        def window(t, _):
            cols = pl.ds(mult(t, tile), tile)
            at = window_start(sc, t, rows, tile)
            n = tile + 2 * LMAX
            masks = (span_ref[0:1, cols], span_ref[1:2, cols])
            g_h = g_s[h_rows, cols]
            d = jnp.sum(o_s[h_rows, cols].astype(F32) * g_h.astype(F32), axis=0, keepdims=True)
            both = pair_up(q_ref[h_rows, cols], g_h)
            l = lse_s[pl.ds(mult(h, 8), 8), cols][0:1]
            dq_s[:, cols] += chunk(
                cbuf, c_rows, acc_c, pl.ds(at, n), at, masks, both, l, d, h
            )
            return 0

        lax.fori_loop(0, 4 * near, window, 0)
        for k in range(4):
            cols = pl.ds(mult(sc[Z] ^ k, tile), tile)
            dq_ref[k, h_rows, :] = (dq_s[:, cols] * HD**-0.5).astype(BF)

        def give(acc, row, out):
            turned = acc[pl.ds(mult(row, rows), rows), :].T.astype(BF)
            out[h_rows, :] = turned[:HD]
            out[pl.ds(mult(h, HD) + wide, HD), :] = turned[HD:]

        @pl.when(sc[Y] == 0)
        def _():
            give(acc_p, sc[C], d_own)
            give(acc_p, 1 - sc[C], d_par)

        @pl.when(sc[Y] == 1)
        def _():
            give(acc_c, sc[C], d_own)
            give(acc_c, 1 - sc[C], d_par)
            give(acc_p, sc[C], d_r0)
            give(acc_p, 1 - sc[C], d_r1)

        return 0

    lax.fori_loop(0, heads, one_head, 0)


def norm(value):
    mean = jnp.mean(value, axis=-1, keepdims=True)
    centred = value - mean
    inv = lax.rsqrt(jnp.mean(centred * centred, axis=-1, keepdims=True) + EPS)
    return centred * inv, inv


def norm_back(e, n, inv):
    return (
        e - jnp.mean(e, axis=-1, keepdims=True) - n * jnp.mean(e * n, axis=-1, keepdims=True)
    ) * inv


def mid_body(sc, *refs):
    mixed = refs[0:4]
    x_hbm, cot_hbm = refs[4:6]
    packs = refs[6:8]
    others = refs[8:24]
    (
        out_ref,
        mb0,
        mb1,
        mb2,
        mb3,
        nl_ref,
        fb_ref,
        ab_ref,
        act_own,
        act_oth,
        ib_own,
        ib_oth,
        mix_own,
        mix_oth,
        gf_ref,
    ) = refs[24:39]
    we, ws, wc, mix_s, act_s, gp_s, ib_s, vec_s, thr_s, mb_s, pk_s, x_ref, cot_ref, small_ref, sems, psems = refs[39:]
    wide, tile = mixed[0].shape
    width = x_ref.shape[1]
    half = width // 2
    hidden = we.shape[1]
    block = hidden // 4
    hb = block // 2
    hw = wide // 2
    c = sc[C]
    hs = hb // 2
    n_pack = half + hs
    n_other = hw // 2 + hs // 2 + 16

    stages = [[], [], []]
    small = []

    def move(stage, src, dst):
        n = len(stages[stage])
        stages[stage].append(pltpu.make_async_copy(src, dst, sems.at[stage, n]))

    for k in range(4):
        z = sc[Z] ^ k
        for j in range(2):
            xc = pl.ds(mult(sc[X] ^ j, half), half)
            for q in range(4):
                cc, yy = c ^ (q // 2), sc[Y] ^ (q % 2)
                piece = others[4 * q + k]
                at = j * n_other
                rows = pl.multiple_of(z * wide + cc * hw + yy * (hw // 2), hw // 2)
                move(0, piece.at[pl.ds(at, hw // 2), :], wc.at[pl.ds(rows, hw // 2), xc])
                rows = z * block + cc * hb + hs + yy * (hs // 2)
                rows = pl.ds(pl.multiple_of(rows, hs // 2), hs // 2)
                move(2, piece.at[pl.ds(at + hw // 2, hs // 2), :], ws.at[rows, xc])
            n = 2 * k + j
            small.append(
                pltpu.make_async_copy(
                    others[k].at[pl.ds(at + hw // 2 + hs // 2, 16), :], pk_s.at[n], psems.at[n]
                )
            )
    for xh in range(2):
        xc = pl.ds(xh * half, half)
        for z in range(4):
            at = (xh * 4 + z) * n_pack
            for i in range(2):
                cc = c ^ i
                place = pl.ds(pl.multiple_of(z * block + cc * hb, hb), hb)
                move(1, packs[i].at[pl.ds(at, half), :], we.at[xc, place])
                place = pl.ds(pl.multiple_of(z * block + cc * hb, hs), hs)
                move(2, packs[i].at[pl.ds(at + half, hs), :], ws.at[place, xc])
    mine = pl.ds(mult(sc[Z], tile), tile)
    small.append(pltpu.make_async_copy(x_hbm.at[mine, :], x_ref, psems.at[8]))
    small.append(pltpu.make_async_copy(cot_hbm.at[mine, :], cot_ref, psems.at[9]))
    for stage in [small] + stages:
        for copy in stage:
            copy.start()

    for copy in small:
        copy.wait()
    for k in range(4):
        mix_s[pl.ds(mult(sc[Z] ^ k, wide), wide), :] = mixed[k][...]
    for k in range(4):
        for j in range(2):
            pack = pk_s[2 * k + j].astype(F32)
            at = pl.multiple_of((sc[Z] ^ k) * block + (sc[X] ^ j) * half, 128)
            thr_s[:, pl.ds(at, half)] = pack[:8]
            if k == 0:
                vec_s[:, pl.ds(mult(sc[X] ^ j, half), half)] = pack[:8]

    baseline = vec_s[0:1, :]
    scaling = vec_s[1:2, :]
    shifting = vec_s[2:3, :]
    settling = vec_s[3:4, :]
    rescaling = vec_s[4:5, :]
    reshifting = vec_s[5:6, :]

    for copy in stages[0]:
        copy.wait()
    first = x_ref[...].astype(F32) + tdot(mix_s[...], wc[...]) + baseline
    n1, inv1 = norm(first)
    normed = n1 * scaling + shifting
    low = normed.astype(BF)
    nl_ref[...] = low
    for copy in stages[1]:
        copy.wait()
    for copy in stages[2]:
        copy.wait()
    feed = jnp.zeros((tile, width), F32)
    for n in range(4):
        cols = slice(n * block, (n + 1) * block)
        inner = dot(low, we[:, cols]) + thr_s[6:7, cols]
        cdf = 0.5 * (1.0 + lax.erf(inner * (0.5**0.5)))
        pdf = jnp.exp(-0.5 * inner * inner) * (1.0 / math.sqrt(2.0 * math.pi))
        active = (inner * cdf).astype(BF)
        act_s[:, cols] = active
        gp_s[:, cols] = cdf + inner * pdf
        feed = feed + dot(active, ws[cols, :])
    second = normed + feed + settling
    n2, inv2 = norm(second)
    out_ref[:tile, :] = (n2 * rescaling + reshifting).astype(BF)
    dy = cot_ref[...].astype(F32)
    small_ref[...] = jnp.zeros_like(small_ref)
    small_ref[4:5, :] = jnp.sum(dy * n2, axis=0, keepdims=True)
    small_ref[5:6, :] = jnp.sum(dy, axis=0, keepdims=True)
    grad = norm_back(rescaling * dy, n2, inv2)
    small_ref[3:4, :] = jnp.sum(grad, axis=0, keepdims=True)
    feed_back = grad.astype(BF)
    fb_ref[...] = feed_back
    for n in range(4):
        cols = slice(n * block, (n + 1) * block)
        inner_back = (dot_t(feed_back, ws[cols, :]) * gp_s[:, cols]).astype(BF)
        ib_s[:, cols] = inner_back
        small_ref[8 + n : 9 + n, :] = jnp.sum(inner_back.astype(F32), axis=0, keepdims=True)
        grad = grad + dot_t(inner_back, we[:, cols])
    small_ref[1:2, :] = jnp.sum(grad * n1, axis=0, keepdims=True)
    small_ref[2:3, :] = jnp.sum(grad, axis=0, keepdims=True)
    grad_first = norm_back(scaling * grad, n1, inv1)
    small_ref[0:1, :] = jnp.sum(grad_first, axis=0, keepdims=True)
    out_ref[tile:, :] = small_ref[...].astype(BF)
    gf_ref[...] = grad_first
    attended_back = grad_first.astype(BF)
    ab_ref[...] = attended_back
    mb_s[...] = dot_t(wc[...], attended_back).astype(BF)
    for k, mb in enumerate((mb0, mb1, mb2, mb3)):
        mb[...] = mb_s[pl.ds(mult(sc[Z] ^ k, wide), wide), :]
    for n in range(4):
        mine = pl.ds(pl.multiple_of(n * block + c * hb, 128), hb)
        other = pl.ds(pl.multiple_of(n * block + (1 - c) * hb, 128), hb)
        cols = slice(n * hb, (n + 1) * hb)
        act_own[:, cols] = act_s[:, mine]
        act_oth[:, cols] = act_s[:, other]
        ib_own[:, cols] = ib_s[:, mine]
        ib_oth[:, cols] = ib_s[:, other]
        mine = pl.ds(pl.multiple_of(n * wide + c * hw, hw), hw)
        other = pl.ds(pl.multiple_of(n * wide + (1 - c) * hw, hw), hw)
        mix_own[n * hw : (n + 1) * hw, :] = mix_s[mine, :]
        mix_oth[n * hw : (n + 1) * hw, :] = mix_s[other, :]


def wg_body(sc, *refs):
    nl, fb, ab, act, ib, mix = [(refs[i], refs[6 + i]) for i in range(6)]
    g_ref = refs[12]
    half = nl[0].shape[1] // 2
    hb = act[0].shape[1] // 4
    hw = mix[0].shape[0] // 4
    for x in range(2):
        xc = slice(x * half, (x + 1) * half)
        for k in range(4):
            z = sc[Z] ^ k
            zc = pl.ds(mult(z, hb), hb)
            e = sum(tdot(nl[i][:, xc], ib[i][:, zc]) for i in range(2)).astype(BF)
            s = sum(tdot(act[i][:, zc], fb[i][:, xc]) for i in range(2)).astype(BF)
            zr = pl.ds(mult(z, hw), hw)
            m = sum(dot(mix[i][zr, :], ab[i][:, xc]) for i in range(2)).astype(BF)
            at = 0
            for v in (e, s, m):
                n = v.shape[0] // 2
                for yh in range(2):
                    g_ref[yh, x, k, at : at + n, :] = v[yh * n : (yh + 1) * n]
                at += n


def wfin_body(sc, *refs):
    quarters = refs[0:4]
    e_ref, s_ref, m_ref = refs[4:7]
    he = e_ref.shape[0] // 2
    hb = e_ref.shape[1] // 2
    hs = hb // 2
    hm = m_ref.shape[0] // 4
    for i in range(2):
        c = sc[C] ^ i
        for j in range(2):
            part = quarters[2 * i + j]
            y = sc[Y] ^ j
            rows = pl.ds(mult(y, he), he)
            e_ref[rows, pl.ds(mult(c, hb), hb)] = part[:he, :].astype(F32)
            at = pl.multiple_of(c * hb + y * hs, hs)
            s_ref[pl.ds(at, hs), :] = part[he : he + hs, :].astype(F32)
            at = pl.multiple_of((c * 2 + y) * hm, hm)
            m_ref[pl.ds(at, hm), :] = part[he + hs :, :].astype(F32)


def ib_body(sc, a_ref, b_ref, c_ref, dq_ref, wt_ref, kv_ref, *outs):
    wide = dq_ref.shape[1]
    tile = dq_ref.shape[2]
    for k in (3, 2, 1, 0):
        cols = pl.ds(mult(sc[Z] ^ k, tile), tile)
        total = a_ref[:, cols].astype(F32) + b_ref[:, cols].astype(F32)
        kv = (total + c_ref[:, cols].astype(F32)).astype(BF)
        kv_ref[k] = kv
        part = tdot(dq_ref[k], wt_ref[:wide, :]) + tdot(kv, wt_ref[wide:, :])
        outs[k][...] = part.astype(BF)


def pair_body(a_ref, b_ref, out_ref):
    out_ref[...] = (a_ref[...].astype(F32) + b_ref[...].astype(F32)).astype(BF)


def fin_body(a_ref, b_ref, c_ref, gf_ref, out_ref):
    total = a_ref[...].astype(F32) + b_ref[...].astype(F32)
    out_ref[...] = (total + c_ref[...].astype(F32) + gf_ref[...]).astype(BF)


def gp_body(sc, dq_ref, kv_ref, x_ref, small_ref, out_ref, acc, line, parts):
    wide = dq_ref.shape[1]
    tile = dq_ref.shape[2]
    half = out_ref.shape[3]
    ones = jnp.ones((8, tile), BF)
    top = bot = s_top = s_bot = 0.0
    for k in range(4):
        rows = x_ref[pl.ds(mult(sc[Z] ^ k, tile), tile), :]
        top = top + dot(dq_ref[k], rows)
        bot = bot + dot(kv_ref[k], rows)
        s_top = s_top + dot_t(ones, dq_ref[k])
        s_bot = s_bot + dot_t(ones, kv_ref[k, wide:, :])
        parts[k] = small_ref[k].astype(F32)
    acc[:wide, :] = top
    acc[wide:, :] = bot
    parts[0] = ((parts[0] + parts[1]) + parts[2]) + parts[3]
    line[...] = jnp.zeros_like(line)
    line[0, 0:1, :wide] = s_top[0:1]
    line[0, 0:1, wide:] = s_bot[0:1]
    line[1, 0:1, :wide] = s_top[0:1]
    line[1, 0:1, wide:] = s_bot[0:1]
    for h in range(2):
        hc = slice(h * half, (h + 1) * half)
        line[h, 1:7, :] = parts[0, 0:6, hc]
        line[h, 7:8, :] = parts[0, pl.ds(8 + sc[Z], 1), hc]
    n_rows = out_ref.shape[2] - 16
    for i in range(2):
        at = pl.multiple_of((sc[C] ^ i) * n_rows, n_rows)
        for m in range(2):
            cols = pl.ds(mult(sc[X] ^ m, half), half)
            out_ref[i, m, :n_rows, :] = acc[pl.ds(at, n_rows), cols].astype(BF)
            out_ref[i, m, n_rows:, :] = line[sc[X] ^ m].astype(BF)


def join_body(dtype, sc, *refs):
    out = refs[4]
    tile = out.shape[0] // 4
    for k in range(4):
        out[pl.ds(mult(sc[Z] ^ k, tile), tile), :] = refs[k][:tile, :].astype(dtype)


def gpfin_body(sc, a_ref, b_ref, out, line, *vecs):
    n_rows = a_ref.shape[0] - 16
    rows = a_ref[n_rows : n_rows + 8, :].astype(F32)
    line[...] = rows
    for i, vec in enumerate(vecs):
        vec[...] = rows[1 + i]
    for i, ref in enumerate((a_ref, b_ref)):
        at = pl.multiple_of((sc[C] ^ i) * n_rows, n_rows)
        out[pl.ds(at, n_rows), :] = ref[:n_rows, :].astype(F32)


def make_device(n_dp, n_ctx, n_t, generic):
    def swap(axis, size, k):
        return lambda v: lax.ppermute(v, axis, [(i, i ^ k) for i in range(size)])

    pc = swap("core", 2, 1)
    py = swap("cy", n_ctx // 2, 1)
    px = swap("dp", n_dp, 1)
    pz = [lambda v: v] + [swap("tensor", n_t, k) for k in range(1, n_t)]

    def on_device(
        tokens,
        cotangent,
        segments,
        pairing,
        project,
        offsets,
        combine,
        baseline,
        scaling,
        shifting,
        expand,
        thresholds,
        shrink,
        settling,
        rescaling,
        reshifting,
    ):
        _, rows, width = tokens.shape
        heads = pairing.shape[0] // n_t
        wide = heads * HD
        tile = rows // n_t
        half = width // 2
        block = expand.shape[1]
        hidden = block * n_t
        hb = block // 2
        hw = wide // 2
        x = tokens[0]
        cot = cotangent[0]
        c = lax.axis_index("core")
        y = lax.axis_index("cy")
        ctx = 2 * y + c
        z = lax.axis_index("tensor")
        dp = lax.axis_index("dp")
        xi = jnp.zeros_like(dp) if generic else dp
        pairs = lax.dynamic_slice_in_dim(pairing, z * heads, heads, 0).reshape(-1)
        sc = jnp.concatenate(
            [jnp.stack([ctx, z, xi, c, y, c, c, c]).astype(jnp.int32), pairs.astype(jnp.int32)]
        )

        def both_halves(v, axis):
            full = lax.all_gather(v, "dp", axis=axis, tiled=True)
            return jnp.split(full, 2, axis=axis)

        wt = jnp.transpose(project, (1, 2, 0)).reshape(3 * wide, -1)
        vectors = [baseline, scaling, shifting, settling, rescaling, reshifting]

        hq = wide // 2
        part = 3 * wide // 2
        def pack(wt_h, e_h, s_h, m_h, off_h, vecs_h):
            return call(
                pack_body,
                (
                    sds((16, half), F32),
                    sds((part + 16, half), BF),
                    sds((half + hb // 2, half), BF),
                    sds((hw // 2 + hb // 4 + 16, half), BF),
                ),
                ins=[SM] + [VM] * 12,
                cost=cost(0, 8 * half * width),
            )(sc, wt_h, e_h, s_h, m_h, off_h, *vecs_h)

        vectors = vectors + [thresholds]
        if generic:
            own_wt, other_wt = both_halves(wt, 1)
            parts = [both_halves(v, 0) for v in [expand] + vectors]
            cols = [both_halves(v, 1) for v in (shrink, combine, offsets)]
            packed = [
                pack(
                    w, parts[0][j], cols[0][j], cols[1][j], cols[2][j], [p[j] for p in parts[1:]]
                )
                for j, w in enumerate((own_wt, other_wt))
            ]
            small, wtc = packed[0][0], packed[0][1]
            got_wt = packed[1][1]
            weights = jnp.stack(
                [lax.all_gather(p[2], "tensor", axis=0) for p in packed]
            ).reshape(-1, half)
            other_wide = jnp.concatenate([p[3] for p in packed])
        else:
            own_wt = wt
            small, wtc, wpack, o_c = pack(wt, expand, shrink, combine, offsets, vectors)
            got_wt = px(wtc)
            weights = lax.all_gather(wpack, ("dp", "tensor"), axis=0, tiled=True)
            other_wide = jnp.concatenate([o_c, px(o_c)])

        def after(v, *deps):
            return lax.optimization_barrier((v, *deps))[0]

        got_wt2 = after(pc(got_wt), other_wide)

        qT, kvT, wt_full = call(
            qkv_body,
            (
                sds((wide, rows), BF),
                sds((2 * wide, rows), BF),
                sds((3 * wide, width), BF),
            ),
            ins=[SM] + [VM] * 5,
            scratch=[pltpu.VMEM((3 * wide, half), BF), pltpu.VMEM((16, 3 * wide), BF)],
            cost=cost(2 * rows * width * 3 * wide, 4 * rows * width),
        )(sc, x, own_wt, small, got_wt, got_wt2)

        seg = segments[0]
        mine = lax.dynamic_slice_in_dim(seg, c * rows, rows, 0)
        low = jnp.sum((seg[:, None] < mine[None, :]).astype(jnp.int32), axis=0)
        high = jnp.sum((seg[:, None] <= mine[None, :]).astype(jnp.int32), axis=0)
        span = jnp.concatenate(
            [low[None], high[None], jnp.zeros((6, rows), jnp.int32)], axis=0
        )

        z_near = pz[1](other_wide)
        z_far = pz[2](other_wide)
        other_z = [other_wide, z_near, z_far, pz[1](z_far)]

        par = pc(kvT)
        ra = lax.ppermute(kvT, "cy", [(0, 1)])

        kv_scratch = [pltpu.VMEM((2 * wide, 2 * rows), BF), pltpu.VMEM((2 * wide, 2 * rows), BF)]
        state = [
            sds((wide, rows), F32),
            sds((8 * heads, rows), F32),
            sds((8 * heads, rows), F32),
        ]
        sofar = call(
            fwd_near_body,
            tuple(state),
            ins=[SM, VM, VM] + [ANY] * 2,
            scratch=[kv_scratch[0], pltpu.SemaphoreType.DMA((2,))],
            cost=cost(0, 1000),
        )(sc, qT, span, kvT, par)
        ra = after(ra, sofar[0])
        rb = pc(after(ra, z_near, z_far))
        other_y = [py(after(w, ra)) for w in other_z[:3]]
        *o_tiles, lse = call(
            fwd_far_body,
            (*[sds((wide, tile), BF)] * 4, sds((8 * heads, rows), F32)),
            ins=[SM, VM] + [ANY] * 2 + [VM] * 3,
            scratch=[kv_scratch[0]]
            + [pltpu.VMEM(v.shape, v.dtype) for v in state]
            + [pltpu.SemaphoreType.DMA((2,))],
            cost=cost(0, 1000),
        )(sc, qT, ra, rb, *sofar)
        relayed = after(other_z[3], o_tiles[0])
        o_tiles = [after(o, *other_y, relayed) for o in o_tiles]
        other_y = other_y + [py(relayed)]
        mixed = [pz[k](o_tiles[k]) for k in range(4)]
        weights2 = pc(after(weights, *mixed, other_y[3]))
        others = other_z + other_y
        others = others + [pc(after(w, o_tiles[0])) for w in others]

        outs = call(
            mid_body,
            (
                sds((tile + 16, width), BF),
                *[sds((wide, tile), BF)] * 4,
                *[sds((tile, width), BF)] * 3,
                *[sds((tile, hidden // 2), BF)] * 4,
                *[sds((width // 2, tile), BF)] * 2,
                sds((tile, width), F32),
            ),
            ins=[SM] + [VM] * 4 + [ANY] * 20,
            scratch=[
                pltpu.VMEM((width, hidden), BF),
                pltpu.VMEM((hidden, width), BF),
                pltpu.VMEM((width, width), BF),
                pltpu.VMEM((width, tile), BF),
                pltpu.VMEM((tile, hidden), BF),
                pltpu.VMEM((tile, hidden), F32),
                pltpu.VMEM((tile, hidden), BF),
                pltpu.VMEM((8, width), F32),
                pltpu.VMEM((8, hidden), F32),
                pltpu.VMEM((width, tile), BF),
                pltpu.VMEM((8, 16, half), BF),
                pltpu.VMEM((tile, width), BF),
                pltpu.VMEM((tile, width), BF),
                pltpu.VMEM((16, width), F32),
                pltpu.SemaphoreType.DMA((3, 48)),
                pltpu.SemaphoreType.DMA((10,)),
            ],
            cost=cost(8 * tile * width * hidden + 4 * tile * width * width, 4 * width * hidden),
        )(sc, *mixed, x, cot, weights, weights2, *others)
        out_low = outs[0]
        mb = outs[1:5]
        nl, fb, ab, act_own, act_oth, ib_own, ib_oth, mix_own, mix_oth, grad_first = outs[5:]
        grads = [mb[0]] + [pz[k](mb[k]) for k in range(1, 4)]

        theirs = [pc(v) for v in (nl, fb, ab, act_oth, ib_oth, mix_oth)]
        gathered = lax.all_gather(out_low, "tensor", axis=0)

        outs = call(
            bwd_body,
            (sds((4, wide, tile), BF), *[sds((2 * wide, rows), BF)] * 4),
            ins=[SM, VM, VM] + [ANY] * 4 + [VM] * 9,
            scratch=kv_scratch
            + [
                pltpu.VMEM((wide, rows), BF),
                pltpu.VMEM((wide, rows), BF),
                pltpu.VMEM((2 * rows, 2 * HD), F32),
                pltpu.VMEM((2 * rows, 2 * HD), F32),
                pltpu.VMEM((2 * rows, 2 * HD), BF),
                pltpu.VMEM((2 * rows, 2 * HD), BF),
                pltpu.VMEM((2 * HD, 2 * rows), BF),
                pltpu.VMEM((HD, rows), F32),
                pltpu.SemaphoreType.DMA((4,)),
            ],
            cost=cost(10 * B * rows * wide, 4 * 4 * wide * rows, B * rows * heads),
        )(sc, qT, span, kvT, par, ra, rb, *o_tiles, lse, *grads)
        dq, d_own, d_par, d_r0, d_r1 = outs
        got_par = pc(d_par)
        got_r = pc(d_r1)
        prompt_part = (d_r0.astype(F32) + got_r.astype(F32)).astype(BF)
        nl = after(nl, prompt_part, got_par)
        n_part = half // 2 + hb // 2 + hw // 2
        g = call(
            wg_body,
            sds((2, 2, 4, n_part, half), BF),
            ins=[SM] + [VM] * 12,
            cost=cost(4 * tile * width * hidden, 4 * width * hidden),
        )(sc, nl, fb, ab, act_own, ib_own, mix_own, *theirs)
        from_y = lax.ppermute(prompt_part, "cy", [(1, 0)])
        outs = call(
            ib_body,
            (sds((4, 2 * wide, tile), BF), *[sds((tile, width), BF)] * 4),
            ins=[SM] + [VM] * 5,
            cost=cost(2 * rows * width * 3 * wide, 8 * rows * width),
        )(sc, after(d_own, gathered), got_par, from_y, dq, wt_full)
        kv_back, back = outs[0], outs[1:]
        gathered = after(gathered, kv_back)
        layer_out = gathered[:, :tile].reshape(rows, width)
        passed = pz[1](back[3])
        relay = call(pair_body, sds((tile, width), BF), ins=[VM] * 2)(back[2], passed)
        near = pz[1](after(back[1], passed))
        far = pz[2](relay)
        gp = call(
            gp_body,
            sds((2, 2, 3 * wide // 2 + 16, half), BF),
            ins=[SM] + [VM] * 4,
            scratch=[
                pltpu.VMEM((3 * wide, width), F32),
                pltpu.VMEM((2, 16, half), F32),
                pltpu.VMEM((4, 16, width), F32),
            ],
            cost=cost(2 * rows * width * 3 * wide, 4 * rows * width),
        )(sc, dq, kv_back, x, after(gathered[:, tile:], layer_out))

        def add(a, b):
            return (a.astype(F32) + b.astype(F32)).astype(BF)

        gp_c = add(gp[0], pc(gp[1]))
        low_tokens = call(
            fin_body,
            sds((tile, width), BF),
            ins=[VM] * 4,
            cost=cost(4 * tile * width, 12 * tile * width),
        )(back[0], near, far, after(grad_first, gp_c))
        gp_c = after(gp_c, low_tokens)
        tiles_near = pz[1](low_tokens)
        tiles_far = pz[2](low_tokens)
        token_tiles = [low_tokens, tiles_near, tiles_far, pz[1](tiles_far)]
        grad_tokens = call(
            functools.partial(join_body, F32),
            sds((rows, width), F32),
            ins=[SM] + [VM] * 4,
            cost=cost(rows * width, 6 * rows * width),
        )(sc, *token_tiles)
        def sum_z(parts, wait=()):
            relay = after(add(parts[2], pz[1](parts[3])), *wait)
            near = pz[1](parts[1])
            far = pz[2](relay)
            total = parts[0].astype(F32) + near.astype(F32) + far.astype(F32)
            return total.astype(BF)

        def finish_ff(mine, *wait):
            quarters = [mine, after(py(mine), *wait)]
            quarters = quarters + [pc(q) for q in quarters]
            return call(
                wfin_body,
                (sds((half, block), F32), sds((block, half), F32), sds((wide, half), F32)),
                ins=[SM] + [VM] * 4,
            )(sc, *quarters)

        def finish_gp(mine):
            return call(
                gpfin_body,
                (
                    sds((3 * wide, half), F32),
                    sds((8, half), F32),
                    *[sds((half,), F32)] * 7,
                ),
                ins=[SM] + [VM] * 2,
            )(sc, mine, pc(mine))

        gp = add(gp_c, py(gp_c))
        if generic:
            g = lax.psum_scatter(g, "cy", scatter_dimension=0, tiled=False)
            parts = [
                finish_ff(sum_z(v))
                for v in (g[0], g[1])
            ]

            def scatter(two, axis):
                full = jnp.concatenate(two, axis=axis).astype(BF)
                return lax.psum_scatter(
                    full, "dp", scatter_dimension=axis, tiled=True
                ).astype(F32)

            summed = [scatter([p[i] for p in parts], i and 1) for i in range(3)]
            both = [finish_gp(gp[j]) for j in range(2)]
            grad_project = scatter([b[0] for b in both], 1)
            grad_offsets = scatter([both[0][1][0].reshape(2, wide)], 1)
            vecs = [scatter([b[2 + i] for b in both], 0) for i in range(7)]
        else:
            g = after(g, from_y)
            g = lax.psum_scatter(
                g.reshape(-1, half), ("cy", "dp"), scatter_dimension=0, tiled=True
            )
            g = after(g, tiles_near, tiles_far)
            g = sum_z(g.reshape(4, n_part, half))
            grad_project, lines, *vecs = finish_gp(add(gp[0], px(gp[1])))
            summed = finish_ff(g, grad_tokens, layer_out, grad_project)
            n_off = offsets.shape[1]
            grad_offsets = lax.dynamic_slice_in_dim(
                lines[0].reshape(2, wide), dp * n_off, n_off, 1
            )
        grad_expand, grad_shrink, grad_combine = summed
        grad_project = jnp.transpose(grad_project.reshape(3, wide, -1), (2, 0, 1))

        return (
            layer_out[None],
            grad_tokens[None],
            grad_project,
            grad_offsets,
            grad_combine,
            vecs[0],
            vecs[1],
            vecs[2],
            grad_expand,
            vecs[6],
            grad_shrink,
            vecs[3],
            vecs[4],
            vecs[5],
        )

    return on_device


def solution(mesh):
    in_specs = (
        P("dp", ("cy", "core"), None),
        P("dp", ("cy", "core"), None),
        P("dp", None),
        P(),
        P("dp", None, "tensor"),
        P(None, ("tensor", "dp")),
        P("tensor", "dp"),
        P("dp"),
        P("dp"),
        P("dp"),
        P("dp", "tensor"),
        P(("tensor", "dp")),
        P("tensor", "dp"),
        P("dp"),
        P("dp"),
        P("dp"),
    )
    out_specs = (
        P("dp", ("cy", "core"), None),
        P("dp", ("cy", "core"), None),
        P("dp", None, "tensor"),
        P(None, ("tensor", "dp")),
        P("tensor", "dp"),
        P("dp"),
        P("dp"),
        P("dp"),
        P("dp", "tensor"),
        P(("tensor", "dp")),
        P("tensor", "dp"),
        P("dp"),
        P("dp"),
        P("dp"),
    )
    n_dp, n_ctx, n_t = mesh.shape["dp"], mesh.shape["ctx"], mesh.shape["tensor"]
    split = Mesh(mesh.devices.reshape(n_dp, n_ctx // 2, 2, n_t), ("dp", "cy", "core", "tensor"))
    on_device = make_device(n_dp, n_ctx, n_t, n_dp != 2)
    return jax.shard_map(
        on_device, mesh=split, in_specs=in_specs, out_specs=out_specs, check_vma=False
    )
```

```python
import functools
import math

import jax
import jax.numpy as jnp
from jax import lax
from jax.experimental import pallas as pl
from jax.experimental.pallas import tpu as pltpu
from jax.sharding import Mesh
from jax.sharding import PartitionSpec as P

P_SIZE = 2048
LMAX = 256
B = 1152
HD = 64
EPS = 1e-06
NEG = -1e30

BF = jnp.bfloat16
F32 = jnp.float32

VM = pl.BlockSpec(memory_space=pltpu.VMEM)
ANY = pl.BlockSpec(memory_space=pl.ANY)
SM = pl.BlockSpec(memory_space=pltpu.SMEM)
LIMIT = 60 << 20


def call(body, outs, scratch=(), ins=None, cost=None):
    out_specs = tuple([VM] * len(outs)) if isinstance(outs, tuple) else VM
    return pl.pallas_call(
        body,
        out_shape=outs,
        in_specs=ins,
        out_specs=out_specs,
        scratch_shapes=scratch,
        cost_estimate=cost,
        compiler_params=pltpu.CompilerParams(vmem_limit_bytes=LIMIT),
    )


def gathered_rows(n):
    return n // 3


def sds(shape, dtype):
    return jax.ShapeDtypeStruct(shape, dtype)


def cost(flops, nbytes, trans=0):
    return pl.CostEstimate(flops=int(flops), bytes_accessed=int(nbytes), transcendentals=int(trans))


def dot(a, b):
    return lax.dot_general(a, b, (((1,), (0,)), ((), ())), preferred_element_type=F32)


def dot_t(a, b):
    return lax.dot_general(a, b, (((1,), (1,)), ((), ())), preferred_element_type=F32)


def tdot(a, b):
    return lax.dot_general(a, b, (((0,), (0,)), ((), ())), preferred_element_type=F32)


def mult(value, by):
    return pl.multiple_of(value * by, by)


CTX, Z, X, C, Y, PAIR = 0, 1, 2, 3, 4, 8


def qkv_body(sc, x_ref, own_ref, small_ref, w0_ref, w1_ref, q_ref, kv_ref, wt_ref, oth, row):
    half = own_ref.shape[1]
    wide = q_ref.shape[0]
    part = own_ref.shape[0] // 2
    hq = wide // 2
    oth[pl.ds(mult(sc[C], part), part), :] = w0_ref[:part, :]
    oth[pl.ds(mult(1 - sc[C], part), part), :] = w1_ref[:part, :]
    mine, theirs = small_ref[...].astype(BF), w0_ref[part:, :]
    even = jnp.where(sc[X] == 0, mine, theirs)
    odd = jnp.where(sc[X] == 0, theirs, mine)
    row[...] = jnp.zeros_like(row)
    for at, rank in ((0, 7), (2 * wide, 8)):
        row[0:1, at : at + hq] = even[rank : rank + 1, :hq]
        row[0:1, at + hq : at + wide] = odd[rank : rank + 1, :hq]
    a0 = x_ref[:, pl.ds(mult(sc[X], half), half)]
    a1 = x_ref[:, pl.ds(mult(1 - sc[X], half), half)]
    first = lax.broadcasted_iota(jnp.int32, (row.shape[0], x_ref.shape[0]), 0) == 0
    bias = tdot(row[...], jnp.where(first, 1.0, 0.0).astype(BF))
    low = (dot_t(own_ref[...], a0) + dot_t(oth[...], a1) + bias).astype(BF)
    q_ref[...] = low[:wide] * jnp.asarray(HD**-0.5, BF)
    kv_ref[...] = low[wide:]
    wt_ref[:, pl.ds(mult(sc[X], half), half)] = own_ref[...]
    wt_ref[:, pl.ds(mult(1 - sc[X], half), half)] = oth[...]


def pack_body(sc, *refs):
    wt, e_ref, s_ref, m_ref, off = refs[0:5]
    vecs = refs[5:12]
    small, wtc, wc, tq = refs[12:16]
    part = wt.shape[0] // 2
    hb = e_ref.shape[1] // 2
    hw = m_ref.shape[0] // 2
    half = s_ref.shape[1]
    c = sc[C]
    small[...] = jnp.zeros_like(small)
    for i, vec in enumerate(vecs):
        small[i : i + 1, :] = vec[...].astype(F32).reshape(1, half)
    small[7:9, : off.shape[1]] = off[...].astype(F32)
    low = small[...].astype(BF)
    wtc[:part, :] = wt[pl.ds(mult(c, part), part), :]
    wtc[part:, :] = low
    hs = wc.shape[0] - half
    ht = hb - hs
    y = sc[Y]
    wc[:half, :] = e_ref[:, pl.ds(mult(c, hb), hb)]
    wc[half:, :] = s_ref[pl.ds(mult(c, hb), hs), :]
    at = 0
    for ref, start, n in (
        (m_ref, (c * 2 + y) * (hw // 2), hw // 2),
        (s_ref, c * hb + hs + y * (ht // 2), ht // 2),
    ):
        tq[at : at + n, :] = ref[pl.ds(pl.multiple_of(start, 16), n), :]
        at += n
    tq[at:, :] = low


def load_pairs(sc, own, par, ra, rb, pbuf, cbuf, sems):
    rows = own.shape[1]
    here = pl.ds(mult(sc[C], rows), rows)
    there = pl.ds(mult(1 - sc[C], rows), rows)

    def run(moves):
        copies = [
            pltpu.make_async_copy(src, dst, sems.at[i]) for i, (src, dst) in enumerate(moves)
        ]
        for copy in copies:
            copy.start()
        for copy in copies:
            copy.wait()

    @pl.when(sc[Y] == 0)
    def _():
        run([(own, pbuf.at[:, here]), (par, pbuf.at[:, there])])

    @pl.when(sc[Y] == 1)
    def _():
        run(
            [
                (ra, pbuf.at[:, here]),
                (rb, pbuf.at[:, there]),
                (own, cbuf.at[:, here]),
                (par, cbuf.at[:, there]),
            ]
        )


def window_start(sc, t, rows, tile):
    local = sc[C] * rows + t * tile
    return pl.multiple_of(jnp.clip(local - LMAX, 0, 2 * rows - tile - 2 * LMAX), 128)


FAR = 1e30


def attend(src, state, q_h, h, at, n, ok, masks, cols):
    acc, peaks, totals = state
    wide = acc.shape[0]
    h_rows = pl.ds(mult(h, HD), HD)
    v_rows = pl.ds(mult(h, HD) + wide, HD)
    h8 = pl.ds(mult(h, 8), 8)
    place = pl.ds(at, n)
    s = tdot(src[h_rows, place], q_h)
    if masks is not None:
        pos = lax.broadcasted_iota(jnp.int32, s.shape, 0) + at
        s = jnp.where((pos >= masks[0]) & (pos < masks[1]), s, NEG)
    peak = peaks[h8, cols]
    new = jnp.maximum(peak, jnp.max(s, axis=0, keepdims=True))
    cap = new
    if ok is not None:
        new = jnp.where(ok, new, peak)
        cap = jnp.where(ok, new, FAR)
    e = jnp.exp(s - cap[0:1])
    alpha = jnp.exp(peak - new)
    peaks[h8, cols] = new
    totals[h8, cols] = totals[h8, cols] * alpha + jnp.sum(e, axis=0, keepdims=True)
    acc[h_rows, cols] = acc[h_rows, cols] * alpha[0:1] + dot(src[v_rows, place], e.astype(BF))


def whole_block(paired):
    at = pl.multiple_of(paired * (P_SIZE - B), 128)
    return at, (paired * B, B + paired * (P_SIZE - B))


def attend_prompt(sc, src, state, q_h, h, blk, ok, cols):
    paired = sc[PAIR + 2 * h + blk]
    start = paired * B
    count = 4 - paired

    def run(i, _):
        at = pl.multiple_of(start + i * 256, 128)
        attend(src, state, q_h, h, at, 256, ok, None, cols)
        return 0

    lax.fori_loop(0, count, run, 0)
    at = pl.multiple_of(start + count * 256, 128)
    attend(src, state, q_h, h, at, 128, ok, None, cols)


def load_two(sc, first, second, buf, sems):
    rows = first.shape[1]
    copies = [
        pltpu.make_async_copy(first, buf.at[:, pl.ds(mult(sc[C], rows), rows)], sems.at[0]),
        pltpu.make_async_copy(second, buf.at[:, pl.ds(mult(1 - sc[C], rows), rows)], sems.at[1]),
    ]
    for copy in copies:
        copy.start()
    for copy in copies:
        copy.wait()


def fwd_near_body(sc, q_ref, span_ref, own, par, acc, peaks, totals, buf, sems):
    load_two(sc, own, par, buf, sems)
    rows = own.shape[1]
    tile = rows // 4
    state = (acc, peaks, totals)
    peaks[...] = jnp.full_like(peaks, NEG)
    totals[...] = jnp.zeros_like(totals)
    acc[...] = jnp.zeros_like(acc)
    whole = slice(0, rows)
    lane = lax.broadcasted_iota(jnp.int32, (8, rows), 1)
    late = jnp.logical_not((lane < B - rows) & (sc[CTX] == 1))

    def one_head(h, _):
        h_rows = pl.ds(mult(h, HD), HD)

        @pl.when(sc[Y] == 0)
        def _():
            attend_prompt(sc, buf, state, q_ref[h_rows, :], h, sc[CTX], late, whole)

        @pl.when(sc[CTX] == 1)
        def _():
            early = B - rows
            at, masks = whole_block(sc[PAIR + 2 * h])
            attend(buf, state, q_ref[h_rows, :early], h, at, B, None, masks, slice(0, early))

        def window(t, _):
            cols = pl.ds(mult(t, tile), tile)
            at = window_start(sc, t, rows, tile)
            masks = (span_ref[0:1, cols], span_ref[1:2, cols])
            n = tile + 2 * LMAX
            attend(buf, state, q_ref[h_rows, cols], h, at, n, None, masks, cols)
            return 0

        near = jnp.where((sc[Y] == 1) & (sc[PAIR + 2 * h + 1] == 1), 4, 0)
        lax.fori_loop(0, near, window, 0)
        return 0

    lax.fori_loop(0, acc.shape[0] // HD, one_head, 0)


def fwd_far_body(sc, q_ref, ra, rb, acc_in, peaks_in, totals_in, *refs):
    outs = refs[0:4]
    lse_ref = refs[4]
    buf, acc, peaks, totals, sems = refs[5:]
    rows = ra.shape[1]
    tile = outs[0].shape[1]
    acc[...] = acc_in[...]
    peaks[...] = peaks_in[...]
    totals[...] = totals_in[...]

    @pl.when(sc[Y] == 1)
    def _():
        load_two(sc, ra, rb, buf, sems)
        state = (acc, peaks, totals)

        def one_head(h, _):
            q_h = q_ref[pl.ds(mult(h, HD), HD), :]
            attend_prompt(sc, buf, state, q_h, h, 1, None, slice(0, rows))
            return 0

        lax.fori_loop(0, acc.shape[0] // HD, one_head, 0)

    lse_ref[...] = peaks[...] + jnp.log(totals[...])
    for h in range(acc.shape[0] // HD):
        h_rows = slice(h * HD, (h + 1) * HD)
        acc[h_rows, :] = acc[h_rows, :] / totals[8 * h : 8 * h + 1, :]
    for k in range(4):
        outs[k][...] = acc[:, pl.ds(mult(sc[Z] ^ k, tile), tile)].astype(BF)


def bwd_body(
    sc,
    q_ref,
    span_ref,
    own,
    par,
    ra,
    rb,
    *refs,
):
    o_in = refs[0:4]
    lse_s = refs[4]
    g_in = refs[5:9]
    dq_ref, d_own, d_par, d_r0, d_r1 = refs[9:14]
    pbuf, cbuf, o_s, g_s, acc_p, acc_c, p_rows, c_rows, both_s, dq_s, sems = refs[14:]
    load_pairs(sc, own, par, ra, rb, pbuf, cbuf, sems)
    rows = own.shape[1]
    wide, tile = o_in[0].shape
    heads = wide // HD
    for k in range(4):
        cols = pl.ds(mult(sc[Z] ^ k, tile), tile)
        o_s[:, cols] = o_in[k][...]
        g_s[:, cols] = g_in[k][...]
    later = jnp.where(sc[CTX] > 0, 1, 0)
    split = jnp.where(sc[CTX] == 1, 1, 0)
    early = B - rows

    def chunk(src, flat, acc_ref, place, pos, masks, both, lse, delta, h):
        n_q = lse.shape[1]
        pair = dot(flat[place, :], both)
        s = pair[:, :n_q]
        if masks is not None:
            row = lax.broadcasted_iota(jnp.int32, s.shape, 0) + pos
            s = jnp.where((row >= masks[0]) & (row < masks[1]), s, NEG)
        probs = jnp.exp(s - lse)
        ds = (probs * (pair[:, n_q:] - delta)).astype(BF)
        acc_ref[place, :] += dot_t(jnp.concatenate([ds, probs.astype(BF)], axis=1), both)
        return dot(src[pl.ds(mult(h, HD), HD), place], ds)

    def pair_up(q_h, g_h):
        zero = jnp.zeros_like(q_h)
        return jnp.concatenate(
            [jnp.concatenate([q_h, zero], axis=1), jnp.concatenate([zero, g_h], axis=1)], axis=0
        )

    def one_head(h, _):
        h_rows = pl.ds(mult(h, HD), HD)
        v_rows = pl.ds(mult(h, HD) + wide, HD)
        near = jnp.where((sc[Y] == 1) & (sc[PAIR + 2 * h + 1] == 1), 1, 0)

        def turn(src, dst):
            dst[...] = jnp.concatenate([src[h_rows, :], src[v_rows, :]], axis=0).T

        acc_p[...] = jnp.zeros_like(acc_p)
        turn(pbuf, p_rows)

        @pl.when(sc[Y] == 1)
        def _():
            acc_c[...] = jnp.zeros_like(acc_c)

        @pl.when(near == 1)
        def _():
            turn(cbuf, c_rows)

        lse = lse_s[pl.ds(mult(h, 8), 8), :][0:1]
        delta = jnp.sum(
            o_s[h_rows, :].astype(F32) * g_s[h_rows, :].astype(F32), axis=0, keepdims=True
        )
        both_s[...] = pair_up(q_ref[h_rows, :], g_s[h_rows, :])
        dq_s[...] = jnp.zeros_like(dq_s)
        lane = lax.broadcasted_iota(jnp.int32, lse.shape, 1)
        first = (lane < early) & (split == 1)

        def prompt(blk, both, lse, delta, n_q):
            start = sc[PAIR + 2 * h + blk] * B
            count = 4 - sc[PAIR + 2 * h + blk]

            def step(at, n):
                at = pl.multiple_of(at, 128)
                place = pl.ds(at, n)
                dq_s[:, :n_q] += chunk(
                    pbuf, p_rows, acc_p, place, at, None, both, lse, delta, h
                )

            def run(i, _):
                step(start + i * 256, 256)
                return 0

            lax.fori_loop(0, count, run, 0)
            step(start + count * 256, 128)

        prompt(later, both_s[...], jnp.where(first, FAR, lse), delta, rows)

        @pl.when(split == 1)
        def _():
            both = pair_up(q_ref[h_rows, :early], g_s[h_rows, :early])
            at, masks = whole_block(sc[PAIR + 2 * h])
            dq_s[:, :early] += chunk(
                pbuf,
                p_rows,
                acc_p,
                pl.ds(at, B),
                at,
                masks,
                both,
                lse[:, :early],
                delta[:, :early],
                h,
            )

        def window(t, _):
            cols = pl.ds(mult(t, tile), tile)
            at = window_start(sc, t, rows, tile)
            n = tile + 2 * LMAX
            masks = (span_ref[0:1, cols], span_ref[1:2, cols])
            g_h = g_s[h_rows, cols]
            d = jnp.sum(o_s[h_rows, cols].astype(F32) * g_h.astype(F32), axis=0, keepdims=True)
            both = pair_up(q_ref[h_rows, cols], g_h)
            l = lse_s[pl.ds(mult(h, 8), 8), cols][0:1]
            dq_s[:, cols] += chunk(
                cbuf, c_rows, acc_c, pl.ds(at, n), at, masks, both, l, d, h
            )
            return 0

        lax.fori_loop(0, 4 * near, window, 0)
        for k in range(4):
            cols = pl.ds(mult(sc[Z] ^ k, tile), tile)
            dq_ref[k, h_rows, :] = (dq_s[:, cols] * HD**-0.5).astype(BF)

        def give(acc, row, out):
            turned = acc[pl.ds(mult(row, rows), rows), :].T.astype(BF)
            out[h_rows, :] = turned[:HD]
            out[pl.ds(mult(h, HD) + wide, HD), :] = turned[HD:]

        @pl.when(sc[Y] == 0)
        def _():
            give(acc_p, sc[C], d_own)
            give(acc_p, 1 - sc[C], d_par)

        @pl.when(sc[Y] == 1)
        def _():
            give(acc_c, sc[C], d_own)
            give(acc_c, 1 - sc[C], d_par)
            give(acc_p, sc[C], d_r0)
            give(acc_p, 1 - sc[C], d_r1)

        return 0

    lax.fori_loop(0, heads, one_head, 0)


def norm(value):
    mean = jnp.mean(value, axis=-1, keepdims=True)
    centred = value - mean
    inv = lax.rsqrt(jnp.mean(centred * centred, axis=-1, keepdims=True) + EPS)
    return centred * inv, inv


def norm_back(e, n, inv):
    return (
        e - jnp.mean(e, axis=-1, keepdims=True) - n * jnp.mean(e * n, axis=-1, keepdims=True)
    ) * inv


def mid_body(sc, *refs):
    mixed = refs[0:4]
    x_hbm, cot_hbm = refs[4:6]
    packs = refs[6:8]
    others = refs[8:24]
    (
        out_ref,
        mb0,
        mb1,
        mb2,
        mb3,
        nl_ref,
        fb_ref,
        ab_ref,
        act_own,
        act_oth,
        ib_own,
        ib_oth,
        mix_own,
        mix_oth,
        gf_ref,
    ) = refs[24:39]
    we, ws, wc, mix_s, act_s, gp_s, ib_s, vec_s, thr_s, mb_s, pk_s, x_ref, cot_ref, small_ref, sems, psems = refs[39:]
    wide, tile = mixed[0].shape
    width = x_ref.shape[1]
    half = width // 2
    hidden = we.shape[1]
    block = hidden // 4
    hb = block // 2
    hw = wide // 2
    c = sc[C]
    hs = gathered_rows(hb)
    ht = hb - hs
    n_pack = half + hs
    n_other = hw // 2 + ht // 2 + 16

    stages = [[], [], []]
    small = []

    def move(stage, src, dst):
        n = len(stages[stage])
        stages[stage].append(pltpu.make_async_copy(src, dst, sems.at[stage, n]))

    for k in range(4):
        z = sc[Z] ^ k
        for j in range(2):
            xc = pl.ds(mult(sc[X] ^ j, half), half)
            for q in range(4):
                cc, yy = c ^ (q // 2), sc[Y] ^ (q % 2)
                piece = others[4 * q + k]
                at = j * n_other
                rows = pl.multiple_of(z * wide + cc * hw + yy * (hw // 2), hw // 2)
                move(0, piece.at[pl.ds(at, hw // 2), :], wc.at[pl.ds(rows, hw // 2), xc])
                rows = z * block + cc * hb + hs + yy * (ht // 2)
                rows = pl.ds(pl.multiple_of(rows, 16), ht // 2)
                move(2, piece.at[pl.ds(at + hw // 2, ht // 2), :], ws.at[rows, xc])
            n = 2 * k + j
            small.append(
                pltpu.make_async_copy(
                    others[k].at[pl.ds(at + hw // 2 + ht // 2, 16), :], pk_s.at[n], psems.at[n]
                )
            )
    for xh in range(2):
        xc = pl.ds(xh * half, half)
        for z in range(4):
            at = (xh * 4 + z) * n_pack
            for i in range(2):
                cc = c ^ i
                place = pl.ds(pl.multiple_of(z * block + cc * hb, hb), hb)
                move(1, packs[i].at[pl.ds(at, half), :], we.at[xc, place])
                place = pl.ds(pl.multiple_of(z * block + cc * hb, 16), hs)
                move(2, packs[i].at[pl.ds(at + half, hs), :], ws.at[place, xc])
    mine = pl.ds(mult(sc[Z], tile), tile)
    small.append(pltpu.make_async_copy(x_hbm.at[mine, :], x_ref, psems.at[8]))
    small.append(pltpu.make_async_copy(cot_hbm.at[mine, :], cot_ref, psems.at[9]))
    for stage in [small] + stages:
        for copy in stage:
            copy.start()

    for copy in small:
        copy.wait()
    for k in range(4):
        mix_s[pl.ds(mult(sc[Z] ^ k, wide), wide), :] = mixed[k][...]
    for k in range(4):
        for j in range(2):
            pack = pk_s[2 * k + j].astype(F32)
            at = pl.multiple_of((sc[Z] ^ k) * block + (sc[X] ^ j) * half, 128)
            thr_s[:, pl.ds(at, half)] = pack[:8]
            if k == 0:
                vec_s[:, pl.ds(mult(sc[X] ^ j, half), half)] = pack[:8]

    baseline = vec_s[0:1, :]
    scaling = vec_s[1:2, :]
    shifting = vec_s[2:3, :]
    settling = vec_s[3:4, :]
    rescaling = vec_s[4:5, :]
    reshifting = vec_s[5:6, :]

    for copy in stages[0]:
        copy.wait()
    first = x_ref[...].astype(F32) + tdot(mix_s[...], wc[...]) + baseline
    n1, inv1 = norm(first)
    normed = n1 * scaling + shifting
    low = normed.astype(BF)
    nl_ref[...] = low
    for copy in stages[1]:
        copy.wait()
    for copy in stages[2]:
        copy.wait()
    feed = jnp.zeros((tile, width), F32)
    for n in range(4):
        cols = slice(n * block, (n + 1) * block)
        inner = dot(low, we[:, cols]) + thr_s[6:7, cols]
        cdf = 0.5 * (1.0 + lax.erf(inner * (0.5**0.5)))
        pdf = jnp.exp(-0.5 * inner * inner) * (1.0 / math.sqrt(2.0 * math.pi))
        active = (inner * cdf).astype(BF)
        act_s[:, cols] = active
        gp_s[:, cols] = cdf + inner * pdf
        feed = feed + dot(active, ws[cols, :])
    second = normed + feed + settling
    n2, inv2 = norm(second)
    out_ref[:tile, :] = (n2 * rescaling + reshifting).astype(BF)
    dy = cot_ref[...].astype(F32)
    small_ref[...] = jnp.zeros_like(small_ref)
    small_ref[4:5, :] = jnp.sum(dy * n2, axis=0, keepdims=True)
    small_ref[5:6, :] = jnp.sum(dy, axis=0, keepdims=True)
    grad = norm_back(rescaling * dy, n2, inv2)
    small_ref[3:4, :] = jnp.sum(grad, axis=0, keepdims=True)
    feed_back = grad.astype(BF)
    fb_ref[...] = feed_back
    for n in range(4):
        cols = slice(n * block, (n + 1) * block)
        inner_back = (dot_t(feed_back, ws[cols, :]) * gp_s[:, cols]).astype(BF)
        ib_s[:, cols] = inner_back
        small_ref[8 + n : 9 + n, :] = jnp.sum(inner_back.astype(F32), axis=0, keepdims=True)
        grad = grad + dot_t(inner_back, we[:, cols])
    small_ref[1:2, :] = jnp.sum(grad * n1, axis=0, keepdims=True)
    small_ref[2:3, :] = jnp.sum(grad, axis=0, keepdims=True)
    grad_first = norm_back(scaling * grad, n1, inv1)
    small_ref[0:1, :] = jnp.sum(grad_first, axis=0, keepdims=True)
    out_ref[tile:, :] = small_ref[...].astype(BF)
    gf_ref[...] = grad_first
    attended_back = grad_first.astype(BF)
    ab_ref[...] = attended_back
    mb_s[...] = dot_t(wc[...], attended_back).astype(BF)
    for k, mb in enumerate((mb0, mb1, mb2, mb3)):
        mb[...] = mb_s[pl.ds(mult(sc[Z] ^ k, wide), wide), :]
    for n in range(4):
        mine = pl.ds(pl.multiple_of(n * block + c * hb, 128), hb)
        other = pl.ds(pl.multiple_of(n * block + (1 - c) * hb, 128), hb)
        cols = slice(n * hb, (n + 1) * hb)
        act_own[:, cols] = act_s[:, mine]
        act_oth[:, cols] = act_s[:, other]
        ib_own[:, cols] = ib_s[:, mine]
        ib_oth[:, cols] = ib_s[:, other]
        mine = pl.ds(pl.multiple_of(n * wide + c * hw, hw), hw)
        other = pl.ds(pl.multiple_of(n * wide + (1 - c) * hw, hw), hw)
        mix_own[n * hw : (n + 1) * hw, :] = mix_s[mine, :]
        mix_oth[n * hw : (n + 1) * hw, :] = mix_s[other, :]


def wg_body(sc, *refs):
    nl, fb, ab, act, ib, mix = [(refs[i], refs[6 + i]) for i in range(6)]
    g_ref = refs[12]
    half = nl[0].shape[1] // 2
    hb = act[0].shape[1] // 4
    hw = mix[0].shape[0] // 4
    for x in range(2):
        xc = slice(x * half, (x + 1) * half)
        for k in range(4):
            z = sc[Z] ^ k
            zc = pl.ds(mult(z, hb), hb)
            e = sum(tdot(nl[i][:, xc], ib[i][:, zc]) for i in range(2)).astype(BF)
            s = sum(tdot(act[i][:, zc], fb[i][:, xc]) for i in range(2)).astype(BF)
            zr = pl.ds(mult(z, hw), hw)
            m = sum(dot(mix[i][zr, :], ab[i][:, xc]) for i in range(2)).astype(BF)
            at = 0
            for v in (e, s, m):
                n = v.shape[0] // 2
                for yh in range(2):
                    g_ref[yh, x, k, at : at + n, :] = v[yh * n : (yh + 1) * n]
                at += n


def wfin_body(sc, *refs):
    quarters = refs[0:4]
    e_ref, s_ref, m_ref = refs[4:7]
    he = e_ref.shape[0] // 2
    hb = e_ref.shape[1] // 2
    hs = hb // 2
    hm = m_ref.shape[0] // 4
    for i in range(2):
        c = sc[C] ^ i
        for j in range(2):
            part = quarters[2 * i + j]
            y = sc[Y] ^ j
            rows = pl.ds(mult(y, he), he)
            e_ref[rows, pl.ds(mult(c, hb), hb)] = part[:he, :].astype(F32)
            at = pl.multiple_of(c * hb + y * hs, hs)
            s_ref[pl.ds(at, hs), :] = part[he : he + hs, :].astype(F32)
            at = pl.multiple_of((c * 2 + y) * hm, hm)
            m_ref[pl.ds(at, hm), :] = part[he + hs :, :].astype(F32)


def ib_body(sc, a_ref, b_ref, c_ref, dq_ref, wt_ref, kv_ref, *outs):
    wide = dq_ref.shape[1]
    tile = dq_ref.shape[2]
    for k in (3, 2, 1, 0):
        cols = pl.ds(mult(sc[Z] ^ k, tile), tile)
        total = a_ref[:, cols].astype(F32) + b_ref[:, cols].astype(F32)
        kv = (total + c_ref[:, cols].astype(F32)).astype(BF)
        kv_ref[k] = kv
        part = tdot(dq_ref[k], wt_ref[:wide, :]) + tdot(kv, wt_ref[wide:, :])
        outs[k][...] = part.astype(BF)


def pair_body(a_ref, b_ref, out_ref):
    out_ref[...] = (a_ref[...].astype(F32) + b_ref[...].astype(F32)).astype(BF)


def fin_body(a_ref, b_ref, c_ref, gf_ref, out_ref):
    total = a_ref[...].astype(F32) + b_ref[...].astype(F32)
    out_ref[...] = (total + c_ref[...].astype(F32) + gf_ref[...]).astype(BF)


def gp_body(sc, dq_ref, kv_ref, x_ref, all_ref, out_ref, acc, line, parts, small_ref, sems):
    wide = dq_ref.shape[1]
    tile = dq_ref.shape[2]
    half = out_ref.shape[3]
    copies = [
        pltpu.make_async_copy(all_ref.at[k, pl.ds(tile, 16), :], small_ref.at[k], sems.at[k])
        for k in range(4)
    ]
    for copy in copies:
        copy.start()
    ones = jnp.ones((8, tile), BF)
    top = bot = s_top = s_bot = 0.0
    for k in range(4):
        rows = x_ref[pl.ds(mult(sc[Z] ^ k, tile), tile), :]
        top = top + dot(dq_ref[k], rows)
        bot = bot + dot(kv_ref[k], rows)
        s_top = s_top + dot_t(ones, dq_ref[k])
        s_bot = s_bot + dot_t(ones, kv_ref[k, wide:, :])
    acc[:wide, :] = top
    acc[wide:, :] = bot
    for k in range(4):
        copies[k].wait()
        parts[k] = small_ref[k].astype(F32)
    parts[0] = ((parts[0] + parts[1]) + parts[2]) + parts[3]
    line[...] = jnp.zeros_like(line)
    line[0, 0:1, :wide] = s_top[0:1]
    line[0, 0:1, wide:] = s_bot[0:1]
    line[1, 0:1, :wide] = s_top[0:1]
    line[1, 0:1, wide:] = s_bot[0:1]
    for h in range(2):
        hc = slice(h * half, (h + 1) * half)
        line[h, 1:7, :] = parts[0, 0:6, hc]
        line[h, 7:8, :] = parts[0, pl.ds(8 + sc[Z], 1), hc]
    n_rows = out_ref.shape[2] - 16
    for i in range(2):
        at = pl.multiple_of((sc[C] ^ i) * n_rows, n_rows)
        for m in range(2):
            cols = pl.ds(mult(sc[X] ^ m, half), half)
            out_ref[i, m, :n_rows, :] = acc[pl.ds(at, n_rows), cols].astype(BF)
            out_ref[i, m, n_rows:, :] = line[sc[X] ^ m].astype(BF)


def join_body(dtype, sc, *refs):
    out = refs[4]
    tile = out.shape[0] // 4
    for k in range(4):
        out[pl.ds(mult(sc[Z] ^ k, tile), tile), :] = refs[k][:tile, :].astype(dtype)


def gpfin_body(sc, a_ref, b_ref, out, line, *vecs):
    n_rows = a_ref.shape[0] - 16
    rows = a_ref[n_rows : n_rows + 8, :].astype(F32)
    line[...] = rows
    for i, vec in enumerate(vecs):
        vec[...] = rows[1 + i]
    for i, ref in enumerate((a_ref, b_ref)):
        at = pl.multiple_of((sc[C] ^ i) * n_rows, n_rows)
        out[pl.ds(at, n_rows), :] = ref[:n_rows, :].astype(F32)


def make_device(n_dp, n_ctx, n_t, generic):
    def swap(axis, size, k):
        return lambda v: lax.ppermute(v, axis, [(i, i ^ k) for i in range(size)])

    pc = swap("core", 2, 1)
    py = swap("cy", n_ctx // 2, 1)
    px = swap("dp", n_dp, 1)
    pz = [lambda v: v] + [swap("tensor", n_t, k) for k in range(1, n_t)]

    def on_device(
        tokens,
        cotangent,
        segments,
        pairing,
        project,
        offsets,
        combine,
        baseline,
        scaling,
        shifting,
        expand,
        thresholds,
        shrink,
        settling,
        rescaling,
        reshifting,
    ):
        _, rows, width = tokens.shape
        heads = pairing.shape[0] // n_t
        wide = heads * HD
        tile = rows // n_t
        half = width // 2
        block = expand.shape[1]
        hidden = block * n_t
        hb = block // 2
        hw = wide // 2
        x = tokens[0]
        cot = cotangent[0]
        c = lax.axis_index("core")
        y = lax.axis_index("cy")
        ctx = 2 * y + c
        z = lax.axis_index("tensor")
        dp = lax.axis_index("dp")
        xi = jnp.zeros_like(dp) if generic else dp
        pairs = lax.dynamic_slice_in_dim(pairing, z * heads, heads, 0).reshape(-1)
        sc = jnp.concatenate(
            [jnp.stack([ctx, z, xi, c, y, c, c, c]).astype(jnp.int32), pairs.astype(jnp.int32)]
        )

        def both_halves(v, axis):
            full = lax.all_gather(v, "dp", axis=axis, tiled=True)
            return jnp.split(full, 2, axis=axis)

        wt = jnp.transpose(project, (1, 2, 0)).reshape(3 * wide, -1)
        vectors = [baseline, scaling, shifting, settling, rescaling, reshifting]

        hq = wide // 2
        part = 3 * wide // 2
        def pack(wt_h, e_h, s_h, m_h, off_h, vecs_h):
            return call(
                pack_body,
                (
                    sds((16, half), F32),
                    sds((part + 16, half), BF),
                    sds((half + gathered_rows(hb), half), BF),
                    sds((hw // 2 + (hb - gathered_rows(hb)) // 2 + 16, half), BF),
                ),
                ins=[SM] + [VM] * 12,
                cost=cost(0, 8 * half * width),
            )(sc, wt_h, e_h, s_h, m_h, off_h, *vecs_h)

        vectors = vectors + [thresholds]
        if generic:
            own_wt, other_wt = both_halves(wt, 1)
            parts = [both_halves(v, 0) for v in [expand] + vectors]
            cols = [both_halves(v, 1) for v in (shrink, combine, offsets)]
            packed = [
                pack(
                    w, parts[0][j], cols[0][j], cols[1][j], cols[2][j], [p[j] for p in parts[1:]]
                )
                for j, w in enumerate((own_wt, other_wt))
            ]
            small, wtc = packed[0][0], packed[0][1]
            got_wt = packed[1][1]
            weights = jnp.stack(
                [lax.all_gather(p[2], "tensor", axis=0) for p in packed]
            ).reshape(-1, half)
            other_wide = jnp.concatenate([p[3] for p in packed])
        else:
            own_wt = wt
            small, wtc, wpack, o_c = pack(wt, expand, shrink, combine, offsets, vectors)
            got_wt = px(wtc)
            weights = lax.all_gather(wpack, ("dp", "tensor"), axis=0, tiled=True)
            other_wide = jnp.concatenate([o_c, px(o_c)])

        def after(v, *deps):
            return lax.optimization_barrier((v, *deps))[0]

        got_wt2 = after(pc(got_wt), other_wide)

        qT, kvT, wt_full = call(
            qkv_body,
            (
                sds((wide, rows), BF),
                sds((2 * wide, rows), BF),
                sds((3 * wide, width), BF),
            ),
            ins=[SM] + [VM] * 5,
            scratch=[pltpu.VMEM((3 * wide, half), BF), pltpu.VMEM((16, 3 * wide), BF)],
            cost=cost(2 * rows * width * 3 * wide, 4 * rows * width),
        )(sc, x, own_wt, small, got_wt, got_wt2)

        seg = segments[0]
        mine = lax.dynamic_slice_in_dim(seg, c * rows, rows, 0)
        low = jnp.sum((seg[:, None] < mine[None, :]).astype(jnp.int32), axis=0)
        high = jnp.sum((seg[:, None] <= mine[None, :]).astype(jnp.int32), axis=0)
        span = jnp.concatenate(
            [low[None], high[None], jnp.zeros((6, rows), jnp.int32)], axis=0
        )

        z_near = pz[1](other_wide)
        z_far = pz[2](other_wide)
        other_z = [other_wide, z_near, z_far, pz[1](z_far)]

        par = pc(kvT)
        ra = lax.ppermute(kvT, "cy", [(0, 1)])

        kv_scratch = [pltpu.VMEM((2 * wide, 2 * rows), BF), pltpu.VMEM((2 * wide, 2 * rows), BF)]
        state = [
            sds((wide, rows), F32),
            sds((8 * heads, rows), F32),
            sds((8 * heads, rows), F32),
        ]
        sofar = call(
            fwd_near_body,
            tuple(state),
            ins=[SM, VM, VM] + [ANY] * 2,
            scratch=[kv_scratch[0], pltpu.SemaphoreType.DMA((2,))],
            cost=cost(0, 1000),
        )(sc, qT, span, kvT, par)
        ra = after(ra, sofar[0])
        rb = pc(after(ra, z_near, z_far))
        other_y = [py(after(w, ra)) for w in other_z[:3]]
        *o_tiles, lse = call(
            fwd_far_body,
            (*[sds((wide, tile), BF)] * 4, sds((8 * heads, rows), F32)),
            ins=[SM, VM] + [ANY] * 2 + [VM] * 3,
            scratch=[kv_scratch[0]]
            + [pltpu.VMEM(v.shape, v.dtype) for v in state]
            + [pltpu.SemaphoreType.DMA((2,))],
            cost=cost(0, 1000),
        )(sc, qT, ra, rb, *sofar)
        relayed = after(other_z[3], o_tiles[0])
        o_tiles = [after(o, *other_y, relayed) for o in o_tiles]
        other_y = other_y + [py(relayed)]
        mixed = [pz[k](o_tiles[k]) for k in range(4)]
        weights2 = pc(after(weights, *mixed, other_y[3]))
        others = other_z + other_y
        others = others + [pc(after(w, o_tiles[0])) for w in others]

        outs = call(
            mid_body,
            (
                sds((tile + 16, width), BF),
                *[sds((wide, tile), BF)] * 4,
                *[sds((tile, width), BF)] * 3,
                *[sds((tile, hidden // 2), BF)] * 4,
                *[sds((width // 2, tile), BF)] * 2,
                sds((tile, width), F32),
            ),
            ins=[SM] + [VM] * 4 + [ANY] * 20,
            scratch=[
                pltpu.VMEM((width, hidden), BF),
                pltpu.VMEM((hidden, width), BF),
                pltpu.VMEM((width, width), BF),
                pltpu.VMEM((width, tile), BF),
                pltpu.VMEM((tile, hidden), BF),
                pltpu.VMEM((tile, hidden), F32),
                pltpu.VMEM((tile, hidden), BF),
                pltpu.VMEM((8, width), F32),
                pltpu.VMEM((8, hidden), F32),
                pltpu.VMEM((width, tile), BF),
                pltpu.VMEM((8, 16, half), BF),
                pltpu.VMEM((tile, width), BF),
                pltpu.VMEM((tile, width), BF),
                pltpu.VMEM((16, width), F32),
                pltpu.SemaphoreType.DMA((3, 48)),
                pltpu.SemaphoreType.DMA((10,)),
            ],
            cost=cost(8 * tile * width * hidden + 4 * tile * width * width, 4 * width * hidden),
        )(sc, *mixed, x, cot, weights, weights2, *others)
        out_low = outs[0]
        mb = outs[1:5]
        nl, fb, ab, act_own, act_oth, ib_own, ib_oth, mix_own, mix_oth, grad_first = outs[5:]
        grads = [mb[0]] + [pz[k](mb[k]) for k in range(1, 4)]

        theirs = [pc(v) for v in (nl, fb, ab, act_oth, ib_oth, mix_oth)]
        gathered = lax.all_gather(out_low, "tensor", axis=0)

        outs = call(
            bwd_body,
            (sds((4, wide, tile), BF), *[sds((2 * wide, rows), BF)] * 4),
            ins=[SM, VM, VM] + [ANY] * 4 + [VM] * 9,
            scratch=kv_scratch
            + [
                pltpu.VMEM((wide, rows), BF),
                pltpu.VMEM((wide, rows), BF),
                pltpu.VMEM((2 * rows, 2 * HD), F32),
                pltpu.VMEM((2 * rows, 2 * HD), F32),
                pltpu.VMEM((2 * rows, 2 * HD), BF),
                pltpu.VMEM((2 * rows, 2 * HD), BF),
                pltpu.VMEM((2 * HD, 2 * rows), BF),
                pltpu.VMEM((HD, rows), F32),
                pltpu.SemaphoreType.DMA((4,)),
            ],
            cost=cost(10 * B * rows * wide, 4 * 4 * wide * rows, B * rows * heads),
        )(sc, qT, span, kvT, par, ra, rb, *o_tiles, lse, *grads)
        dq, d_own, d_par, d_r0, d_r1 = outs
        got_par = pc(d_par)
        got_r = pc(d_r1)
        prompt_part = (d_r0.astype(F32) + got_r.astype(F32)).astype(BF)
        nl = after(nl, prompt_part, got_par)
        n_part = half // 2 + hb // 2 + hw // 2
        g = call(
            wg_body,
            sds((2, 2, 4, n_part, half), BF),
            ins=[SM] + [VM] * 12,
            cost=cost(4 * tile * width * hidden, 4 * width * hidden),
        )(sc, nl, fb, ab, act_own, ib_own, mix_own, *theirs)
        from_y = lax.ppermute(prompt_part, "cy", [(1, 0)])
        outs = call(
            ib_body,
            (sds((4, 2 * wide, tile), BF), *[sds((tile, width), BF)] * 4),
            ins=[SM] + [VM] * 5,
            cost=cost(2 * rows * width * 3 * wide, 8 * rows * width),
        )(sc, after(d_own, gathered), got_par, from_y, dq, wt_full)
        kv_back, back = outs[0], outs[1:]
        layer_out = after(gathered, kv_back)[:, :tile].reshape(rows, width)
        passed = pz[1](back[3])
        relay = call(pair_body, sds((tile, width), BF), ins=[VM] * 2)(back[2], passed)
        near = pz[1](after(back[1], passed))
        far = pz[2](relay)
        gp = call(
            gp_body,
            sds((2, 2, 3 * wide // 2 + 16, half), BF),
            ins=[SM] + [VM] * 3 + [ANY],
            scratch=[
                pltpu.VMEM((3 * wide, width), F32),
                pltpu.VMEM((2, 16, half), F32),
                pltpu.VMEM((4, 16, width), F32),
                pltpu.VMEM((4, 16, width), BF),
                pltpu.SemaphoreType.DMA((4,)),
            ],
            cost=cost(2 * rows * width * 3 * wide, 4 * rows * width),
        )(sc, dq, kv_back, x, gathered)

        def add(a, b):
            return (a.astype(F32) + b.astype(F32)).astype(BF)

        gp_c = add(gp[0], pc(gp[1]))
        low_tokens = call(
            fin_body,
            sds((tile, width), BF),
            ins=[VM] * 4,
            cost=cost(4 * tile * width, 12 * tile * width),
        )(back[0], near, far, after(grad_first, gp_c, layer_out))
        gp_c = after(gp_c, low_tokens)
        tiles_near = pz[1](low_tokens)
        tiles_far = pz[2](low_tokens)
        token_tiles = [low_tokens, tiles_near, tiles_far, pz[1](tiles_far)]
        grad_tokens = call(
            functools.partial(join_body, F32),
            sds((rows, width), F32),
            ins=[SM] + [VM] * 4,
            cost=cost(rows * width, 6 * rows * width),
        )(sc, *token_tiles)
        def sum_z(parts, wait=()):
            relay = after(add(parts[2], pz[1](parts[3])), *wait)
            near = pz[1](parts[1])
            far = pz[2](relay)
            total = parts[0].astype(F32) + near.astype(F32) + far.astype(F32)
            return total.astype(BF)

        def finish_ff(mine, *wait):
            quarters = [mine, after(py(mine), *wait)]
            quarters = quarters + [pc(q) for q in quarters]
            return call(
                wfin_body,
                (sds((half, block), F32), sds((block, half), F32), sds((wide, half), F32)),
                ins=[SM] + [VM] * 4,
            )(sc, *quarters)

        def finish_gp(mine):
            return call(
                gpfin_body,
                (
                    sds((3 * wide, half), F32),
                    sds((8, half), F32),
                    *[sds((half,), F32)] * 7,
                ),
                ins=[SM] + [VM] * 2,
            )(sc, mine, pc(mine))

        gp = add(gp_c, py(gp_c))
        if generic:
            g = lax.psum_scatter(g, "cy", scatter_dimension=0, tiled=False)
            parts = [
                finish_ff(sum_z(v))
                for v in (g[0], g[1])
            ]

            def scatter(two, axis):
                full = jnp.concatenate(two, axis=axis).astype(BF)
                return lax.psum_scatter(
                    full, "dp", scatter_dimension=axis, tiled=True
                ).astype(F32)

            summed = [scatter([p[i] for p in parts], i and 1) for i in range(3)]
            both = [finish_gp(gp[j]) for j in range(2)]
            grad_project = scatter([b[0] for b in both], 1)
            grad_offsets = scatter([both[0][1][0].reshape(2, wide)], 1)
            vecs = [scatter([b[2 + i] for b in both], 0) for i in range(7)]
        else:
            g = after(g, from_y)
            g = lax.psum_scatter(
                g.reshape(-1, half), ("cy", "dp"), scatter_dimension=0, tiled=True
            )
            g = after(g, tiles_near, tiles_far)
            g = sum_z(g.reshape(4, n_part, half))
            grad_project, lines, *vecs = finish_gp(add(gp[0], px(gp[1])))
            summed = finish_ff(g, grad_tokens, layer_out, grad_project)
            n_off = offsets.shape[1]
            grad_offsets = lax.dynamic_slice_in_dim(
                lines[0].reshape(2, wide), dp * n_off, n_off, 1
            )
        grad_expand, grad_shrink, grad_combine = summed
        grad_project = jnp.transpose(grad_project.reshape(3, wide, -1), (2, 0, 1))

        return (
            layer_out[None],
            grad_tokens[None],
            grad_project,
            grad_offsets,
            grad_combine,
            vecs[0],
            vecs[1],
            vecs[2],
            grad_expand,
            vecs[6],
            grad_shrink,
            vecs[3],
            vecs[4],
            vecs[5],
        )

    return on_device


def solution(mesh):
    in_specs = (
        P("dp", ("cy", "core"), None),
        P("dp", ("cy", "core"), None),
        P("dp", None),
        P(),
        P("dp", None, "tensor"),
        P(None, ("tensor", "dp")),
        P("tensor", "dp"),
        P("dp"),
        P("dp"),
        P("dp"),
        P("dp", "tensor"),
        P(("tensor", "dp")),
        P("tensor", "dp"),
        P("dp"),
        P("dp"),
        P("dp"),
    )
    out_specs = (
        P("dp", ("cy", "core"), None),
        P("dp", ("cy", "core"), None),
        P("dp", None, "tensor"),
        P(None, ("tensor", "dp")),
        P("tensor", "dp"),
        P("dp"),
        P("dp"),
        P("dp"),
        P("dp", "tensor"),
        P(("tensor", "dp")),
        P("tensor", "dp"),
        P("dp"),
        P("dp"),
        P("dp"),
    )
    n_dp, n_ctx, n_t = mesh.shape["dp"], mesh.shape["ctx"], mesh.shape["tensor"]
    split = Mesh(mesh.devices.reshape(n_dp, n_ctx // 2, 2, n_t), ("dp", "cy", "core", "tensor"))
    on_device = make_device(n_dp, n_ctx, n_t, n_dp != 2)
    return jax.shard_map(
        on_device, mesh=split, in_specs=in_specs, out_specs=out_specs, check_vma=False
    )
```

```python
import functools
import math

import jax
import jax.numpy as jnp
from jax import lax
from jax.experimental import pallas as pl
from jax.experimental.pallas import tpu as pltpu
from jax.sharding import Mesh
from jax.sharding import PartitionSpec as P

P_SIZE = 2048
LMAX = 256
B = 1152
HD = 64
EPS = 1e-06
NEG = -1e30

BF = jnp.bfloat16
F32 = jnp.float32

VM = pl.BlockSpec(memory_space=pltpu.VMEM)
ANY = pl.BlockSpec(memory_space=pl.ANY)
SM = pl.BlockSpec(memory_space=pltpu.SMEM)
LIMIT = 60 << 20


def call(body, outs, scratch=(), ins=None, cost=None):
    out_specs = tuple([VM] * len(outs)) if isinstance(outs, tuple) else VM
    return pl.pallas_call(
        body,
        out_shape=outs,
        in_specs=ins,
        out_specs=out_specs,
        scratch_shapes=scratch,
        cost_estimate=cost,
        compiler_params=pltpu.CompilerParams(vmem_limit_bytes=LIMIT),
    )


def gathered_rows(n):
    return n // 3


def sds(shape, dtype):
    return jax.ShapeDtypeStruct(shape, dtype)


def cost(flops, nbytes, trans=0):
    return pl.CostEstimate(flops=int(flops), bytes_accessed=int(nbytes), transcendentals=int(trans))


def dot(a, b):
    return lax.dot_general(a, b, (((1,), (0,)), ((), ())), preferred_element_type=F32)


def dot_t(a, b):
    return lax.dot_general(a, b, (((1,), (1,)), ((), ())), preferred_element_type=F32)


def tdot(a, b):
    return lax.dot_general(a, b, (((0,), (0,)), ((), ())), preferred_element_type=F32)


def mult(value, by):
    return pl.multiple_of(value * by, by)


CTX, Z, X, C, Y, PAIR = 0, 1, 2, 3, 4, 8


def qkv_body(sc, x_ref, own_ref, small_ref, w0_ref, w1_ref, q_ref, kv_ref, wt_ref, oth, row):
    half = own_ref.shape[1]
    wide = q_ref.shape[0]
    part = own_ref.shape[0] // 2
    hq = wide // 2
    oth[pl.ds(mult(sc[C], part), part), :] = w0_ref[:part, :]
    oth[pl.ds(mult(1 - sc[C], part), part), :] = w1_ref[:part, :]
    mine, theirs = small_ref[...].astype(BF), w0_ref[part:, :]
    even = jnp.where(sc[X] == 0, mine, theirs)
    odd = jnp.where(sc[X] == 0, theirs, mine)
    row[...] = jnp.zeros_like(row)
    for at, rank in ((0, 7), (2 * wide, 8)):
        row[0:1, at : at + hq] = even[rank : rank + 1, :hq]
        row[0:1, at + hq : at + wide] = odd[rank : rank + 1, :hq]
    a0 = x_ref[:, pl.ds(mult(sc[X], half), half)]
    a1 = x_ref[:, pl.ds(mult(1 - sc[X], half), half)]
    first = lax.broadcasted_iota(jnp.int32, (row.shape[0], x_ref.shape[0]), 0) == 0
    bias = tdot(row[...], jnp.where(first, 1.0, 0.0).astype(BF))
    low = (dot_t(own_ref[...], a0) + dot_t(oth[...], a1) + bias).astype(BF)
    q_ref[...] = low[:wide] * jnp.asarray(HD**-0.5, BF)
    kv_ref[...] = low[wide:]
    wt_ref[:, pl.ds(mult(sc[X], half), half)] = own_ref[...]
    wt_ref[:, pl.ds(mult(1 - sc[X], half), half)] = oth[...]


def pack_body(sc, *refs):
    wt, e_ref, s_ref, m_ref, off = refs[0:5]
    vecs = refs[5:12]
    small, wtc, wc, tq = refs[12:16]
    part = wt.shape[0] // 2
    hb = e_ref.shape[1] // 2
    hw = m_ref.shape[0] // 2
    half = s_ref.shape[1]
    c = sc[C]
    small[...] = jnp.zeros_like(small)
    for i, vec in enumerate(vecs):
        small[i : i + 1, :] = vec[...].astype(F32).reshape(1, half)
    small[7:9, : off.shape[1]] = off[...].astype(F32)
    low = small[...].astype(BF)
    wtc[:part, :] = wt[pl.ds(mult(c, part), part), :]
    wtc[part:, :] = low
    hs = wc.shape[0] - half
    ht = hb - hs
    y = sc[Y]
    wc[:half, :] = e_ref[:, pl.ds(mult(c, hb), hb)]
    wc[half:, :] = s_ref[pl.ds(mult(c, hb), hs), :]
    at = 0
    for ref, start, n in (
        (m_ref, (c * 2 + y) * (hw // 2), hw // 2),
        (s_ref, c * hb + hs + y * (ht // 2), ht // 2),
    ):
        tq[at : at + n, :] = ref[pl.ds(pl.multiple_of(start, 16), n), :]
        at += n
    tq[at:, :] = low


def load_pairs(sc, own, par, ra, rb, pbuf, cbuf, sems):
    rows = own.shape[1]
    here = pl.ds(mult(sc[C], rows), rows)
    there = pl.ds(mult(1 - sc[C], rows), rows)

    def run(moves):
        copies = [
            pltpu.make_async_copy(src, dst, sems.at[i]) for i, (src, dst) in enumerate(moves)
        ]
        for copy in copies:
            copy.start()
        for copy in copies:
            copy.wait()

    @pl.when(sc[Y] == 0)
    def _():
        run([(own, pbuf.at[:, here]), (par, pbuf.at[:, there])])

    @pl.when(sc[Y] == 1)
    def _():
        run(
            [
                (ra, pbuf.at[:, here]),
                (rb, pbuf.at[:, there]),
                (own, cbuf.at[:, here]),
                (par, cbuf.at[:, there]),
            ]
        )


def window_start(sc, t, rows, tile):
    local = sc[C] * rows + t * tile
    return pl.multiple_of(jnp.clip(local - LMAX, 0, 2 * rows - tile - 2 * LMAX), 128)


FAR = 1e30


def attend(src, state, q_h, h, at, n, ok, masks, cols):
    acc, peaks, totals = state
    wide = acc.shape[0]
    h_rows = pl.ds(mult(h, HD), HD)
    v_rows = pl.ds(mult(h, HD) + wide, HD)
    h8 = pl.ds(mult(h, 8), 8)
    place = pl.ds(at, n)
    s = tdot(src[h_rows, place], q_h)
    if masks is not None:
        pos = lax.broadcasted_iota(jnp.int32, s.shape, 0) + at
        s = jnp.where((pos >= masks[0]) & (pos < masks[1]), s, NEG)
    peak = peaks[h8, cols]
    new = jnp.maximum(peak, jnp.max(s, axis=0, keepdims=True))
    cap = new
    if ok is not None:
        new = jnp.where(ok, new, peak)
        cap = jnp.where(ok, new, FAR)
    e = jnp.exp(s - cap[0:1])
    alpha = jnp.exp(peak - new)
    peaks[h8, cols] = new
    totals[h8, cols] = totals[h8, cols] * alpha + jnp.sum(e, axis=0, keepdims=True)
    acc[h_rows, cols] = acc[h_rows, cols] * alpha[0:1] + dot(src[v_rows, place], e.astype(BF))


def whole_block(paired):
    at = pl.multiple_of(paired * (P_SIZE - B), 128)
    return at, (paired * B, B + paired * (P_SIZE - B))


def attend_prompt(sc, src, state, q_h, h, blk, ok, cols):
    paired = sc[PAIR + 2 * h + blk]
    start = paired * B
    count = 4 - paired

    def run(i, _):
        at = pl.multiple_of(start + i * 256, 128)
        attend(src, state, q_h, h, at, 256, ok, None, cols)
        return 0

    lax.fori_loop(0, count, run, 0)
    at = pl.multiple_of(start + count * 256, 128)
    attend(src, state, q_h, h, at, 128, ok, None, cols)


def load_two(sc, first, second, buf, sems):
    rows = first.shape[1]
    copies = [
        pltpu.make_async_copy(first, buf.at[:, pl.ds(mult(sc[C], rows), rows)], sems.at[0]),
        pltpu.make_async_copy(second, buf.at[:, pl.ds(mult(1 - sc[C], rows), rows)], sems.at[1]),
    ]
    for copy in copies:
        copy.start()
    for copy in copies:
        copy.wait()


def fwd_near_body(sc, q_ref, span_ref, own, par, acc, peaks, totals, buf, sems):
    load_two(sc, own, par, buf, sems)
    rows = own.shape[1]
    tile = rows // 4
    state = (acc, peaks, totals)
    peaks[...] = jnp.full_like(peaks, NEG)
    totals[...] = jnp.zeros_like(totals)
    acc[...] = jnp.zeros_like(acc)
    whole = slice(0, rows)
    lane = lax.broadcasted_iota(jnp.int32, (8, rows), 1)
    late = jnp.logical_not((lane < B - rows) & (sc[CTX] == 1))

    def one_head(h, _):
        h_rows = pl.ds(mult(h, HD), HD)

        @pl.when(sc[Y] == 0)
        def _():
            attend_prompt(sc, buf, state, q_ref[h_rows, :], h, sc[CTX], late, whole)

        @pl.when(sc[CTX] == 1)
        def _():
            early = B - rows
            at, masks = whole_block(sc[PAIR + 2 * h])
            attend(buf, state, q_ref[h_rows, :early], h, at, B, None, masks, slice(0, early))

        def window(t, _):
            cols = pl.ds(mult(t, tile), tile)
            at = window_start(sc, t, rows, tile)
            masks = (span_ref[0:1, cols], span_ref[1:2, cols])
            n = tile + 2 * LMAX
            attend(buf, state, q_ref[h_rows, cols], h, at, n, None, masks, cols)
            return 0

        near = jnp.where((sc[Y] == 1) & (sc[PAIR + 2 * h + 1] == 1), 4, 0)
        lax.fori_loop(0, near, window, 0)
        return 0

    lax.fori_loop(0, acc.shape[0] // HD, one_head, 0)


def fwd_far_body(sc, q_ref, ra, rb, acc_in, peaks_in, totals_in, *refs):
    outs = refs[0:4]
    lse_ref = refs[4]
    buf, acc, peaks, totals, sems = refs[5:]
    rows = ra.shape[1]
    tile = outs[0].shape[1]
    acc[...] = acc_in[...]
    peaks[...] = peaks_in[...]
    totals[...] = totals_in[...]

    @pl.when(sc[Y] == 1)
    def _():
        load_two(sc, ra, rb, buf, sems)
        state = (acc, peaks, totals)

        def one_head(h, _):
            q_h = q_ref[pl.ds(mult(h, HD), HD), :]
            attend_prompt(sc, buf, state, q_h, h, 1, None, slice(0, rows))
            return 0

        lax.fori_loop(0, acc.shape[0] // HD, one_head, 0)

    lse_ref[...] = peaks[...] + jnp.log(totals[...])
    for h in range(acc.shape[0] // HD):
        h_rows = slice(h * HD, (h + 1) * HD)
        acc[h_rows, :] = acc[h_rows, :] / totals[8 * h : 8 * h + 1, :]
    for k in range(4):
        outs[k][...] = acc[:, pl.ds(mult(sc[Z] ^ k, tile), tile)].astype(BF)


def bwd_body(
    sc,
    q_ref,
    span_ref,
    own,
    par,
    ra,
    rb,
    *refs,
):
    o_in = refs[0:4]
    lse_s = refs[4]
    g_in = refs[5:9]
    dq_ref, d_own, d_par, d_r0, d_r1 = refs[9:14]
    pbuf, cbuf, o_s, g_s, acc_p, acc_c, p_rows, c_rows, both_s, dq_s, sems = refs[14:]
    load_pairs(sc, own, par, ra, rb, pbuf, cbuf, sems)
    rows = own.shape[1]
    wide, tile = o_in[0].shape
    heads = wide // HD
    for k in range(4):
        cols = pl.ds(mult(sc[Z] ^ k, tile), tile)
        o_s[:, cols] = o_in[k][...]
        g_s[:, cols] = g_in[k][...]
    later = jnp.where(sc[CTX] > 0, 1, 0)
    split = jnp.where(sc[CTX] == 1, 1, 0)
    early = B - rows

    def chunk(src, flat, acc_ref, place, pos, masks, both, lse, delta, h):
        n_q = lse.shape[1]
        pair = dot(flat[place, :], both)
        s = pair[:, :n_q]
        if masks is not None:
            row = lax.broadcasted_iota(jnp.int32, s.shape, 0) + pos
            s = jnp.where((row >= masks[0]) & (row < masks[1]), s, NEG)
        probs = jnp.exp(s - lse)
        ds = (probs * (pair[:, n_q:] - delta)).astype(BF)
        acc_ref[place, :] += dot_t(jnp.concatenate([ds, probs.astype(BF)], axis=1), both)
        return dot(src[pl.ds(mult(h, HD), HD), place], ds)

    def pair_up(q_h, g_h):
        zero = jnp.zeros_like(q_h)
        return jnp.concatenate(
            [jnp.concatenate([q_h, zero], axis=1), jnp.concatenate([zero, g_h], axis=1)], axis=0
        )

    def one_head(h, _):
        h_rows = pl.ds(mult(h, HD), HD)
        v_rows = pl.ds(mult(h, HD) + wide, HD)
        near = jnp.where((sc[Y] == 1) & (sc[PAIR + 2 * h + 1] == 1), 1, 0)

        def turn(src, dst):
            dst[...] = jnp.concatenate([src[h_rows, :], src[v_rows, :]], axis=0).T

        acc_p[...] = jnp.zeros_like(acc_p)
        turn(pbuf, p_rows)

        @pl.when(sc[Y] == 1)
        def _():
            acc_c[...] = jnp.zeros_like(acc_c)

        @pl.when(near == 1)
        def _():
            turn(cbuf, c_rows)

        lse = lse_s[pl.ds(mult(h, 8), 8), :][0:1]
        delta = jnp.sum(
            o_s[h_rows, :].astype(F32) * g_s[h_rows, :].astype(F32), axis=0, keepdims=True
        )
        both_s[...] = pair_up(q_ref[h_rows, :], g_s[h_rows, :])
        dq_s[...] = jnp.zeros_like(dq_s)
        lane = lax.broadcasted_iota(jnp.int32, lse.shape, 1)
        first = (lane < early) & (split == 1)

        def prompt(blk, both, lse, delta, n_q):
            start = sc[PAIR + 2 * h + blk] * B
            count = 4 - sc[PAIR + 2 * h + blk]

            def step(at, n):
                at = pl.multiple_of(at, 128)
                place = pl.ds(at, n)
                dq_s[:, :n_q] += chunk(
                    pbuf, p_rows, acc_p, place, at, None, both, lse, delta, h
                )

            def run(i, _):
                step(start + i * 256, 256)
                return 0

            lax.fori_loop(0, count, run, 0)
            step(start + count * 256, 128)

        prompt(later, both_s[...], jnp.where(first, FAR, lse), delta, rows)

        @pl.when(split == 1)
        def _():
            both = pair_up(q_ref[h_rows, :early], g_s[h_rows, :early])
            at, masks = whole_block(sc[PAIR + 2 * h])
            dq_s[:, :early] += chunk(
                pbuf,
                p_rows,
                acc_p,
                pl.ds(at, B),
                at,
                masks,
                both,
                lse[:, :early],
                delta[:, :early],
                h,
            )

        def window(t, _):
            cols = pl.ds(mult(t, tile), tile)
            at = window_start(sc, t, rows, tile)
            n = tile + 2 * LMAX
            masks = (span_ref[0:1, cols], span_ref[1:2, cols])
            g_h = g_s[h_rows, cols]
            d = jnp.sum(o_s[h_rows, cols].astype(F32) * g_h.astype(F32), axis=0, keepdims=True)
            both = pair_up(q_ref[h_rows, cols], g_h)
            l = lse_s[pl.ds(mult(h, 8), 8), cols][0:1]
            dq_s[:, cols] += chunk(
                cbuf, c_rows, acc_c, pl.ds(at, n), at, masks, both, l, d, h
            )
            return 0

        lax.fori_loop(0, 4 * near, window, 0)
        for k in range(4):
            cols = pl.ds(mult(sc[Z] ^ k, tile), tile)
            dq_ref[k, h_rows, :] = (dq_s[:, cols] * HD**-0.5).astype(BF)

        def give(acc, row, out):
            turned = acc[pl.ds(mult(row, rows), rows), :].T.astype(BF)
            out[h_rows, :] = turned[:HD]
            out[pl.ds(mult(h, HD) + wide, HD), :] = turned[HD:]

        @pl.when(sc[Y] == 0)
        def _():
            give(acc_p, sc[C], d_own)
            give(acc_p, 1 - sc[C], d_par)

        @pl.when(sc[Y] == 1)
        def _():
            give(acc_c, sc[C], d_own)
            give(acc_c, 1 - sc[C], d_par)
            give(acc_p, sc[C], d_r0)
            give(acc_p, 1 - sc[C], d_r1)

        return 0

    lax.fori_loop(0, heads, one_head, 0)


def norm(value):
    mean = jnp.mean(value, axis=-1, keepdims=True)
    centred = value - mean
    inv = lax.rsqrt(jnp.mean(centred * centred, axis=-1, keepdims=True) + EPS)
    return centred * inv, inv


def norm_back(e, n, inv):
    return (
        e - jnp.mean(e, axis=-1, keepdims=True) - n * jnp.mean(e * n, axis=-1, keepdims=True)
    ) * inv


def mid_body(sc, *refs):
    mixed = refs[0:4]
    x_hbm, cot_hbm = refs[4:6]
    packs = refs[6:8]
    others = refs[8:24]
    (
        out_ref,
        mb0,
        mb1,
        mb2,
        mb3,
        nl_ref,
        fb_ref,
        ab_ref,
        act_own,
        act_oth,
        ib_own,
        ib_oth,
        mix_own,
        mix_oth,
        gf_ref,
    ) = refs[24:39]
    we, ws, wc, mix_s, act_s, gp_s, ib_s, vec_s, thr_s, mb_s, pk_s, x_ref, cot_ref, small_ref, sems, psems = refs[39:]
    wide, tile = mixed[0].shape
    width = x_ref.shape[1]
    half = width // 2
    hidden = we.shape[1]
    block = hidden // 4
    hb = block // 2
    hw = wide // 2
    c = sc[C]
    hs = gathered_rows(hb)
    ht = hb - hs
    n_pack = half + hs
    n_other = hw // 2 + ht // 2 + 16

    stages = [[], [], [], []]
    small = []

    def move(stage, src, dst):
        n = len(stages[stage])
        stages[stage].append(pltpu.make_async_copy(src, dst, sems.at[stage, n]))

    for k in range(4):
        z = sc[Z] ^ k
        for j in range(2):
            xc = pl.ds(mult(sc[X] ^ j, half), half)
            for q in range(4):
                cc, yy = c ^ (q // 2), sc[Y] ^ (q % 2)
                piece = others[4 * q + k]
                at = j * n_other
                rows = pl.multiple_of(z * wide + cc * hw + yy * (hw // 2), hw // 2)
                move(0, piece.at[pl.ds(at, hw // 2), :], wc.at[pl.ds(rows, hw // 2), xc])
                rows = z * block + cc * hb + hs + yy * (ht // 2)
                rows = pl.ds(pl.multiple_of(rows, 16), ht // 2)
                move(2, piece.at[pl.ds(at + hw // 2, ht // 2), :], ws.at[rows, xc])
            n = 2 * k + j
            small.append(
                pltpu.make_async_copy(
                    others[k].at[pl.ds(at + hw // 2 + ht // 2, 16), :], pk_s.at[n], psems.at[n]
                )
            )
    for k in range(4):
        z = sc[Z] ^ k
        for xh in range(2):
            xc = pl.ds(xh * half, half)
            at = pl.multiple_of((xh * 4 + z) * n_pack, 16)
            for i in range(2):
                cc = c ^ i
                place = pl.ds(pl.multiple_of(z * block + cc * hb, hb), hb)
                move(1, packs[i].at[pl.ds(at, half), :], we.at[xc, place])
                place = pl.ds(pl.multiple_of(z * block + cc * hb, 16), hs)
                move(3, packs[i].at[pl.ds(at + half, hs), :], ws.at[place, xc])
    mine = pl.ds(mult(sc[Z], tile), tile)
    small.append(pltpu.make_async_copy(x_hbm.at[mine, :], x_ref, psems.at[8]))
    small.append(pltpu.make_async_copy(cot_hbm.at[mine, :], cot_ref, psems.at[9]))
    for stage in [small] + stages:
        for copy in stage:
            copy.start()

    for copy in small:
        copy.wait()
    for k in range(4):
        mix_s[pl.ds(mult(sc[Z] ^ k, wide), wide), :] = mixed[k][...]
    for k in range(4):
        for j in range(2):
            pack = pk_s[2 * k + j].astype(F32)
            at = pl.multiple_of((sc[Z] ^ k) * block + (sc[X] ^ j) * half, 128)
            thr_s[:, pl.ds(at, half)] = pack[:8]
            if k == 0:
                vec_s[:, pl.ds(mult(sc[X] ^ j, half), half)] = pack[:8]

    baseline = vec_s[0:1, :]
    scaling = vec_s[1:2, :]
    shifting = vec_s[2:3, :]
    settling = vec_s[3:4, :]
    rescaling = vec_s[4:5, :]
    reshifting = vec_s[5:6, :]

    for copy in stages[0]:
        copy.wait()
    first = x_ref[...].astype(F32) + tdot(mix_s[...], wc[...]) + baseline
    n1, inv1 = norm(first)
    normed = n1 * scaling + shifting
    low = normed.astype(BF)
    nl_ref[...] = low
    feed = jnp.zeros((tile, width), F32)
    for k in range(4):
        for stage, n in ((1, 4), (3, 4), (2, 8)):
            for copy in stages[stage][k * n : (k + 1) * n]:
                copy.wait()
        cols = pl.ds(mult(sc[Z] ^ k, block), block)
        inner = dot(low, we[:, cols]) + thr_s[6:7, cols]
        cdf = 0.5 * (1.0 + lax.erf(inner * (0.5**0.5)))
        pdf = jnp.exp(-0.5 * inner * inner) * (1.0 / math.sqrt(2.0 * math.pi))
        active = (inner * cdf).astype(BF)
        act_s[:, cols] = active
        gp_s[:, cols] = cdf + inner * pdf
        feed = feed + dot(active, ws[cols, :])
    second = normed + feed + settling
    n2, inv2 = norm(second)
    out_ref[:tile, :] = (n2 * rescaling + reshifting).astype(BF)
    dy = cot_ref[...].astype(F32)
    small_ref[...] = jnp.zeros_like(small_ref)
    small_ref[4:5, :] = jnp.sum(dy * n2, axis=0, keepdims=True)
    small_ref[5:6, :] = jnp.sum(dy, axis=0, keepdims=True)
    grad = norm_back(rescaling * dy, n2, inv2)
    small_ref[3:4, :] = jnp.sum(grad, axis=0, keepdims=True)
    feed_back = grad.astype(BF)
    fb_ref[...] = feed_back
    for n in range(4):
        cols = slice(n * block, (n + 1) * block)
        inner_back = (dot_t(feed_back, ws[cols, :]) * gp_s[:, cols]).astype(BF)
        ib_s[:, cols] = inner_back
        small_ref[8 + n : 9 + n, :] = jnp.sum(inner_back.astype(F32), axis=0, keepdims=True)
        grad = grad + dot_t(inner_back, we[:, cols])
    small_ref[1:2, :] = jnp.sum(grad * n1, axis=0, keepdims=True)
    small_ref[2:3, :] = jnp.sum(grad, axis=0, keepdims=True)
    grad_first = norm_back(scaling * grad, n1, inv1)
    small_ref[0:1, :] = jnp.sum(grad_first, axis=0, keepdims=True)
    out_ref[tile:, :] = small_ref[...].astype(BF)
    gf_ref[...] = grad_first
    attended_back = grad_first.astype(BF)
    ab_ref[...] = attended_back
    mb_s[...] = dot_t(wc[...], attended_back).astype(BF)
    for k, mb in enumerate((mb0, mb1, mb2, mb3)):
        mb[...] = mb_s[pl.ds(mult(sc[Z] ^ k, wide), wide), :]
    for n in range(4):
        mine = pl.ds(pl.multiple_of(n * block + c * hb, 128), hb)
        other = pl.ds(pl.multiple_of(n * block + (1 - c) * hb, 128), hb)
        cols = slice(n * hb, (n + 1) * hb)
        act_own[:, cols] = act_s[:, mine]
        act_oth[:, cols] = act_s[:, other]
        ib_own[:, cols] = ib_s[:, mine]
        ib_oth[:, cols] = ib_s[:, other]
        mine = pl.ds(pl.multiple_of(n * wide + c * hw, hw), hw)
        other = pl.ds(pl.multiple_of(n * wide + (1 - c) * hw, hw), hw)
        mix_own[n * hw : (n + 1) * hw, :] = mix_s[mine, :]
        mix_oth[n * hw : (n + 1) * hw, :] = mix_s[other, :]


def wg_body(sc, *refs):
    nl, fb, ab, act, ib, mix = [(refs[i], refs[6 + i]) for i in range(6)]
    g_ref = refs[12]
    half = nl[0].shape[1] // 2
    hb = act[0].shape[1] // 4
    hw = mix[0].shape[0] // 4
    for x in range(2):
        xc = slice(x * half, (x + 1) * half)
        for k in range(4):
            z = sc[Z] ^ k
            zc = pl.ds(mult(z, hb), hb)
            e = sum(tdot(nl[i][:, xc], ib[i][:, zc]) for i in range(2)).astype(BF)
            s = sum(tdot(act[i][:, zc], fb[i][:, xc]) for i in range(2)).astype(BF)
            zr = pl.ds(mult(z, hw), hw)
            m = sum(dot(mix[i][zr, :], ab[i][:, xc]) for i in range(2)).astype(BF)
            at = 0
            for v in (e, s, m):
                n = v.shape[0] // 2
                for yh in range(2):
                    g_ref[yh, x, k, at : at + n, :] = v[yh * n : (yh + 1) * n]
                at += n


def wfin_body(sc, *refs):
    quarters = refs[0:4]
    e_ref, s_ref, m_ref = refs[4:7]
    he = e_ref.shape[0] // 2
    hb = e_ref.shape[1] // 2
    hs = hb // 2
    hm = m_ref.shape[0] // 4
    for i in range(2):
        c = sc[C] ^ i
        for j in range(2):
            part = quarters[2 * i + j]
            y = sc[Y] ^ j
            rows = pl.ds(mult(y, he), he)
            e_ref[rows, pl.ds(mult(c, hb), hb)] = part[:he, :].astype(F32)
            at = pl.multiple_of(c * hb + y * hs, hs)
            s_ref[pl.ds(at, hs), :] = part[he : he + hs, :].astype(F32)
            at = pl.multiple_of((c * 2 + y) * hm, hm)
            m_ref[pl.ds(at, hm), :] = part[he + hs :, :].astype(F32)


def ib_body(sc, a_ref, b_ref, c_ref, dq_ref, wt_ref, kv_ref, *outs):
    wide = dq_ref.shape[1]
    tile = dq_ref.shape[2]
    for k in (3, 2, 1, 0):
        cols = pl.ds(mult(sc[Z] ^ k, tile), tile)
        total = a_ref[:, cols].astype(F32) + b_ref[:, cols].astype(F32)
        kv = (total + c_ref[:, cols].astype(F32)).astype(BF)
        kv_ref[k] = kv
        part = tdot(dq_ref[k], wt_ref[:wide, :]) + tdot(kv, wt_ref[wide:, :])
        outs[k][...] = part.astype(BF)


def pair_body(a_ref, b_ref, out_ref):
    out_ref[...] = (a_ref[...].astype(F32) + b_ref[...].astype(F32)).astype(BF)


def fin_body(a_ref, b_ref, c_ref, gf_ref, out_ref):
    total = a_ref[...].astype(F32) + b_ref[...].astype(F32)
    out_ref[...] = (total + c_ref[...].astype(F32) + gf_ref[...]).astype(BF)


def gp_body(sc, dq_ref, kv_ref, x_ref, all_ref, out_ref, acc, line, parts, small_ref, sems):
    wide = dq_ref.shape[1]
    tile = dq_ref.shape[2]
    half = out_ref.shape[3]
    copies = [
        pltpu.make_async_copy(all_ref.at[k, pl.ds(tile, 16), :], small_ref.at[k], sems.at[k])
        for k in range(4)
    ]
    for copy in copies:
        copy.start()
    ones = jnp.ones((8, tile), BF)
    top = bot = s_top = s_bot = 0.0
    for k in range(4):
        rows = x_ref[pl.ds(mult(sc[Z] ^ k, tile), tile), :]
        top = top + dot(dq_ref[k], rows)
        bot = bot + dot(kv_ref[k], rows)
        s_top = s_top + dot_t(ones, dq_ref[k])
        s_bot = s_bot + dot_t(ones, kv_ref[k, wide:, :])
    acc[:wide, :] = top
    acc[wide:, :] = bot
    for k in range(4):
        copies[k].wait()
        parts[k] = small_ref[k].astype(F32)
    parts[0] = ((parts[0] + parts[1]) + parts[2]) + parts[3]
    line[...] = jnp.zeros_like(line)
    line[0, 0:1, :wide] = s_top[0:1]
    line[0, 0:1, wide:] = s_bot[0:1]
    line[1, 0:1, :wide] = s_top[0:1]
    line[1, 0:1, wide:] = s_bot[0:1]
    for h in range(2):
        hc = slice(h * half, (h + 1) * half)
        line[h, 1:7, :] = parts[0, 0:6, hc]
        line[h, 7:8, :] = parts[0, pl.ds(8 + sc[Z], 1), hc]
    n_rows = out_ref.shape[2] - 16
    for i in range(2):
        at = pl.multiple_of((sc[C] ^ i) * n_rows, n_rows)
        for m in range(2):
            cols = pl.ds(mult(sc[X] ^ m, half), half)
            out_ref[i, m, :n_rows, :] = acc[pl.ds(at, n_rows), cols].astype(BF)
            out_ref[i, m, n_rows:, :] = line[sc[X] ^ m].astype(BF)


def join_body(dtype, sc, *refs):
    out = refs[4]
    tile = out.shape[0] // 4
    for k in range(4):
        out[pl.ds(mult(sc[Z] ^ k, tile), tile), :] = refs[k][:tile, :].astype(dtype)


def gpfin_body(sc, a_ref, b_ref, out, line, *vecs):
    n_rows = a_ref.shape[0] - 16
    rows = a_ref[n_rows : n_rows + 8, :].astype(F32)
    line[...] = rows
    for i, vec in enumerate(vecs):
        vec[...] = rows[1 + i]
    for i, ref in enumerate((a_ref, b_ref)):
        at = pl.multiple_of((sc[C] ^ i) * n_rows, n_rows)
        out[pl.ds(at, n_rows), :] = ref[:n_rows, :].astype(F32)


def make_device(n_dp, n_ctx, n_t, generic):
    def swap(axis, size, k):
        return lambda v: lax.ppermute(v, axis, [(i, i ^ k) for i in range(size)])

    pc = swap("core", 2, 1)
    py = swap("cy", n_ctx // 2, 1)
    px = swap("dp", n_dp, 1)
    pz = [lambda v: v] + [swap("tensor", n_t, k) for k in range(1, n_t)]

    def on_device(
        tokens,
        cotangent,
        segments,
        pairing,
        project,
        offsets,
        combine,
        baseline,
        scaling,
        shifting,
        expand,
        thresholds,
        shrink,
        settling,
        rescaling,
        reshifting,
    ):
        _, rows, width = tokens.shape
        heads = pairing.shape[0] // n_t
        wide = heads * HD
        tile = rows // n_t
        half = width // 2
        block = expand.shape[1]
        hidden = block * n_t
        hb = block // 2
        hw = wide // 2
        x = tokens[0]
        cot = cotangent[0]
        c = lax.axis_index("core")
        y = lax.axis_index("cy")
        ctx = 2 * y + c
        z = lax.axis_index("tensor")
        dp = lax.axis_index("dp")
        xi = jnp.zeros_like(dp) if generic else dp
        pairs = lax.dynamic_slice_in_dim(pairing, z * heads, heads, 0).reshape(-1)
        sc = jnp.concatenate(
            [jnp.stack([ctx, z, xi, c, y, c, c, c]).astype(jnp.int32), pairs.astype(jnp.int32)]
        )

        def both_halves(v, axis):
            full = lax.all_gather(v, "dp", axis=axis, tiled=True)
            return jnp.split(full, 2, axis=axis)

        wt = jnp.transpose(project, (1, 2, 0)).reshape(3 * wide, -1)
        vectors = [baseline, scaling, shifting, settling, rescaling, reshifting]

        hq = wide // 2
        part = 3 * wide // 2
        def pack(wt_h, e_h, s_h, m_h, off_h, vecs_h):
            return call(
                pack_body,
                (
                    sds((16, half), F32),
                    sds((part + 16, half), BF),
                    sds((half + gathered_rows(hb), half), BF),
                    sds((hw // 2 + (hb - gathered_rows(hb)) // 2 + 16, half), BF),
                ),
                ins=[SM] + [VM] * 12,
                cost=cost(0, 8 * half * width),
            )(sc, wt_h, e_h, s_h, m_h, off_h, *vecs_h)

        vectors = vectors + [thresholds]
        if generic:
            own_wt, other_wt = both_halves(wt, 1)
            parts = [both_halves(v, 0) for v in [expand] + vectors]
            cols = [both_halves(v, 1) for v in (shrink, combine, offsets)]
            packed = [
                pack(
                    w, parts[0][j], cols[0][j], cols[1][j], cols[2][j], [p[j] for p in parts[1:]]
                )
                for j, w in enumerate((own_wt, other_wt))
            ]
            small, wtc = packed[0][0], packed[0][1]
            got_wt = packed[1][1]
            weights = jnp.stack(
                [lax.all_gather(p[2], "tensor", axis=0) for p in packed]
            ).reshape(-1, half)
            other_wide = jnp.concatenate([p[3] for p in packed])
        else:
            own_wt = wt
            small, wtc, wpack, o_c = pack(wt, expand, shrink, combine, offsets, vectors)
            got_wt = px(wtc)
            weights = lax.all_gather(wpack, ("dp", "tensor"), axis=0, tiled=True)
            other_wide = jnp.concatenate([o_c, px(o_c)])

        def after(v, *deps):
            return lax.optimization_barrier((v, *deps))[0]

        got_wt2 = after(pc(got_wt), other_wide)

        qT, kvT, wt_full = call(
            qkv_body,
            (
                sds((wide, rows), BF),
                sds((2 * wide, rows), BF),
                sds((3 * wide, width), BF),
            ),
            ins=[SM] + [VM] * 5,
            scratch=[pltpu.VMEM((3 * wide, half), BF), pltpu.VMEM((16, 3 * wide), BF)],
            cost=cost(2 * rows * width * 3 * wide, 4 * rows * width),
        )(sc, x, own_wt, small, got_wt, got_wt2)

        seg = segments[0]
        mine = lax.dynamic_slice_in_dim(seg, c * rows, rows, 0)
        low = jnp.sum((seg[:, None] < mine[None, :]).astype(jnp.int32), axis=0)
        high = jnp.sum((seg[:, None] <= mine[None, :]).astype(jnp.int32), axis=0)
        span = jnp.concatenate(
            [low[None], high[None], jnp.zeros((6, rows), jnp.int32)], axis=0
        )

        z_near = pz[1](other_wide)
        z_far = pz[2](other_wide)
        other_z = [other_wide, z_near, z_far, pz[1](z_far)]

        par = pc(kvT)
        ra = lax.ppermute(kvT, "cy", [(0, 1)])

        kv_scratch = [pltpu.VMEM((2 * wide, 2 * rows), BF), pltpu.VMEM((2 * wide, 2 * rows), BF)]
        state = [
            sds((wide, rows), F32),
            sds((8 * heads, rows), F32),
            sds((8 * heads, rows), F32),
        ]
        sofar = call(
            fwd_near_body,
            tuple(state),
            ins=[SM, VM, VM] + [ANY] * 2,
            scratch=[kv_scratch[0], pltpu.SemaphoreType.DMA((2,))],
            cost=cost(0, 1000),
        )(sc, qT, span, kvT, par)
        ra = after(ra, sofar[0])
        rb = pc(after(ra, z_near, z_far))
        other_y = [py(after(w, ra)) for w in other_z[:3]]
        *o_tiles, lse = call(
            fwd_far_body,
            (*[sds((wide, tile), BF)] * 4, sds((8 * heads, rows), F32)),
            ins=[SM, VM] + [ANY] * 2 + [VM] * 3,
            scratch=[kv_scratch[0]]
            + [pltpu.VMEM(v.shape, v.dtype) for v in state]
            + [pltpu.SemaphoreType.DMA((2,))],
            cost=cost(0, 1000),
        )(sc, qT, ra, rb, *sofar)
        relayed = after(other_z[3], o_tiles[0])
        o_tiles = [after(o, *other_y, relayed) for o in o_tiles]
        other_y = other_y + [py(relayed)]
        mixed = [pz[k](o_tiles[k]) for k in range(4)]
        weights2 = pc(after(weights, *mixed, other_y[3]))
        others = other_z + other_y
        others = others + [pc(after(w, o_tiles[0])) for w in others]

        outs = call(
            mid_body,
            (
                sds((tile + 16, width), BF),
                *[sds((wide, tile), BF)] * 4,
                *[sds((tile, width), BF)] * 3,
                *[sds((tile, hidden // 2), BF)] * 4,
                *[sds((width // 2, tile), BF)] * 2,
                sds((tile, width), F32),
            ),
            ins=[SM] + [VM] * 4 + [ANY] * 20,
            scratch=[
                pltpu.VMEM((width, hidden), BF),
                pltpu.VMEM((hidden, width), BF),
                pltpu.VMEM((width, width), BF),
                pltpu.VMEM((width, tile), BF),
                pltpu.VMEM((tile, hidden), BF),
                pltpu.VMEM((tile, hidden), F32),
                pltpu.VMEM((tile, hidden), BF),
                pltpu.VMEM((8, width), F32),
                pltpu.VMEM((8, hidden), F32),
                pltpu.VMEM((width, tile), BF),
                pltpu.VMEM((8, 16, half), BF),
                pltpu.VMEM((tile, width), BF),
                pltpu.VMEM((tile, width), BF),
                pltpu.VMEM((16, width), F32),
                pltpu.SemaphoreType.DMA((4, 32)),
                pltpu.SemaphoreType.DMA((10,)),
            ],
            cost=cost(8 * tile * width * hidden + 4 * tile * width * width, 4 * width * hidden),
        )(sc, *mixed, x, cot, weights, weights2, *others)
        out_low = outs[0]
        mb = outs[1:5]
        nl, fb, ab, act_own, act_oth, ib_own, ib_oth, mix_own, mix_oth, grad_first = outs[5:]
        grads = [mb[0]] + [pz[k](mb[k]) for k in range(1, 4)]

        theirs = [pc(v) for v in (nl, fb, ab, act_oth, ib_oth, mix_oth)]
        gathered = lax.all_gather(out_low, "tensor", axis=0)

        outs = call(
            bwd_body,
            (sds((4, wide, tile), BF), *[sds((2 * wide, rows), BF)] * 4),
            ins=[SM, VM, VM] + [ANY] * 4 + [VM] * 9,
            scratch=kv_scratch
            + [
                pltpu.VMEM((wide, rows), BF),
                pltpu.VMEM((wide, rows), BF),
                pltpu.VMEM((2 * rows, 2 * HD), F32),
                pltpu.VMEM((2 * rows, 2 * HD), F32),
                pltpu.VMEM((2 * rows, 2 * HD), BF),
                pltpu.VMEM((2 * rows, 2 * HD), BF),
                pltpu.VMEM((2 * HD, 2 * rows), BF),
                pltpu.VMEM((HD, rows), F32),
                pltpu.SemaphoreType.DMA((4,)),
            ],
            cost=cost(10 * B * rows * wide, 4 * 4 * wide * rows, B * rows * heads),
        )(sc, qT, span, kvT, par, ra, rb, *o_tiles, lse, *grads)
        dq, d_own, d_par, d_r0, d_r1 = outs
        got_par = pc(d_par)
        got_r = pc(d_r1)
        prompt_part = (d_r0.astype(F32) + got_r.astype(F32)).astype(BF)
        nl = after(nl, prompt_part, got_par)
        n_part = half // 2 + hb // 2 + hw // 2
        g = call(
            wg_body,
            sds((2, 2, 4, n_part, half), BF),
            ins=[SM] + [VM] * 12,
            cost=cost(4 * tile * width * hidden, 4 * width * hidden),
        )(sc, nl, fb, ab, act_own, ib_own, mix_own, *theirs)
        from_y = lax.ppermute(prompt_part, "cy", [(1, 0)])
        outs = call(
            ib_body,
            (sds((4, 2 * wide, tile), BF), *[sds((tile, width), BF)] * 4),
            ins=[SM] + [VM] * 5,
            cost=cost(2 * rows * width * 3 * wide, 8 * rows * width),
        )(sc, after(d_own, gathered), got_par, from_y, dq, wt_full)
        kv_back, back = outs[0], outs[1:]
        layer_out = after(gathered, kv_back)[:, :tile].reshape(rows, width)
        passed = pz[1](back[3])
        relay = call(pair_body, sds((tile, width), BF), ins=[VM] * 2)(back[2], passed)
        near = pz[1](after(back[1], passed))
        far = pz[2](relay)
        gp = call(
            gp_body,
            sds((2, 2, 3 * wide // 2 + 16, half), BF),
            ins=[SM] + [VM] * 3 + [ANY],
            scratch=[
                pltpu.VMEM((3 * wide, width), F32),
                pltpu.VMEM((2, 16, half), F32),
                pltpu.VMEM((4, 16, width), F32),
                pltpu.VMEM((4, 16, width), BF),
                pltpu.SemaphoreType.DMA((4,)),
            ],
            cost=cost(2 * rows * width * 3 * wide, 4 * rows * width),
        )(sc, dq, kv_back, x, gathered)

        def add(a, b):
            return (a.astype(F32) + b.astype(F32)).astype(BF)

        gp_c = add(gp[0], pc(gp[1]))
        low_tokens = call(
            fin_body,
            sds((tile, width), BF),
            ins=[VM] * 4,
            cost=cost(4 * tile * width, 12 * tile * width),
        )(back[0], near, far, after(grad_first, gp_c, layer_out))
        gp_c = after(gp_c, low_tokens)
        tiles_near = pz[1](low_tokens)
        tiles_far = pz[2](low_tokens)
        token_tiles = [low_tokens, tiles_near, tiles_far, pz[1](tiles_far)]
        grad_tokens = call(
            functools.partial(join_body, F32),
            sds((rows, width), F32),
            ins=[SM] + [VM] * 4,
            cost=cost(rows * width, 6 * rows * width),
        )(sc, *token_tiles)
        def sum_z(parts, wait=()):
            relay = after(add(parts[2], pz[1](parts[3])), *wait)
            near = pz[1](parts[1])
            far = pz[2](relay)
            total = parts[0].astype(F32) + near.astype(F32) + far.astype(F32)
            return total.astype(BF)

        def finish_ff(mine, *wait):
            quarters = [mine, after(py(mine), *wait)]
            quarters = quarters + [pc(q) for q in quarters]
            return call(
                wfin_body,
                (sds((half, block), F32), sds((block, half), F32), sds((wide, half), F32)),
                ins=[SM] + [VM] * 4,
            )(sc, *quarters)

        def finish_gp(mine):
            return call(
                gpfin_body,
                (
                    sds((3 * wide, half), F32),
                    sds((8, half), F32),
                    *[sds((half,), F32)] * 7,
                ),
                ins=[SM] + [VM] * 2,
            )(sc, mine, pc(mine))

        gp = add(gp_c, py(gp_c))
        if generic:
            g = lax.psum_scatter(g, "cy", scatter_dimension=0, tiled=False)
            parts = [
                finish_ff(sum_z(v))
                for v in (g[0], g[1])
            ]

            def scatter(two, axis):
                full = jnp.concatenate(two, axis=axis).astype(BF)
                return lax.psum_scatter(
                    full, "dp", scatter_dimension=axis, tiled=True
                ).astype(F32)

            summed = [scatter([p[i] for p in parts], i and 1) for i in range(3)]
            both = [finish_gp(gp[j]) for j in range(2)]
            grad_project = scatter([b[0] for b in both], 1)
            grad_offsets = scatter([both[0][1][0].reshape(2, wide)], 1)
            vecs = [scatter([b[2 + i] for b in both], 0) for i in range(7)]
        else:
            g = after(g, from_y)
            g = lax.psum_scatter(
                g.reshape(-1, half), ("cy", "dp"), scatter_dimension=0, tiled=True
            )
            g = after(g, tiles_near, tiles_far)
            g = sum_z(g.reshape(4, n_part, half))
            grad_project, lines, *vecs = finish_gp(add(gp[0], px(gp[1])))
            summed = finish_ff(g, grad_tokens, layer_out, grad_project)
            n_off = offsets.shape[1]
            grad_offsets = lax.dynamic_slice_in_dim(
                lines[0].reshape(2, wide), dp * n_off, n_off, 1
            )
        grad_expand, grad_shrink, grad_combine = summed
        grad_project = jnp.transpose(grad_project.reshape(3, wide, -1), (2, 0, 1))

        return (
            layer_out[None],
            grad_tokens[None],
            grad_project,
            grad_offsets,
            grad_combine,
            vecs[0],
            vecs[1],
            vecs[2],
            grad_expand,
            vecs[6],
            grad_shrink,
            vecs[3],
            vecs[4],
            vecs[5],
        )

    return on_device


def solution(mesh):
    in_specs = (
        P("dp", ("cy", "core"), None),
        P("dp", ("cy", "core"), None),
        P("dp", None),
        P(),
        P("dp", None, "tensor"),
        P(None, ("tensor", "dp")),
        P("tensor", "dp"),
        P("dp"),
        P("dp"),
        P("dp"),
        P("dp", "tensor"),
        P(("tensor", "dp")),
        P("tensor", "dp"),
        P("dp"),
        P("dp"),
        P("dp"),
    )
    out_specs = (
        P("dp", ("cy", "core"), None),
        P("dp", ("cy", "core"), None),
        P("dp", None, "tensor"),
        P(None, ("tensor", "dp")),
        P("tensor", "dp"),
        P("dp"),
        P("dp"),
        P("dp"),
        P("dp", "tensor"),
        P(("tensor", "dp")),
        P("tensor", "dp"),
        P("dp"),
        P("dp"),
        P("dp"),
    )
    n_dp, n_ctx, n_t = mesh.shape["dp"], mesh.shape["ctx"], mesh.shape["tensor"]
    split = Mesh(mesh.devices.reshape(n_dp, n_ctx // 2, 2, n_t), ("dp", "cy", "core", "tensor"))
    on_device = make_device(n_dp, n_ctx, n_t, n_dp != 2)
    return jax.shard_map(
        on_device, mesh=split, in_specs=in_specs, out_specs=out_specs, check_vma=False
    )
```
